256 devices in a mesh: ctx: 64 (over y, x, z_hi), ch: 2 (over core), fsdp: 2 (over z_lo).
Axes of the slice: x: 4, y: 4, z: 8 (z_hi: 4, z_lo: 2; z = z_hi * 2 + z_lo), core: 2. Of those that a mesh axis runs over, the one named last changes fastest.
Arguments:
- query_rows: bfloat16 [16384, 8192], P(('ctx', 'fsdp'), 'ch'), may hold values from -6 to 6
- key_rows: bfloat16 [16384, 8192], P(('ctx', 'fsdp'), 'ch'), may hold values from -6 to 6
- value_rows: bfloat16 [16384, 8192], P(('ctx', 'fsdp'), 'ch'), may hold values from -6 to 6
- upstream: bfloat16 [16384, 8192], P(('ctx', 'fsdp'), 'ch'), may hold values from -6 to 6
- decay_rate: float32 [8, 512], P(None, 'fsdp'), may hold values from 0.1 to 341
- residue: float32 [8, 512], P(None, 'fsdp'), may hold values from -4 to 4
Outputs:
- grad_query: bfloat16 [16384, 8192], P(('ctx', 'fsdp'), 'ch')
- grad_key: bfloat16 [16384, 8192], P(('ctx', 'fsdp'), 'ch')
- grad_value: bfloat16 [16384, 8192], P(('ctx', 'fsdp'), 'ch')
- residue_grad: float32 [8, 512], P(None, 'fsdp')
The draws below stay inside these ranges and needn't reach their ends.
All inputs are finite; a program needn't handle non-finite values.
Results may differ from the reference program's by a relative error of at most 0.0017.
Values sent between devices are 32-bit elements; how exact they have to be, the bound alone decides.
No kernel may reach another device: no remote copies, remote signals or barrier semaphores. Data moves between devices by JAX's collectives and lax.ppermute only.
A program may use at most 128 MiB of HBM per device.

```python
import math
import jax
import jax.numpy as jnp
from jax import lax

D = 8192
FILTERS = 512
ORDER = 8
TOKENS = 16384


def block_scale(rng, shape, cuts, low, high):
    gain, own = 1.0, jax.random.fold_in(rng, 6)
    for axis_at, parts in cuts:
        steps = jnp.exp(jax.random.uniform(jax.random.fold_in(own, axis_at), (parts,), jnp.float32, low / len(cuts), high / len(cuts)))
        gain = gain * jnp.repeat(steps, shape[axis_at] // parts).reshape([-1 if axis == axis_at else 1 for axis in range(len(shape))])
    return gain


def normal_values(rng, shape, spread, most, pieces=(), kind=jnp.bfloat16):
    array = jax.random.normal(rng, shape, jnp.float32) * spread
    if len(pieces) > 0:
        array = block_scale(rng, shape, pieces, -0.22, 0.18) * array
    return jnp.clip(array, min=-most, max=most).astype(kind)


def setup_inputs(seed: int = 0) -> dict:
    streams_of = jax.random.split(jax.random.key(seed), 7)
    query_rows = normal_values(streams_of[0], (TOKENS, D), 1.0, 6.0, ((0, 128), (1, 2)))
    key_rows = normal_values(streams_of[1], (TOKENS, D), 1.0, 6.0, ((0, 128), (1, 2)))
    value_rows = normal_values(streams_of[2], (TOKENS, D), 1.0, 6.0, ((0, 128), (1, 2)))
    upstream = normal_values(streams_of[3], (TOKENS, D), 1.0, 6.0, ((0, 128), (1, 2)))
    decay_rate = jnp.clip(jnp.exp(math.log(341.0) - 8.1344676 * jax.random.uniform(streams_of[4], (ORDER, FILTERS), jnp.float32) ** block_scale(streams_of[4], (ORDER, FILTERS), ((1, 2),), -0.2, 0.2)), 0.1, 341.0)
    residue = normal_values(streams_of[5], (ORDER, FILTERS), 0.25, 4.0, ((1, 2),), jnp.float32)
    return {"query_rows": query_rows, "key_rows": key_rows, "value_rows": value_rows, "upstream": upstream, "decay_rate": decay_rate, "residue": residue}


def reference(query_rows, key_rows, value_rows, upstream, decay_rate, residue):
    repeat = D // FILTERS
    log_decay = decay_rate / TOKENS
    mode_gain = jnp.sqrt((1.0 + decay_rate) / TOKENS)
    decay = jnp.tile(jnp.exp(-log_decay), (1, repeat))
    weight = jnp.tile(residue * mode_gain, (1, repeat))
    zeros = jnp.zeros((ORDER, D), jnp.float32)

    def forward(carry, row):
        state, total = carry
        query_one, key_one, value_one, grad_one = row
        product = key_one.astype(jnp.float32) * value_one.astype(jnp.float32)
        gated = grad_one.astype(jnp.float32) * query_one.astype(jnp.float32)
        state = decay * state + product[None, :]
        conv = lax.optimization_barrier(jnp.sum(weight * state, axis=0))
        total = total + gated[None, :] * state
        return ((state, total), (grad_one.astype(jnp.float32) * conv).astype(jnp.bfloat16))
    (final_state, total), grad_query = lax.scan(forward, (zeros, zeros), (query_rows, key_rows, value_rows, upstream))

    def backward(state, row):
        query_one, key_one, value_one, grad_one = row
        gated = grad_one.astype(jnp.float32) * query_one.astype(jnp.float32)
        state = decay * state + gated[None, :]
        flowing = lax.optimization_barrier(jnp.sum(weight * state, axis=0))
        return (state, ((flowing * value_one.astype(jnp.float32)).astype(jnp.bfloat16), (flowing * key_one.astype(jnp.float32)).astype(jnp.bfloat16)))
    last_state, (grad_key, grad_value) = lax.scan(backward, zeros, (query_rows, key_rows, value_rows, upstream), reverse=True)
    grouped = lax.optimization_barrier(jnp.sum(total.reshape(ORDER, repeat, FILTERS), axis=1))
    residue_grad = mode_gain * grouped / math.sqrt(TOKENS)
    return (grad_query, grad_key, grad_value, residue_grad)
```

```python
import functools
import math

import jax
import jax.numpy as jnp
from jax import lax
from jax.experimental import pallas as pl
from jax.experimental.pallas import tpu as pltpu
from jax.sharding import PartitionSpec as P

TOKENS = 16384
ROWS = 128
MODES = 8
FILTERS = 512
BLOCKS = 8
SUB = 8
RUN = ROWS // SUB
LANES = 128
STRIPS = FILTERS // LANES
PAIRS = BLOCKS // 2
WIDTH = BLOCKS * FILTERS
SHARDS = TOKENS // ROWS
ALL = ("ctx", "fsdp")
f32 = jnp.float32


def sublane():
    return lax.broadcasted_iota(jnp.int32, (SUB, LANES), 0)


def rows_of(ref, j):
    return ref[pl.ds(j, SUB, stride=RUN), :]


def owner(n, pair, strip):
    return (n * PAIRS + pair) * STRIPS + strip


def summarize_kernel(rate_ref, q_ref, k_ref, v_ref, u_ref, send_ref, cf_ref, cb_ref, tab, ps, gs):
    blk = pl.program_id(0)
    s = sublane()

    @pl.when(blk == 0)
    def _():
        def make(i, _):
            strip, n = i // MODES, i % MODES
            log_decay = jnp.broadcast_to(rate_ref[pl.ds(n * STRIPS + strip, 1), :], (SUB, LANES)) / TOKENS
            tab[0, i] = jnp.exp(-log_decay)
            for step in range(3):
                hop = 1 << step
                factor = jnp.exp(-log_decay * (RUN * hop))
                tab[1 + step, i] = jnp.where(s >= hop, factor, 0.0)
                tab[4 + step, i] = jnp.where(s < SUB - hop, factor, 0.0)
            return 0

        lax.fori_loop(0, STRIPS * MODES, make, 0)

    pair, odd = blk // 2, blk % 2

    def strip_body(strip, _):
        cols = pl.ds(pl.multiple_of(strip * LANES, LANES), LANES)
        ps[...] = k_ref[:, cols].astype(f32) * v_ref[:, cols].astype(f32)
        gs[...] = u_ref[:, cols].astype(f32) * q_ref[:, cols].astype(f32)
        base = strip * MODES
        decay = [tab[0, base + n] for n in range(MODES)]
        behind = [None] * MODES
        for j in reversed(range(RUN)):
            gated = rows_of(gs, j)
            for n in range(MODES):
                behind[n] = gated if j == RUN - 1 else decay[n] * behind[n] + gated
        ahead, terms = [None] * MODES, [None] * MODES
        for j in range(RUN):
            product, gated = rows_of(ps, j), rows_of(gs, j)
            for n in range(MODES):
                if j == 0:
                    ahead[n] = product
                    terms[n] = gated * product
                else:
                    ahead[n] = decay[n] * ahead[n] + product
                    terms[n] = terms[n] + gated * ahead[n]
        for n in range(MODES):
            place = owner(n, pair, strip)
            total = ahead[n]
            for step in range(3):
                total = total + tab[1 + step, base + n] * pltpu.roll(total, 1 << step, 0)
            send_ref[place, pl.ds(odd, 1), :] = total[SUB - 1 :, :]
            enter = jnp.where(s >= 1, pltpu.roll(total, 1, 0), 0.0)
            cf_ref[n, :, cols] = enter
            term = jnp.sum(terms[n] + decay[n] * behind[n] * enter, axis=0, keepdims=True)
            total = behind[n]
            for step in range(3):
                total = total + tab[4 + step, base + n] * pltpu.roll(total, SUB - (1 << step), 0)
            send_ref[place, pl.ds(2 + odd, 1), :] = total[:1, :]
            cb_ref[n, :, cols] = jnp.where(s < SUB - 1, pltpu.roll(total, SUB - 1, 0), 0.0)

            @pl.when(odd == 0)
            def _():
                send_ref[place, 4:5, :] = term
                send_ref[place, 5:8, :] = jnp.zeros((3, LANES), f32)

            @pl.when(odd == 1)
            def _():
                send_ref[place, 4:5, :] = send_ref[place, 4:5, :] + term

        return 0

    lax.fori_loop(0, STRIPS, strip_body, 0)


def carry_kernel(where_ref, rate_ref, x_ref, y_ref, cross_ref):
    place = where_ref[0]
    n, strip = place // (PAIRS * STRIPS), place % STRIPS
    log_decay = jnp.broadcast_to(rate_ref[pl.ds(n * STRIPS + strip, 1), :], (SUB, LANES)) / TOKENS
    across = jnp.exp(-log_decay * ROWS)
    s = sublane()
    zero = jnp.zeros((SUB, LANES), f32)

    def up(i, state_cross):
        state, cross, terms = state_cross
        x = x_ref[i]
        y_ref[i] = state
        cross = cross + pltpu.roll(x, SUB - 2, 0) * state
        return across * state + x, cross, terms + x

    _, cross, terms = lax.fori_loop(0, SHARDS, up, (zero, zero, zero), unroll=8)
    cross_row = cross[0:1, :] + cross[1:2, :]
    row = jnp.exp(-log_decay[0:1, :]) * cross_row + terms[4:5, :]
    row = jnp.broadcast_to(row, (SUB, LANES))

    def down(i, state):
        at = SHARDS - 1 - i
        y_ref[at] = jnp.where(s < 2, y_ref[at], jnp.where(s < 4, state, row))
        return across * state + x_ref[at]

    lax.fori_loop(0, SHARDS, down, zero, unroll=8)


def finish_kernel(
    rate_ref, residue_ref, q_ref, k_ref, v_ref, u_ref, cf_ref, cb_ref, in_ref,
    gq_ref, gk_ref, gv_ref, tab, ps, gs, cs, fs,
):
    blk = pl.program_id(0)
    s = sublane()

    @pl.when(blk == 0)
    def _():
        def make(i, _):
            strip, n = i // MODES, i % MODES
            at = pl.ds(n * STRIPS + strip, 1)
            rate = jnp.broadcast_to(rate_ref[at, :], (SUB, LANES))
            log_decay = rate / TOKENS
            gain = jnp.sqrt((1.0 + rate) / TOKENS)
            tab[0, i] = jnp.exp(-log_decay)
            tab[1, i] = jnp.broadcast_to(residue_ref[at, :], (SUB, LANES)) * gain
            tab[2, i] = jnp.exp(-log_decay * (RUN * s).astype(f32))
            tab[3, i] = jnp.exp(-log_decay * (RUN * (SUB - 1 - s)).astype(f32))
            return 0

        lax.fori_loop(0, STRIPS * MODES, make, 0)

    pair, odd = blk // 2, blk % 2

    def strip_body(strip, _):
        cols = pl.ds(pl.multiple_of(strip * LANES, LANES), LANES)
        key, value = k_ref[:, cols].astype(f32), v_ref[:, cols].astype(f32)
        grad = u_ref[:, cols].astype(f32)
        ps[...] = key * value
        gs[...] = grad * q_ref[:, cols].astype(f32)
        base = strip * MODES
        decay = [tab[0, base + n] for n in range(MODES)]
        weight = [tab[1, base + n] for n in range(MODES)]

        def weighted(states):
            parts = [weight[n] * states[n] for n in range(MODES)]
            while len(parts) > 1:
                parts = [a + b for a, b in zip(parts[::2], parts[1::2])]
            return parts[0]

        state = []
        for n in range(MODES):
            carry = in_ref[owner(n, pair, strip), pl.ds(odd, 1), :]
            state.append(cf_ref[n, :, cols] + tab[2, base + n] * carry)
        for j in range(RUN):
            product = rows_of(ps, j)
            state = [decay[n] * state[n] + product for n in range(MODES)]
            cs[pl.ds(j, SUB, stride=RUN), :] = weighted(state)
        state = []
        for n in range(MODES):
            carry = in_ref[owner(n, pair, strip), pl.ds(2 + odd, 1), :]
            state.append(cb_ref[n, :, cols] + tab[3, base + n] * carry)
        for j in reversed(range(RUN)):
            gated = rows_of(gs, j)
            state = [decay[n] * state[n] + gated for n in range(MODES)]
            fs[pl.ds(j, SUB, stride=RUN), :] = weighted(state)
        flowing = fs[...]
        gq_ref[:, cols] = (grad * cs[...]).astype(jnp.bfloat16)
        gk_ref[:, cols] = (flowing * value).astype(jnp.bfloat16)
        gv_ref[:, cols] = (flowing * key).astype(jnp.bfloat16)
        return 0

    lax.fori_loop(0, STRIPS, strip_body, 0)


def whole(shape):
    return pl.BlockSpec(shape, lambda *_: (0,) * len(shape))


def local(query_rows, key_rows, value_rows, upstream, decay_rate, residue):
    half = lax.axis_index("fsdp")
    mine = jnp.concatenate([decay_rate, residue], axis=0)
    other = lax.ppermute(mine, "fsdp", [(0, 1), (1, 0)])
    both = jnp.where(
        half == 0, jnp.concatenate([mine, other], 1), jnp.concatenate([other, mine], 1)
    )
    rates, residues = both.reshape(2, MODES * STRIPS, LANES)
    bf16 = jnp.bfloat16
    wide = pl.BlockSpec((ROWS, FILTERS), lambda b: (0, b))
    states = pl.BlockSpec((MODES, SUB, FILTERS), lambda b: (0, 0, b))
    params = whole((MODES * STRIPS, LANES))
    packet = (SHARDS, SUB, LANES)
    packet_shape = jax.ShapeDtypeStruct(packet, f32)
    state_shape = jax.ShapeDtypeStruct((MODES, SUB, WIDTH), f32)
    table = (STRIPS * MODES, SUB, LANES)
    send, enter_ahead, enter_behind = pl.pallas_call(
        summarize_kernel,
        grid=(BLOCKS,),
        in_specs=[params] + [wide] * 4,
        out_specs=[whole(packet), states, states],
        out_shape=[packet_shape, state_shape, state_shape],
        scratch_shapes=[pltpu.VMEM((7,) + table, f32)] + [pltpu.VMEM((ROWS, LANES), f32)] * 2,
        name="summarize",
    )(rates, query_rows, key_rows, value_rows, upstream)
    arrived = lax.all_to_all(send, ALL, 0, 0, tiled=True)
    place = lax.axis_index(ALL).astype(jnp.int32).reshape(1)
    carries = pl.pallas_call(
        carry_kernel,
        in_specs=[pl.BlockSpec(memory_space=pltpu.SMEM)] + [pl.BlockSpec(memory_space=pltpu.VMEM)] * 2,
        out_specs=pl.BlockSpec(memory_space=pltpu.VMEM),
        out_shape=packet_shape,
        scratch_shapes=[pltpu.VMEM((SUB, LANES), f32)],
        name="carry",
    )(place, rates, arrived)
    back = lax.all_to_all(carries, ALL, 0, 0, tiled=True)
    rows = back[:, 4, :].reshape(MODES, PAIRS, FILTERS).sum(axis=1)
    width = FILTERS // 2
    rows = lax.dynamic_slice_in_dim(rows, half * width, width, 1)
    rows = rows + lax.ppermute(rows, "ch", [(0, 1), (1, 0)])
    gain = jnp.sqrt((1.0 + decay_rate) / TOKENS)
    residue_grad = gain * rows / math.sqrt(TOKENS)
    out = jax.ShapeDtypeStruct((ROWS, WIDTH), bf16)
    grads = pl.pallas_call(
        finish_kernel,
        grid=(BLOCKS,),
        in_specs=[params] * 2 + [wide] * 4 + [states] * 2 + [whole(packet)],
        out_specs=[wide] * 3,
        out_shape=[out] * 3,
        scratch_shapes=[pltpu.VMEM((4,) + table, f32)] + [pltpu.VMEM((ROWS, LANES), f32)] * 4,
        name="finish",
    )(rates, residues, query_rows, key_rows, value_rows, upstream, enter_ahead, enter_behind, back)
    return (*grads, residue_grad)


def solution(mesh):
    rows = P(ALL, "ch")
    params = P(None, "fsdp")
    return jax.shard_map(
        local,
        mesh=mesh,
        in_specs=(rows, rows, rows, rows, params, params),
        out_specs=(rows, rows, rows, params),
        check_vma=False,
    )
```

```python
import functools
import math

import jax
import jax.numpy as jnp
from jax import lax
from jax.experimental import pallas as pl
from jax.experimental.pallas import tpu as pltpu
from jax.sharding import PartitionSpec as P

TOKENS = 16384
ROWS = 128
MODES = 8
FILTERS = 512
BLOCKS = 8
SUB = 8
RUN = ROWS // SUB
LANES = 128
STRIPS = FILTERS // LANES
PAIRS = BLOCKS // 2
WIDTH = BLOCKS * FILTERS
SHARDS = TOKENS // ROWS
PACKET = 5 * LANES
ALL = ("ctx", "fsdp")
f32 = jnp.float32
bf16 = jnp.bfloat16


def sublane():
    return lax.broadcasted_iota(jnp.int32, (SUB, LANES), 0)


def owner(strip, pair, n):
    return (strip * PAIRS + pair) * MODES + n


def lanes_of(at):
    return pl.ds(pl.multiple_of(at * LANES, LANES), LANES)


def piece(r):
    return pl.ds(r * LANES, LANES)


def spread(ref, at, natural):
    half = RUN // SUB
    for r in range(ROWS // SUB):
        start = (r % half) * SUB * SUB + r // half
        ref[at, pl.ds(start, SUB, stride=SUB), :] = natural[SUB * r : SUB * (r + 1), :]


def run_rows(ref, at, j):
    return ref[at, SUB * j : SUB * (j + 1), :]


def for_filters(make):
    def body(i, _):
        make(i)
        return 0

    lax.fori_loop(0, STRIPS * MODES, body, 0)


def row_of(ref, i):
    return jnp.broadcast_to(ref[pl.ds(i, 1), :], (SUB, LANES))


def total(parts):
    while len(parts) > 1:
        parts = [a + b for a, b in zip(parts[::2], parts[1::2])]
    return parts[0]


def prepare_kernel(q_hbm, k_hbm, v_hbm, u_hbm, ps, gs, q_ref, k_ref, v_ref, u_ref, sems):
    def copies(blk):
        cols = pl.ds(blk * FILTERS, FILTERS)
        return [
            pltpu.make_async_copy(src.at[:, cols], dst.at[:, cols], sems.at[blk, i])
            for i, (src, dst) in enumerate(
                ((k_hbm, k_ref), (v_hbm, v_ref), (u_hbm, u_ref), (q_hbm, q_ref))
            )
        ]

    for blk in range(BLOCKS):
        for copy in copies(blk):
            copy.start()
    for blk in range(BLOCKS):
        for copy in copies(blk):
            copy.wait()

        def strip_body(strip, _):
            at = blk * STRIPS + strip
            cols = lanes_of(at)
            spread(ps, at, k_ref[:, cols].astype(f32) * v_ref[:, cols].astype(f32))
            spread(gs, at, u_ref[:, cols].astype(f32) * q_ref[:, cols].astype(f32))
            return 0

        lax.fori_loop(0, STRIPS, strip_body, 0)


def summarize_kernel(
    half_ref, rate_ref, other_rate_ref, residue_ref, other_residue_ref, ps, gs,
    send_hbm, cf_hbm, cb_hbm, rates_hbm, residues_hbm,
    tab, send_ref, cf_ref, cb_ref, rates_ref, residues_ref, sems, param_sems,
):
    s = sublane()
    lower = jnp.broadcast_to(half_ref[0], (MODES, LANES)) == 0
    for strip in range(STRIPS):
        cols = pl.ds((strip % 2) * LANES, LANES)
        at = pl.ds(strip * MODES, MODES)
        for mine, other, out in (
            (rate_ref, other_rate_ref, rates_ref),
            (residue_ref, other_residue_ref, residues_ref),
        ):
            here, there = mine[:, cols], other[:, cols]
            if strip < STRIPS // 2:
                out[at, :] = jnp.where(lower, here, there)
            else:
                out[at, :] = jnp.where(lower, there, here)

    stored = [
        pltpu.make_async_copy(rates_ref, rates_hbm, param_sems.at[0]),
        pltpu.make_async_copy(residues_ref, residues_hbm, param_sems.at[1]),
    ]
    for copy in stored:
        copy.start()

    def make(i):
        log_decay = row_of(rates_ref, i) / TOKENS
        tab[0, i] = jnp.exp(-log_decay)
        for step in range(3):
            hop = 1 << step
            factor = jnp.exp(-log_decay * (RUN * hop))
            tab[1 + step, i] = jnp.where(s >= hop, factor, 0.0)
            tab[4 + step, i] = jnp.where(s < SUB - hop, factor, 0.0)

    for_filters(make)

    def sent(strip):
        at = pl.ds(strip * PAIRS * MODES, PAIRS * MODES)
        return [
            pltpu.make_async_copy(send_ref.at[at], send_hbm.at[at], sems.at[strip, 0]),
            pltpu.make_async_copy(cf_ref.at[strip], cf_hbm.at[strip], sems.at[strip, 1]),
            pltpu.make_async_copy(cb_ref.at[strip], cb_hbm.at[strip], sems.at[strip, 2]),
        ]

    def strip_body(strip, _):
        base = strip * MODES

        def pair_body(pair, _):
            gathered = [None] * MODES
            for odd in range(2):
                at = (2 * pair + odd) * STRIPS + strip
                decay = [tab[0, base + n] for n in range(MODES)]
                behind = [None] * MODES
                for j in reversed(range(RUN)):
                    gated = run_rows(gs, at, j)
                    for n in range(MODES):
                        behind[n] = gated if j == RUN - 1 else decay[n] * behind[n] + gated
                ahead, terms = [None] * MODES, [None] * MODES
                for j in range(RUN):
                    product, gated = run_rows(ps, at, j), run_rows(gs, at, j)
                    for n in range(MODES):
                        if j == 0:
                            ahead[n] = product
                            terms[n] = gated * product
                        else:
                            ahead[n] = decay[n] * ahead[n] + product
                            terms[n] = terms[n] + gated * ahead[n]
                first = list(behind)
                for step in range(3):
                    for n in range(MODES):
                        moved = pltpu.roll(ahead[n], 1 << step, 0)
                        ahead[n] = ahead[n] + tab[1 + step, base + n] * moved
                        moved = pltpu.roll(behind[n], SUB - (1 << step), 0)
                        behind[n] = behind[n] + tab[4 + step, base + n] * moved
                for n in range(MODES):
                    place = owner(strip, pair, n)
                    send_ref[place, :, piece(odd)] = ahead[n][SUB - 1 :, :]
                    send_ref[place, :, piece(2 + odd)] = behind[n][:1, :]
                    enter = jnp.where(s >= 1, pltpu.roll(ahead[n], 1, 0), 0.0)
                    leave = jnp.where(s < SUB - 1, pltpu.roll(behind[n], SUB - 1, 0), 0.0)
                    cf_ref[strip, 2 * pair + odd, n] = enter
                    cb_ref[strip, 2 * pair + odd, n] = leave
                    term = terms[n] + decay[n] * first[n] * enter
                    if odd == 0:
                        gathered[n] = term
                    else:
                        term = jnp.sum(gathered[n] + term, axis=0, keepdims=True)
                        send_ref[place, :, piece(4)] = term
            return 0

        lax.fori_loop(0, PAIRS, pair_body, 0)
        for copy in sent(strip):
            copy.start()
        return 0

    lax.fori_loop(0, STRIPS, strip_body, 0)
    for strip in range(STRIPS):
        for copy in sent(strip):
            copy.wait()
    for copy in stored:
        copy.wait()


def inner_kernel(reverse, rates_ref, residues_ref, one_ref, two_ref, enter_ref, out_ref, tab, xs):
    @pl.when(pl.program_id(0) == 0)
    def _():
        def make(i):
            rate = row_of(rates_ref, i)
            tab[0, i] = jnp.exp(-rate / TOKENS)
            tab[1, i] = row_of(residues_ref, i) * jnp.sqrt((1.0 + rate) / TOKENS)

        for_filters(make)

    def body(strip, _):
        base = strip * MODES
        cols = lanes_of(strip)
        spread(xs, 0, one_ref[:, cols].astype(f32) * two_ref[:, cols].astype(f32))
        decay = [tab[0, base + n] for n in range(MODES)]
        weight = [tab[1, base + n] for n in range(MODES)]
        state = [enter_ref[strip, 0, n] for n in range(MODES)]
        for j in reversed(range(RUN)) if reverse else range(RUN):
            x = run_rows(xs, 0, j)
            state = [decay[n] * state[n] + x for n in range(MODES)]
            mixed = total([weight[n] * state[n] for n in range(MODES)])
            out_ref[strip, pl.ds(j, SUB, stride=RUN), :] = mixed
        return 0

    lax.fori_loop(0, STRIPS, body, 0)


def carry_kernel(where_ref, rates_ref, x_ref, y_hbm, y_ref, sem):
    place = where_ref[0]
    at = (place // (PAIRS * MODES)) * MODES + place % MODES
    log_decay = rates_ref[pl.ds(at, 1), :] / TOKENS
    across = jnp.exp(-log_decay * ROWS)
    zero = jnp.zeros((1, LANES), f32)

    def step(i, carried):
        a0, a1, b0, b1, cross, terms = carried
        y_ref[i, :, piece(0)] = a0
        y_ref[i, :, piece(1)] = a1
        cross = cross + (a0 * x_ref[i, :, piece(2)] + a1 * x_ref[i, :, piece(3)])
        terms = terms + x_ref[i, :, piece(4)]
        back = SHARDS - 1 - i
        y_ref[back, :, piece(2)] = b0
        y_ref[back, :, piece(3)] = b1
        return (
            across * a0 + x_ref[i, :, piece(0)],
            across * a1 + x_ref[i, :, piece(1)],
            across * b0 + x_ref[back, :, piece(2)],
            across * b1 + x_ref[back, :, piece(3)],
            cross,
            terms,
        )

    carried = lax.fori_loop(0, SHARDS, step, (zero,) * 6, unroll=8)
    row = jnp.exp(-log_decay) * carried[4] + carried[5]

    def fill(i, _):
        y_ref[i, :, piece(4)] = row
        return 0

    lax.fori_loop(0, SHARDS, fill, 0, unroll=16)
    copy = pltpu.make_async_copy(y_ref, y_hbm, sem)
    copy.start()
    copy.wait()


def finish_kernel(
    rates_ref, residues_ref, k_hbm, v_hbm, u_hbm, conv_hbm, flow_hbm, in_ref,
    gq_hbm, gk_hbm, gv_hbm,
    tab, k_ref, v_ref, u_ref, conv_ref, flow_ref, gq_ref, gk_ref, gv_ref, arrive_sems, sems,
):
    s = sublane()

    def arrivals(blk):
        cols = pl.ds(blk * FILTERS, FILTERS)
        if not isinstance(blk, int):
            cols = pl.ds(pl.multiple_of(blk * FILTERS, FILTERS), FILTERS)
        deep = pl.ds(blk * STRIPS, STRIPS)
        pairs = [(a.at[deep], b.at[deep]) for a, b in ((conv_hbm, conv_ref), (flow_hbm, flow_ref))]
        for a, b in ((u_hbm, u_ref), (v_hbm, v_ref), (k_hbm, k_ref)):
            pairs.append((a.at[:, cols], b.at[:, cols]))
        return [
            pltpu.make_async_copy(a, b, arrive_sems.at[blk, i]) for i, (a, b) in enumerate(pairs)
        ]

    for blk in range(BLOCKS):
        for copy in arrivals(blk):
            copy.start()

    def make(i):
        rate = row_of(rates_ref, i)
        log_decay = rate / TOKENS
        weight = row_of(residues_ref, i) * jnp.sqrt((1.0 + rate) / TOKENS)
        tab[0, i] = jnp.exp(-log_decay * SUB)
        tab[1, i] = weight * jnp.exp(-log_decay * (s + 1).astype(f32))
        tab[2, i] = weight * jnp.exp(-log_decay * (SUB - s).astype(f32))

    for_filters(make)

    def copies(blk):
        cols = pl.ds(pl.multiple_of(blk * FILTERS, FILTERS), FILTERS)
        return [
            pltpu.make_async_copy(src.at[:, cols], dst.at[:, cols], sems.at[blk, i])
            for i, (src, dst) in enumerate(((gq_ref, gq_hbm), (gk_ref, gk_hbm), (gv_ref, gv_hbm)))
        ]

    def pair_body(pair, _):
        for odd in range(2):
            blk = 2 * pair + odd
            for copy in arrivals(blk):
                copy.wait()

            def strip_body(strip, _):
                base = strip * MODES
                col = blk * STRIPS + strip
                cols = lanes_of(col)
                leap = [tab[0, base + n] for n in range(MODES)]
                places = [owner(strip, pair, n) for n in range(MODES)]
                state = [
                    tab[1, base + n] * in_ref[places[n], :, piece(odd)] for n in range(MODES)
                ]
                for i in range(ROWS // 16):
                    parts = []
                    for _ in range(2):
                        parts.append(total(state))
                        state = [leap[n] * state[n] for n in range(MODES)]
                    at = pl.ds(16 * i, 16)
                    conv = conv_ref[col, at, :] + jnp.concatenate(parts, axis=0)
                    gq_ref[at, cols] = (u_ref[at, cols].astype(f32) * conv).astype(bf16)
                state = [
                    tab[2, base + n] * in_ref[places[n], :, piece(2 + odd)] for n in range(MODES)
                ]
                for i in reversed(range(ROWS // 16)):
                    parts = []
                    for _ in range(2):
                        parts.insert(0, total(state))
                        state = [leap[n] * state[n] for n in range(MODES)]
                    at = pl.ds(16 * i, 16)
                    flow = flow_ref[col, at, :] + jnp.concatenate(parts, axis=0)
                    gk_ref[at, cols] = (flow * v_ref[at, cols].astype(f32)).astype(bf16)
                    gv_ref[at, cols] = (flow * k_ref[at, cols].astype(f32)).astype(bf16)
                return 0

            lax.fori_loop(0, STRIPS, strip_body, 0)
            for copy in copies(blk):
                copy.start()
        return 0

    lax.fori_loop(0, PAIRS, pair_body, 0)
    for blk in range(BLOCKS):
        for copy in copies(blk):
            copy.wait()


def in_hbm(*arrays):
    return [pltpu.with_memory_space_constraint(a, pltpu.HBM) for a in arrays]


def local(query_rows, key_rows, value_rows, upstream, decay_rate, residue):
    half = lax.axis_index("fsdp")
    swap = [(0, 1), (1, 0)]
    other_rate = lax.ppermute(decay_rate, "fsdp", swap)
    other_residue = lax.ppermute(residue, "fsdp", swap)
    vmem = pl.BlockSpec(memory_space=pltpu.VMEM)
    smem = pl.BlockSpec(memory_space=pltpu.SMEM)
    hbm = pl.BlockSpec(memory_space=pltpu.HBM)
    limit = pltpu.CompilerParams(vmem_limit_bytes=16 << 20)
    packet = (SHARDS, 1, PACKET)
    packets = pltpu.HBM(packet, f32)
    tiles = (BLOCKS * STRIPS, ROWS, LANES)
    state = (STRIPS, BLOCKS, MODES, SUB, LANES)
    params = (STRIPS * MODES, LANES)
    table = (STRIPS * MODES, SUB, LANES)
    whole = pltpu.VMEM((ROWS, WIDTH), bf16)
    query_rows, key_rows, value_rows, upstream = in_hbm(
        query_rows, key_rows, value_rows, upstream
    )
    ps, gs = pl.pallas_call(
        prepare_kernel,
        in_specs=[hbm] * 4,
        out_specs=[vmem] * 2,
        out_shape=[jax.ShapeDtypeStruct(tiles, f32)] * 2,
        scratch_shapes=[whole] * 4 + [pltpu.SemaphoreType.DMA((BLOCKS, 4))],
        compiler_params=limit,
        cost_estimate=pl.CostEstimate(flops=1 << 22, bytes_accessed=12 << 20, transcendentals=0),
        name="prepare",
    )(query_rows, key_rows, value_rows, upstream)
    send, enter_ahead, enter_behind, rates, residues = pl.pallas_call(
        summarize_kernel,
        in_specs=[smem] + [vmem] * 6,
        out_specs=[hbm] * 5,
        out_shape=[packets] + [pltpu.HBM(state, f32)] * 2 + [pltpu.HBM(params, f32)] * 2,
        scratch_shapes=[
            pltpu.VMEM((7,) + table, f32),
            pltpu.VMEM(packet, f32),
            pltpu.VMEM(state, f32),
            pltpu.VMEM(state, f32),
            pltpu.VMEM(params, f32),
            pltpu.VMEM(params, f32),
            pltpu.SemaphoreType.DMA((STRIPS, 3)),
            pltpu.SemaphoreType.DMA((2,)),
        ],
        compiler_params=limit,
        name="summarize",
    )(half.astype(jnp.int32).reshape(1), decay_rate, other_rate, residue, other_residue, ps, gs)
    arrived = lax.all_to_all(send, ALL, 0, 0, tiled=True)

    def inner(one, two, enter, reverse):
        wide = pl.BlockSpec((ROWS, FILTERS), lambda b: (0, b))
        param = pl.BlockSpec((STRIPS * MODES, LANES), lambda b: (0, 0))
        return pl.pallas_call(
            functools.partial(inner_kernel, reverse),
            grid=(BLOCKS,),
            in_specs=[param] * 2
            + [wide] * 2
            + [pl.BlockSpec((STRIPS, 1, MODES, SUB, LANES), lambda b: (0, b, 0, 0, 0))],
            out_specs=pl.BlockSpec((STRIPS, ROWS, LANES), lambda b: (b, 0, 0)),
            out_shape=pltpu.HBM(tiles, f32),
            scratch_shapes=[pltpu.VMEM((2,) + table, f32), pltpu.VMEM((1, ROWS, LANES), f32)],
            cost_estimate=pl.CostEstimate(
                flops=1 << 24, bytes_accessed=16 << 20, transcendentals=0
            ),
            name="behind" if reverse else "ahead",
        )(rates, residues, one, two, enter)

    conv = inner(key_rows, value_rows, enter_ahead, False)
    arrived, conv = lax.optimization_barrier((arrived, conv))
    place = lax.axis_index(ALL).astype(jnp.int32).reshape(1)
    carries = pl.pallas_call(
        carry_kernel,
        in_specs=[smem] + [vmem] * 2,
        out_specs=hbm,
        out_shape=packets,
        scratch_shapes=[pltpu.VMEM(packet, f32), pltpu.SemaphoreType.DMA],
        compiler_params=limit,
        name="carry",
    )(place, rates, arrived)
    back = lax.all_to_all(carries, ALL, 0, 0, tiled=True)
    flowing = inner(upstream, query_rows, enter_behind, True)
    back, flowing = lax.optimization_barrier((back, flowing))
    rows = back[:, 0, 4 * LANES :].reshape(STRIPS, PAIRS, MODES, LANES)
    count = STRIPS // 2
    rows = lax.dynamic_slice_in_dim(rows, half * count, count, 0).sum(axis=1)
    rows = rows + lax.ppermute(rows, "ch", swap)
    rows = rows.transpose(1, 0, 2).reshape(MODES, count * LANES)
    gain = jnp.sqrt((1.0 + decay_rate) / TOKENS)
    residue_grad = gain * rows / math.sqrt(TOKENS)
    conv, flowing = in_hbm(conv, flowing)
    grads_out = pl.pallas_call(
        finish_kernel,
        in_specs=[vmem] * 2 + [hbm] * 5 + [vmem],
        out_specs=[hbm] * 3,
        out_shape=[pltpu.HBM((ROWS, WIDTH), bf16)] * 3,
        scratch_shapes=[
            pltpu.VMEM((3,) + table, f32),
            whole,
            whole,
            whole,
            pltpu.VMEM(tiles, f32),
            pltpu.VMEM(tiles, f32),
            whole,
            whole,
            whole,
            pltpu.SemaphoreType.DMA((BLOCKS, 5)),
            pltpu.SemaphoreType.DMA((BLOCKS, 3)),
        ],
        compiler_params=limit,
        name="finish",
    )(rates, residues, key_rows, value_rows, upstream, conv, flowing, back)
    return (*grads_out, residue_grad)


def solution(mesh):
    rows = P(ALL, "ch")
    params = P(None, "fsdp")
    return jax.shard_map(
        local,
        mesh=mesh,
        in_specs=(rows, rows, rows, rows, params, params),
        out_specs=(rows, rows, rows, params),
        check_vma=False,
    )
```

```python
import functools
import math

import jax
import jax.numpy as jnp
from jax import lax
from jax.experimental import pallas as pl
from jax.experimental.pallas import tpu as pltpu
from jax.sharding import PartitionSpec as P

TOKENS = 16384
ROWS = 128
MODES = 8
FILTERS = 512
BLOCKS = 8
SUB = 8
RUN = ROWS // SUB
HALF = RUN // 2
LANES = 128
STRIPS = FILTERS // LANES
PAIRS = BLOCKS // 2
WIDTH = BLOCKS * FILTERS
SHARDS = TOKENS // ROWS
PACKET = 5 * LANES
ALL = ("ctx", "fsdp")
f32 = jnp.float32
bf16 = jnp.bfloat16


def sublane():
    return lax.broadcasted_iota(jnp.int32, (SUB, LANES), 0)


def owner(strip, pair, n):
    return (strip * PAIRS + pair) * MODES + n


def lanes_of(at):
    return pl.ds(pl.multiple_of(at * LANES, LANES), LANES)


def piece(r):
    return pl.ds(r * LANES, LANES)


def spread(ref, at, natural):
    half = RUN // SUB
    for r in range(ROWS // SUB):
        start = (r % half) * SUB * SUB + r // half
        ref[(*at, pl.ds(start, SUB, stride=SUB))] = natural[SUB * r : SUB * (r + 1), :]


def run_rows(ref, at, j):
    return ref[(*at, pl.ds(SUB * j, SUB))]


def for_filters(make):
    def body(i, _):
        make(i)
        return 0

    lax.fori_loop(0, STRIPS * MODES, body, 0)


def row_of(ref, i):
    return jnp.broadcast_to(ref[pl.ds(i, 1), :], (SUB, LANES))


def total(parts):
    while len(parts) > 1:
        parts = [a + b for a, b in zip(parts[::2], parts[1::2])]
    return parts[0]


def prepare_kernel(q_hbm, k_hbm, v_hbm, u_hbm, ps, gs, q_ref, k_ref, v_ref, u_ref, sems):
    def copies(blk):
        cols = pl.ds(blk * FILTERS, FILTERS)
        return [
            pltpu.make_async_copy(src.at[:, cols], dst.at[:, cols], sems.at[blk, i])
            for i, (src, dst) in enumerate(
                ((k_hbm, k_ref), (v_hbm, v_ref), (u_hbm, u_ref), (q_hbm, q_ref))
            )
        ]

    for blk in range(BLOCKS):
        for copy in copies(blk):
            copy.start()
    for blk in range(BLOCKS):
        for copy in copies(blk):
            copy.wait()

        def strip_body(strip, _):
            at = (strip, blk)
            cols = lanes_of(blk * STRIPS + strip)
            spread(ps, at, k_ref[:, cols].astype(f32) * v_ref[:, cols].astype(f32))
            spread(gs, at, u_ref[:, cols].astype(f32) * q_ref[:, cols].astype(f32))
            return 0

        lax.fori_loop(0, STRIPS, strip_body, 0)


def summarize_kernel(
    half_ref, mine_ref, other_ref, ps, gs,
    send_hbm, cf_hbm, cb_hbm, rates_hbm, residues_hbm, ps_hbm, gs_hbm,
    tab, lags, joins, send_ref, cf_ref, cb_ref, rates_ref, residues_ref, sems, early_sems,
):
    s = sublane()
    lower = jnp.broadcast_to(half_ref[0], (MODES, LANES)) == 0
    for strip in range(STRIPS):
        cols = pl.ds((strip % 2) * LANES, LANES)
        at = pl.ds(strip * MODES, MODES)
        for part, out in enumerate((rates_ref, residues_ref)):
            rows = pl.ds(part * MODES, MODES)
            here, there = mine_ref[rows, cols], other_ref[rows, cols]
            if strip < STRIPS // 2:
                out[at, :] = jnp.where(lower, here, there)
            else:
                out[at, :] = jnp.where(lower, there, here)

    stored = [
        pltpu.make_async_copy(a, b, early_sems.at[i])
        for i, (a, b) in enumerate(
            ((rates_ref, rates_hbm), (residues_ref, residues_hbm), (ps, ps_hbm), (gs, gs_hbm))
        )
    ]
    for copy in stored:
        copy.start()

    def make(i):
        log_decay = row_of(rates_ref, i) / TOKENS
        tab[0, i] = jnp.exp(-log_decay)
        for step in range(3):
            hop = 1 << step
            factor = jnp.exp(-log_decay * (RUN * hop))
            tab[1 + step, i] = jnp.where(s >= hop, factor, 0.0)
        tab[4, i] = jnp.exp(-log_decay * (RUN * s).astype(f32))

    for_filters(make)

    def sent(strip):
        at = pl.ds(strip * PAIRS * MODES, PAIRS * MODES)
        return [
            pltpu.make_async_copy(send_ref.at[at], send_hbm.at[at], sems.at[strip, 0]),
            pltpu.make_async_copy(cf_ref.at[strip], cf_hbm.at[strip], sems.at[strip, 1]),
            pltpu.make_async_copy(cb_ref.at[strip], cb_hbm.at[strip], sems.at[strip, 2]),
        ]

    def strip_body(strip, _):
        base = strip * MODES

        for lag in range(HALF):
            lags[lag] = jnp.zeros((SUB, LANES), f32)
        for n in range(MODES):
            joins[n] = jnp.zeros((SUB, LANES), f32)

        def pair_body(pair, _):
            for odd in range(2):
                at = (strip, 2 * pair + odd)
                decay = [tab[0, base + n] for n in range(MODES)]
                behind, middle = [None] * MODES, [None] * MODES
                for j in reversed(range(RUN)):
                    gated = run_rows(gs, at, j)
                    for n in range(MODES):
                        behind[n] = gated if j == RUN - 1 else decay[n] * behind[n] + gated
                    if j == HALF:
                        middle = list(behind)
                ahead, joint = [None] * MODES, [None] * MODES
                for j in range(RUN):
                    product = run_rows(ps, at, j)
                    for n in range(MODES):
                        ahead[n] = product if j == 0 else decay[n] * ahead[n] + product
                        if j == HALF - 1:
                            joint[n] = ahead[n] * middle[n]
                for lag in range(HALF):
                    starts = [j for j in range(RUN) if j // HALF == (j + lag) // HALF]
                    pairs = [run_rows(gs, at, j + lag) * run_rows(ps, at, j) for j in starts]
                    while len(pairs) > 1:
                        odd_one = pairs[-1:] if len(pairs) % 2 else []
                        pairs = [a + b for a, b in zip(pairs[::2], pairs[1::2])] + odd_one
                    lags[lag] = lags[lag] + pairs[0]
                for step in range(3):
                    for n in range(MODES):
                        moved = pltpu.roll(ahead[n], 1 << step, 0)
                        ahead[n] = ahead[n] + tab[1 + step, base + n] * moved
                for n in range(MODES):
                    place = owner(strip, pair, n)
                    send_ref[place, :, piece(odd)] = ahead[n][SUB - 1 :, :]
                    first = jnp.sum(tab[4, base + n] * behind[n], axis=0, keepdims=True)
                    send_ref[place, :, piece(2 + odd)] = first
                    enter = jnp.where(s >= 1, pltpu.roll(ahead[n], 1, 0), 0.0)
                    cf_ref[strip, 2 * pair + odd, n] = enter
                    cb_ref[strip, 2 * pair + odd, n] = behind[n]
                    joins[n] = joins[n] + (joint[n] + behind[n] * enter)
            return 0

        lax.fori_loop(0, PAIRS, pair_body, 0)
        for n in range(MODES):
            decay = tab[0, base + n]
            term = lags[HALF - 1]
            for lag in reversed(range(HALF - 1)):
                term = decay * term + lags[lag]
            term = jnp.sum(term + decay * joins[n], axis=0, keepdims=True)
            for pair in range(PAIRS):
                row = term if pair == 0 else jnp.zeros((1, LANES), f32)
                send_ref[owner(strip, pair, n), :, piece(4)] = row
        for copy in sent(strip):
            copy.start()
        return 0

    lax.fori_loop(0, STRIPS, strip_body, 0)
    for strip in range(STRIPS):
        for copy in sent(strip):
            copy.wait()
    for copy in stored:
        copy.wait()


def inner_kernel(
    reverse, rates_hbm, residues_hbm, xs_hbm, enter_hbm, out_hbm,
    tab, rates_ref, residues_ref, xs, enter_ref, out_ref, param_sems, sems,
):
    params = [
        pltpu.make_async_copy(rates_hbm, rates_ref, param_sems.at[0]),
        pltpu.make_async_copy(residues_hbm, residues_ref, param_sems.at[1]),
    ]

    def arrivals(strip):
        return [
            pltpu.make_async_copy(enter_hbm.at[strip], enter_ref.at[strip], sems.at[strip, 0]),
            pltpu.make_async_copy(xs_hbm.at[strip], xs.at[strip], sems.at[strip, 1]),
        ]

    def leaving(strip):
        return pltpu.make_async_copy(out_ref.at[strip], out_hbm.at[strip], sems.at[strip, 2])

    s = sublane()
    for copy in params:
        copy.start()
    for strip in range(STRIPS):
        for copy in arrivals(strip):
            copy.start()
    for copy in params:
        copy.wait()

    def make(i):
        rate = row_of(rates_ref, i)
        tab[0, i] = jnp.exp(-rate / TOKENS)
        tab[1, i] = row_of(residues_ref, i) * jnp.sqrt((1.0 + rate) / TOKENS)
        for step in range(3 if reverse else 0):
            factor = jnp.exp(-rate / TOKENS * (RUN << step))
            tab[2 + step, i] = jnp.where(s < SUB - (1 << step), factor, 0.0)

    for_filters(make)

    def strip_body(strip, _):
        for copy in arrivals(strip):
            copy.wait()
        base = strip * MODES

        def body(blk, _):
            at = (strip, blk)
            decay = [tab[0, base + n] for n in range(MODES)]
            weight = [tab[1, base + n] for n in range(MODES)]
            state = [enter_ref[strip, blk, n] for n in range(MODES)]
            if reverse:
                for step in range(3):
                    for n in range(MODES):
                        moved = pltpu.roll(state[n], SUB - (1 << step), 0)
                        state[n] = state[n] + tab[2 + step, base + n] * moved
                state = [jnp.where(s < SUB - 1, pltpu.roll(a, SUB - 1, 0), 0.0) for a in state]
            for j in reversed(range(RUN)) if reverse else range(RUN):
                x = run_rows(xs, at, j)
                state = [decay[n] * state[n] + x for n in range(MODES)]
                mixed = total([weight[n] * state[n] for n in range(MODES)])
                out_ref[strip, blk, pl.ds(j, SUB, stride=RUN), :] = mixed
            return 0

        lax.fori_loop(0, BLOCKS, body, 0)
        leaving(strip).start()
        return 0

    lax.fori_loop(0, STRIPS, strip_body, 0)
    for strip in range(STRIPS):
        leaving(strip).wait()


def carry_kernel(where_ref, rates_ref, x_ref, y_hbm, y_ref, sem):
    place = where_ref[0]
    at = (place // (PAIRS * MODES)) * MODES + place % MODES
    log_decay = rates_ref[pl.ds(at, 1), :] / TOKENS
    across = jnp.exp(-log_decay * ROWS)
    zero = jnp.zeros((1, LANES), f32)

    def step(i, carried):
        a0, a1, b0, b1, cross, terms = carried
        y_ref[i, :, piece(0)] = a0
        y_ref[i, :, piece(1)] = a1
        cross = cross + (a0 * x_ref[i, :, piece(2)] + a1 * x_ref[i, :, piece(3)])
        terms = terms + x_ref[i, :, piece(4)]
        back = SHARDS - 1 - i
        y_ref[back, :, piece(2)] = b0
        y_ref[back, :, piece(3)] = b1
        return (
            across * a0 + x_ref[i, :, piece(0)],
            across * a1 + x_ref[i, :, piece(1)],
            across * b0 + x_ref[back, :, piece(2)],
            across * b1 + x_ref[back, :, piece(3)],
            cross,
            terms,
        )

    carried = lax.fori_loop(0, SHARDS, step, (zero,) * 6, unroll=8)
    row = jnp.exp(-log_decay) * carried[4] + carried[5]

    def fill(i, _):
        y_ref[i, :, piece(4)] = row
        return 0

    lax.fori_loop(0, SHARDS, fill, 0, unroll=16)
    copy = pltpu.make_async_copy(y_ref, y_hbm, sem)
    copy.start()
    copy.wait()


def finish_kernel(
    rates_ref, residues_ref, k_hbm, v_hbm, u_hbm, conv_hbm, flow_hbm, in_ref,
    gq_hbm, gk_hbm, gv_hbm,
    tab, k_ref, v_ref, u_ref, conv_ref, flow_ref, gq_ref, gk_ref, gv_ref, arrive_sems, sems,
):
    s = sublane()

    def arrivals(blk):
        cols = pl.ds(blk * FILTERS, FILTERS)
        if not isinstance(blk, int):
            cols = pl.ds(pl.multiple_of(blk * FILTERS, FILTERS), FILTERS)
        pairs = [
            (a.at[:, blk], b.at[:, blk]) for a, b in ((conv_hbm, conv_ref), (flow_hbm, flow_ref))
        ]
        for a, b in ((u_hbm, u_ref), (v_hbm, v_ref), (k_hbm, k_ref)):
            pairs.append((a.at[:, cols], b.at[:, cols]))
        return [
            pltpu.make_async_copy(a, b, arrive_sems.at[blk, i]) for i, (a, b) in enumerate(pairs)
        ]

    for blk in range(BLOCKS):
        for copy in arrivals(blk):
            copy.start()

    def make(i):
        rate = row_of(rates_ref, i)
        log_decay = rate / TOKENS
        weight = row_of(residues_ref, i) * jnp.sqrt((1.0 + rate) / TOKENS)
        tab[0, i] = jnp.exp(-log_decay * SUB)
        tab[1, i] = weight * jnp.exp(-log_decay * (s + 1).astype(f32))
        tab[2, i] = weight * jnp.exp(-log_decay * (SUB - s).astype(f32))

    for_filters(make)

    def copies(blk):
        cols = pl.ds(pl.multiple_of(blk * FILTERS, FILTERS), FILTERS)
        return [
            pltpu.make_async_copy(src.at[:, cols], dst.at[:, cols], sems.at[blk, i])
            for i, (src, dst) in enumerate(((gq_ref, gq_hbm), (gk_ref, gk_hbm), (gv_ref, gv_hbm)))
        ]

    def pair_body(pair, _):
        for odd in range(2):
            blk = 2 * pair + odd
            for copy in arrivals(blk):
                copy.wait()

            def strip_body(strip, _):
                base = strip * MODES
                cols = lanes_of(blk * STRIPS + strip)
                leap = [tab[0, base + n] for n in range(MODES)]
                places = [owner(strip, pair, n) for n in range(MODES)]
                state = [
                    tab[1, base + n] * in_ref[places[n], :, piece(odd)] for n in range(MODES)
                ]
                for i in range(ROWS // 16):
                    parts = []
                    for _ in range(2):
                        parts.append(total(state))
                        state = [leap[n] * state[n] for n in range(MODES)]
                    at = pl.ds(16 * i, 16)
                    conv = conv_ref[strip, blk, at, :] + jnp.concatenate(parts, axis=0)
                    gq_ref[at, cols] = (u_ref[at, cols].astype(f32) * conv).astype(bf16)
                state = [
                    tab[2, base + n] * in_ref[places[n], :, piece(2 + odd)] for n in range(MODES)
                ]
                for i in reversed(range(ROWS // 16)):
                    parts = []
                    for _ in range(2):
                        parts.insert(0, total(state))
                        state = [leap[n] * state[n] for n in range(MODES)]
                    at = pl.ds(16 * i, 16)
                    flow = flow_ref[strip, blk, at, :] + jnp.concatenate(parts, axis=0)
                    gk_ref[at, cols] = (flow * v_ref[at, cols].astype(f32)).astype(bf16)
                    gv_ref[at, cols] = (flow * k_ref[at, cols].astype(f32)).astype(bf16)
                return 0

            lax.fori_loop(0, STRIPS, strip_body, 0)
            for copy in copies(blk):
                copy.start()
        return 0

    lax.fori_loop(0, PAIRS, pair_body, 0)
    for blk in range(BLOCKS):
        for copy in copies(blk):
            copy.wait()


def in_hbm(*arrays):
    return [pltpu.with_memory_space_constraint(a, pltpu.HBM) for a in arrays]


def local(query_rows, key_rows, value_rows, upstream, decay_rate, residue):
    half = lax.axis_index("fsdp")
    swap = [(0, 1), (1, 0)]
    first = lax.broadcasted_iota(jnp.int32, (2 * MODES, FILTERS // 2), 0) < MODES
    below, above = ((0, MODES, 0), (0, 0, 0)), ((MODES, 0, 0), (0, 0, 0))
    zero = jnp.zeros((), f32)
    mine = jnp.where(first, lax.pad(decay_rate, zero, below), lax.pad(residue, zero, above))
    other = lax.ppermute(mine, "fsdp", swap)
    vmem = pl.BlockSpec(memory_space=pltpu.VMEM)
    smem = pl.BlockSpec(memory_space=pltpu.SMEM)
    hbm = pl.BlockSpec(memory_space=pltpu.HBM)
    limit = pltpu.CompilerParams(vmem_limit_bytes=16 << 20)
    packet = (SHARDS, 1, PACKET)
    packets = pltpu.HBM(packet, f32)
    tiles = (STRIPS, BLOCKS, ROWS, LANES)
    state = (STRIPS, BLOCKS, MODES, SUB, LANES)
    params = (STRIPS * MODES, LANES)
    table = (STRIPS * MODES, SUB, LANES)
    whole = pltpu.VMEM((ROWS, WIDTH), bf16)
    query_rows, key_rows, value_rows, upstream = in_hbm(
        query_rows, key_rows, value_rows, upstream
    )
    ps, gs = pl.pallas_call(
        prepare_kernel,
        in_specs=[hbm] * 4,
        out_specs=[vmem] * 2,
        out_shape=[jax.ShapeDtypeStruct(tiles, f32)] * 2,
        scratch_shapes=[whole] * 4 + [pltpu.SemaphoreType.DMA((BLOCKS, 4))],
        compiler_params=limit,
        cost_estimate=pl.CostEstimate(flops=1 << 22, bytes_accessed=12 << 20, transcendentals=0),
        name="prepare",
    )(query_rows, key_rows, value_rows, upstream)
    send, enter_ahead, enter_behind, rates, residues, product, gated = pl.pallas_call(
        summarize_kernel,
        in_specs=[smem] + [vmem] * 4,
        out_specs=[hbm] * 7,
        out_shape=[packets]
        + [pltpu.HBM(state, f32)] * 2
        + [pltpu.HBM(params, f32)] * 2
        + [pltpu.HBM(tiles, f32)] * 2,
        scratch_shapes=[
            pltpu.VMEM((5,) + table, f32),
            pltpu.VMEM((HALF, SUB, LANES), f32),
            pltpu.VMEM((MODES, SUB, LANES), f32),
            pltpu.VMEM(packet, f32),
            pltpu.VMEM(state, f32),
            pltpu.VMEM(state, f32),
            pltpu.VMEM(params, f32),
            pltpu.VMEM(params, f32),
            pltpu.SemaphoreType.DMA((STRIPS, 3)),
            pltpu.SemaphoreType.DMA((4,)),
        ],
        compiler_params=limit,
        name="summarize",
    )(half.astype(jnp.int32).reshape(1), mine, other, ps, gs)
    arrived = lax.all_to_all(send, ALL, 0, 0, tiled=True)

    def inner(xs, enter, reverse):
        return pl.pallas_call(
            functools.partial(inner_kernel, reverse),
            in_specs=[hbm] * 4,
            out_specs=hbm,
            out_shape=pltpu.HBM(tiles, f32),
            scratch_shapes=[
                pltpu.VMEM((5 if reverse else 2,) + table, f32),
                pltpu.VMEM(params, f32),
                pltpu.VMEM(params, f32),
                pltpu.VMEM(tiles, f32),
                pltpu.VMEM(state, f32),
                pltpu.VMEM(tiles, f32),
                pltpu.SemaphoreType.DMA((2,)),
                pltpu.SemaphoreType.DMA((STRIPS, 3)),
            ],
            cost_estimate=pl.CostEstimate(
                flops=1 << 24, bytes_accessed=16 << 20, transcendentals=0
            ),
            name="behind" if reverse else "ahead",
        )(rates, residues, xs, enter)

    conv = inner(product, enter_ahead, False)
    arrived, conv = lax.optimization_barrier((arrived, conv))
    place = lax.axis_index(ALL).astype(jnp.int32).reshape(1)
    carries = pl.pallas_call(
        carry_kernel,
        in_specs=[smem] + [vmem] * 2,
        out_specs=hbm,
        out_shape=packets,
        scratch_shapes=[pltpu.VMEM(packet, f32), pltpu.SemaphoreType.DMA],
        compiler_params=limit,
        name="carry",
    )(place, rates, arrived)
    back = lax.all_to_all(carries, ALL, 0, 0, tiled=True)
    flowing = inner(gated, enter_behind, True)
    back, flowing = lax.optimization_barrier((back, flowing))
    rows = back[:, 0, 4 * LANES :].reshape(STRIPS, PAIRS, MODES, LANES)
    count = STRIPS // 2
    rows = lax.dynamic_slice_in_dim(rows, half * count, count, 0).sum(axis=1)
    rows = rows + lax.ppermute(rows, "ch", swap)
    rows = rows.transpose(1, 0, 2).reshape(MODES, count * LANES)
    gain = jnp.sqrt((1.0 + decay_rate) / TOKENS)
    residue_grad = gain * rows / math.sqrt(TOKENS)
    conv, flowing = in_hbm(conv, flowing)
    grads_out = pl.pallas_call(
        finish_kernel,
        in_specs=[vmem] * 2 + [hbm] * 5 + [vmem],
        out_specs=[hbm] * 3,
        out_shape=[pltpu.HBM((ROWS, WIDTH), bf16)] * 3,
        scratch_shapes=[
            pltpu.VMEM((3,) + table, f32),
            whole,
            whole,
            whole,
            pltpu.VMEM(tiles, f32),
            pltpu.VMEM(tiles, f32),
            whole,
            whole,
            whole,
            pltpu.SemaphoreType.DMA((BLOCKS, 5)),
            pltpu.SemaphoreType.DMA((BLOCKS, 3)),
        ],
        compiler_params=limit,
        name="finish",
    )(rates, residues, key_rows, value_rows, upstream, conv, flowing, back)
    return (*grads_out, residue_grad)


def solution(mesh):
    rows = P(ALL, "ch")
    params = P(None, "fsdp")
    return jax.shard_map(
        local,
        mesh=mesh,
        in_specs=(rows, rows, rows, rows, params, params),
        out_specs=(rows, rows, rows, params),
        check_vma=False,
    )
```

```python
import functools
import math

import jax
import jax.numpy as jnp
from jax import lax
from jax.experimental import pallas as pl
from jax.experimental.pallas import tpu as pltpu
from jax.sharding import Mesh
from jax.sharding import PartitionSpec as P

TOKENS = 16384
ROWS = 128
MODES = 8
FILTERS = 512
BLOCKS = 8
SUB = 8
RUN = ROWS // SUB
HALF = RUN // 2
LANES = 128
STRIPS = FILTERS // LANES
PAIRS = BLOCKS // 2
WIDTH = BLOCKS * FILTERS
SHARDS = TOKENS // ROWS
LINE = MODES
LINES = SHARDS // LINE
BACK = STRIPS * BLOCKS
TERMS = 2 * BACK
DEPTH = TERMS + SUB
ALONG = ("zh", "fsdp")
ALL = ("yx",) + ALONG
f32 = jnp.float32
bf16 = jnp.bfloat16


def sublane():
    return lax.broadcasted_iota(jnp.int32, (SUB, LANES), 0)


def lanes_of(at):
    return pl.ds(pl.multiple_of(at * LANES, LANES), LANES)


def spread(ref, at, natural):
    half = RUN // SUB
    for r in range(ROWS // SUB):
        start = (r % half) * SUB * SUB + r // half
        ref[(*at, pl.ds(start, SUB, stride=SUB))] = natural[SUB * r : SUB * (r + 1), :]


def run_rows(ref, at, j):
    return ref[(*at, pl.ds(SUB * j, SUB))]


def for_filters(make):
    def body(i, _):
        make(i)
        return 0

    lax.fori_loop(0, STRIPS * MODES, body, 0)


def row_of(ref, i):
    return jnp.broadcast_to(ref[pl.ds(i, 1), :], (SUB, LANES))


def total(parts):
    while len(parts) > 1:
        parts = [a + b for a, b in zip(parts[::2], parts[1::2])]
    return parts[0]


def prepare_kernel(q_hbm, k_hbm, v_hbm, u_hbm, ps, gs, q_ref, k_ref, v_ref, u_ref, sems):
    def copies(blk):
        cols = pl.ds(blk * FILTERS, FILTERS)
        return [
            pltpu.make_async_copy(src.at[:, cols], dst.at[:, cols], sems.at[blk, i])
            for i, (src, dst) in enumerate(
                ((k_hbm, k_ref), (v_hbm, v_ref), (u_hbm, u_ref), (q_hbm, q_ref))
            )
        ]

    for blk in range(BLOCKS):
        for copy in copies(blk):
            copy.start()
    for blk in range(BLOCKS):
        for copy in copies(blk):
            copy.wait()

        def strip_body(strip, _):
            at = (strip, blk)
            cols = lanes_of(blk * STRIPS + strip)
            spread(ps, at, k_ref[:, cols].astype(f32) * v_ref[:, cols].astype(f32))
            spread(gs, at, u_ref[:, cols].astype(f32) * q_ref[:, cols].astype(f32))
            return 0

        lax.fori_loop(0, STRIPS, strip_body, 0)


def summarize_kernel(
    half_ref, mine_ref, other_ref, ps, gs,
    send_hbm, cf_hbm, cb_hbm, rates_hbm, residues_hbm, ps_hbm, gs_hbm,
    tab, lags, joins, send_ref, cf_ref, cb_ref, rates_ref, residues_ref, sems, early_sems,
):
    s = sublane()
    lower = jnp.broadcast_to(half_ref[0], (MODES, LANES)) == 0
    for strip in range(STRIPS):
        cols = pl.ds((strip % 2) * LANES, LANES)
        at = pl.ds(strip * MODES, MODES)
        for part, out in enumerate((rates_ref, residues_ref)):
            rows = pl.ds(part * MODES, MODES)
            here, there = mine_ref[rows, cols], other_ref[rows, cols]
            if strip < STRIPS // 2:
                out[at, :] = jnp.where(lower, here, there)
            else:
                out[at, :] = jnp.where(lower, there, here)

    stored = [
        pltpu.make_async_copy(a, b, early_sems.at[i])
        for i, (a, b) in enumerate(
            ((rates_ref, rates_hbm), (residues_ref, residues_hbm), (ps, ps_hbm), (gs, gs_hbm))
        )
    ]
    for copy in stored:
        copy.start()

    def make(i):
        log_decay = row_of(rates_ref, i) / TOKENS
        tab[0, i] = jnp.exp(-log_decay)
        for step in range(3):
            hop = 1 << step
            factor = jnp.exp(-log_decay * (RUN * hop))
            tab[1 + step, i] = jnp.where(s >= hop, factor, 0.0)
        tab[4, i] = jnp.exp(-log_decay * (RUN * s).astype(f32))

    for_filters(make)

    def sent(strip):
        ahead_at = pl.ds(pl.multiple_of(strip * BLOCKS, BLOCKS), BLOCKS)
        behind_at = pl.ds(pl.multiple_of(BACK + strip * BLOCKS, BLOCKS), BLOCKS)
        pairs = (
            (send_ref.at[:, ahead_at], send_hbm.at[:, ahead_at]),
            (send_ref.at[:, behind_at], send_hbm.at[:, behind_at]),
            (cf_ref.at[strip], cf_hbm.at[strip]),
            (cb_ref.at[strip], cb_hbm.at[strip]),
        )
        return [pltpu.make_async_copy(a, b, sems.at[strip, i]) for i, (a, b) in enumerate(pairs)]

    for n in range(MODES):
        send_ref[n, TERMS:, :] = jnp.zeros((SUB, LANES), f32)

    def strip_body(strip, _):
        base = strip * MODES

        for lag in range(HALF):
            lags[lag] = jnp.zeros((SUB, LANES), f32)
        for n in range(MODES):
            joins[n] = jnp.zeros((SUB, LANES), f32)

        def pair_body(pair, _):
            for odd in range(2):
                at = (strip, 2 * pair + odd)
                decay = [tab[0, base + n] for n in range(MODES)]
                behind, middle = [None] * MODES, [None] * MODES
                for j in reversed(range(RUN)):
                    gated = run_rows(gs, at, j)
                    for n in range(MODES):
                        behind[n] = gated if j == RUN - 1 else decay[n] * behind[n] + gated
                    if j == HALF:
                        middle = list(behind)
                ahead, joint = [None] * MODES, [None] * MODES
                for j in range(RUN):
                    product = run_rows(ps, at, j)
                    for n in range(MODES):
                        ahead[n] = product if j == 0 else decay[n] * ahead[n] + product
                        if j == HALF - 1:
                            joint[n] = ahead[n] * middle[n]
                for lag in range(HALF):
                    starts = [j for j in range(RUN) if j // HALF == (j + lag) // HALF]
                    pairs = [run_rows(gs, at, j + lag) * run_rows(ps, at, j) for j in starts]
                    while len(pairs) > 1:
                        odd_one = pairs[-1:] if len(pairs) % 2 else []
                        pairs = [a + b for a, b in zip(pairs[::2], pairs[1::2])] + odd_one
                    lags[lag] = lags[lag] + pairs[0]
                for step in range(3):
                    for n in range(MODES):
                        moved = pltpu.roll(ahead[n], 1 << step, 0)
                        ahead[n] = ahead[n] + tab[1 + step, base + n] * moved
                for n in range(MODES):
                    row = strip * BLOCKS + 2 * pair + odd
                    send_ref[n, pl.ds(row, 1), :] = ahead[n][SUB - 1 :, :]
                    first = jnp.sum(tab[4, base + n] * behind[n], axis=0, keepdims=True)
                    send_ref[n, pl.ds(BACK + row, 1), :] = first
                    enter = jnp.where(s >= 1, pltpu.roll(ahead[n], 1, 0), 0.0)
                    cf_ref[strip, 2 * pair + odd, n] = enter
                    cb_ref[strip, 2 * pair + odd, n] = behind[n]
                    joins[n] = joins[n] + (joint[n] + behind[n] * enter)
            return 0

        lax.fori_loop(0, PAIRS, pair_body, 0)
        for n in range(MODES):
            decay = tab[0, base + n]
            term = lags[HALF - 1]
            for lag in reversed(range(HALF - 1)):
                term = decay * term + lags[lag]
            term = jnp.sum(term + decay * joins[n], axis=0, keepdims=True)
            send_ref[n, pl.ds(TERMS + strip, 1), :] = term
        for copy in sent(strip):
            copy.start()
        return 0

    lax.fori_loop(0, STRIPS, strip_body, 0)
    tail = pl.ds(TERMS, SUB)
    last = pltpu.make_async_copy(send_ref.at[:, tail], send_hbm.at[:, tail], early_sems.at[4])
    last.start()
    for strip in range(STRIPS):
        for copy in sent(strip):
            copy.wait()
    for copy in [last] + stored:
        copy.wait()


def inner_kernel(
    reverse, rates_hbm, residues_hbm, xs_hbm, enter_hbm, out_hbm,
    tab, rates_ref, residues_ref, xs, enter_ref, out_ref, param_sems, sems,
):
    params = [
        pltpu.make_async_copy(rates_hbm, rates_ref, param_sems.at[0]),
        pltpu.make_async_copy(residues_hbm, residues_ref, param_sems.at[1]),
    ]

    def arrivals(strip):
        return [
            pltpu.make_async_copy(enter_hbm.at[strip], enter_ref.at[strip], sems.at[strip, 0]),
            pltpu.make_async_copy(xs_hbm.at[strip], xs.at[strip], sems.at[strip, 1]),
        ]

    def leaving(strip):
        return pltpu.make_async_copy(out_ref.at[strip], out_hbm.at[strip], sems.at[strip, 2])

    s = sublane()
    for copy in params:
        copy.start()
    for strip in range(STRIPS):
        for copy in arrivals(strip):
            copy.start()
    for copy in params:
        copy.wait()

    def make(i):
        rate = row_of(rates_ref, i)
        tab[0, i] = jnp.exp(-rate / TOKENS)
        tab[1, i] = row_of(residues_ref, i) * jnp.sqrt((1.0 + rate) / TOKENS)
        for step in range(3 if reverse else 0):
            factor = jnp.exp(-rate / TOKENS * (RUN << step))
            tab[2 + step, i] = jnp.where(s < SUB - (1 << step), factor, 0.0)

    for_filters(make)

    def strip_body(strip, _):
        for copy in arrivals(strip):
            copy.wait()
        base = strip * MODES

        def body(blk, _):
            at = (strip, blk)
            decay = [tab[0, base + n] for n in range(MODES)]
            weight = [tab[1, base + n] for n in range(MODES)]
            state = [enter_ref[strip, blk, n] for n in range(MODES)]
            if reverse:
                for step in range(3):
                    for n in range(MODES):
                        moved = pltpu.roll(state[n], SUB - (1 << step), 0)
                        state[n] = state[n] + tab[2 + step, base + n] * moved
                state = [jnp.where(s < SUB - 1, pltpu.roll(a, SUB - 1, 0), 0.0) for a in state]
            for j in reversed(range(RUN)) if reverse else range(RUN):
                x = run_rows(xs, at, j)
                state = [decay[n] * state[n] + x for n in range(MODES)]
                mixed = total([weight[n] * state[n] for n in range(MODES)])
                out_ref[strip, blk, pl.ds(j, SUB, stride=RUN), :] = mixed
            return 0

        lax.fori_loop(0, BLOCKS, body, 0)
        leaving(strip).start()
        return 0

    lax.fori_loop(0, STRIPS, strip_body, 0)
    for strip in range(STRIPS):
        leaving(strip).wait()


def tile_rows(first):
    return pl.ds(first, SUB)


def line_kernel(where_ref, rates_ref, x_ref, y_hbm, y_ref, sems):
    n = where_ref[0]
    y_ref[TERMS:, :] = jnp.zeros((SUB, LANES), f32)
    for strip in range(STRIPS):
        log_decay = row_of(rates_ref, strip * MODES + n) / TOKENS
        across = jnp.exp(-log_decay * ROWS)
        forth, back = tile_rows(strip * BLOCKS), tile_rows(BACK + strip * BLOCKS)
        state, cross, terms = x_ref[0, forth, :], None, None
        for z in range(1, LINE):
            product = state * x_ref[z, back, :]
            cross = product if cross is None else cross + product
            state = across * state + x_ref[z, forth, :]
        y_ref[forth, :] = state
        state = x_ref[LINE - 1, back, :]
        for z in reversed(range(LINE - 1)):
            state = across * state + x_ref[z, back, :]
        y_ref[back, :] = state
        row = pl.ds(TERMS + strip, 1)
        terms = total([x_ref[z, row, :] for z in range(LINE)])
        cross = jnp.sum(jnp.exp(-log_decay) * cross, axis=0, keepdims=True)
        y_ref[row, :] = terms + cross
    copies = [pltpu.make_async_copy(y_ref, y_hbm.at[g], sems.at[g]) for g in range(LINES)]
    for copy in copies:
        copy.start()
    for copy in copies:
        copy.wait()


def join_kernel(where_ref, rates_ref, x_ref, y_ref, out_hbm, out_ref, sem):
    n = where_ref[0]
    line = jnp.broadcast_to(where_ref[1], (SUB, LANES))
    for z in range(LINE):
        out_ref[z, TERMS:, :] = jnp.zeros((SUB, LANES), f32)
    for strip in range(STRIPS):
        log_decay = row_of(rates_ref, strip * MODES + n) / TOKENS
        across = jnp.exp(-log_decay * ROWS)
        leap = jnp.exp(-log_decay * (ROWS * LINE))
        forth, back = tile_rows(strip * BLOCKS), tile_rows(BACK + strip * BLOCKS)
        zero = jnp.zeros((SUB, LANES), f32)
        state, enter, cross = zero, zero, zero
        for g in range(LINES):
            enter = jnp.where(line == g, state, enter)
            cross = cross + state * y_ref[g, back, :]
            state = leap * state + y_ref[g, forth, :]
        for z in range(LINE):
            out_ref[z, forth, :] = enter
            enter = across * enter + x_ref[z, forth, :]
        state, enter = zero, zero
        for g in reversed(range(LINES)):
            enter = jnp.where(line == g, state, enter)
            state = leap * state + y_ref[g, back, :]
        for z in reversed(range(LINE)):
            out_ref[z, back, :] = enter
            enter = across * enter + x_ref[z, back, :]
        row = pl.ds(TERMS + strip, 1)
        terms = total([y_ref[g, row, :] for g in range(LINES)])
        cross = jnp.sum(jnp.exp(-log_decay) * cross, axis=0, keepdims=True)
        for z in range(LINE):
            out_ref[z, row, :] = terms + cross
    copy = pltpu.make_async_copy(out_ref, out_hbm, sem)
    copy.start()
    copy.wait()


def finish_kernel(
    rates_ref, residues_ref, k_hbm, v_hbm, u_hbm, conv_hbm, flow_hbm, in_ref,
    gq_hbm, gk_hbm, gv_hbm,
    tab, k_ref, v_ref, u_ref, conv_ref, flow_ref, gq_ref, gk_ref, gv_ref, arrive_sems, sems,
):
    s = sublane()

    def arrivals(blk):
        cols = pl.ds(blk * FILTERS, FILTERS)
        if not isinstance(blk, int):
            cols = pl.ds(pl.multiple_of(blk * FILTERS, FILTERS), FILTERS)
        pairs = [
            (a.at[:, blk], b.at[:, blk]) for a, b in ((conv_hbm, conv_ref), (flow_hbm, flow_ref))
        ]
        for a, b in ((u_hbm, u_ref), (v_hbm, v_ref), (k_hbm, k_ref)):
            pairs.append((a.at[:, cols], b.at[:, cols]))
        return [
            pltpu.make_async_copy(a, b, arrive_sems.at[blk, i]) for i, (a, b) in enumerate(pairs)
        ]

    for blk in range(BLOCKS):
        for copy in arrivals(blk):
            copy.start()

    def make(i):
        rate = row_of(rates_ref, i)
        log_decay = rate / TOKENS
        weight = row_of(residues_ref, i) * jnp.sqrt((1.0 + rate) / TOKENS)
        tab[0, i] = jnp.exp(-log_decay * SUB)
        tab[1, i] = weight * jnp.exp(-log_decay * (s + 1).astype(f32))
        tab[2, i] = weight * jnp.exp(-log_decay * (SUB - s).astype(f32))

    for_filters(make)

    def copies(blk):
        cols = pl.ds(pl.multiple_of(blk * FILTERS, FILTERS), FILTERS)
        return [
            pltpu.make_async_copy(src.at[:, cols], dst.at[:, cols], sems.at[blk, i])
            for i, (src, dst) in enumerate(((gq_ref, gq_hbm), (gk_ref, gk_hbm), (gv_ref, gv_hbm)))
        ]

    def pair_body(pair, _):
        for odd in range(2):
            blk = 2 * pair + odd
            for copy in arrivals(blk):
                copy.wait()

            def strip_body(strip, _):
                base = strip * MODES
                cols = lanes_of(blk * STRIPS + strip)
                leap = [tab[0, base + n] for n in range(MODES)]
                row = strip * BLOCKS + blk
                state = [
                    tab[1, base + n] * in_ref[n, pl.ds(row, 1), :] for n in range(MODES)
                ]
                for i in range(ROWS // 16):
                    parts = []
                    for _ in range(2):
                        parts.append(total(state))
                        state = [leap[n] * state[n] for n in range(MODES)]
                    at = pl.ds(16 * i, 16)
                    conv = conv_ref[strip, blk, at, :] + jnp.concatenate(parts, axis=0)
                    gq_ref[at, cols] = (u_ref[at, cols].astype(f32) * conv).astype(bf16)
                state = [
                    tab[2, base + n] * in_ref[n, pl.ds(BACK + row, 1), :] for n in range(MODES)
                ]
                for i in reversed(range(ROWS // 16)):
                    parts = []
                    for _ in range(2):
                        parts.insert(0, total(state))
                        state = [leap[n] * state[n] for n in range(MODES)]
                    at = pl.ds(16 * i, 16)
                    flow = flow_ref[strip, blk, at, :] + jnp.concatenate(parts, axis=0)
                    gk_ref[at, cols] = (flow * v_ref[at, cols].astype(f32)).astype(bf16)
                    gv_ref[at, cols] = (flow * k_ref[at, cols].astype(f32)).astype(bf16)
                return 0

            lax.fori_loop(0, STRIPS, strip_body, 0)
            for copy in copies(blk):
                copy.start()
        return 0

    lax.fori_loop(0, PAIRS, pair_body, 0)
    for blk in range(BLOCKS):
        for copy in copies(blk):
            copy.wait()


def in_hbm(*arrays):
    return [pltpu.with_memory_space_constraint(a, pltpu.HBM) for a in arrays]


def local(query_rows, key_rows, value_rows, upstream, decay_rate, residue):
    half = lax.axis_index("fsdp")
    swap = [(0, 1), (1, 0)]
    first = lax.broadcasted_iota(jnp.int32, (2 * MODES, FILTERS // 2), 0) < MODES
    below, above = ((0, MODES, 0), (0, 0, 0)), ((MODES, 0, 0), (0, 0, 0))
    zero = jnp.zeros((), f32)
    mine = jnp.where(first, lax.pad(decay_rate, zero, below), lax.pad(residue, zero, above))
    other = lax.ppermute(mine, "fsdp", swap)
    vmem = pl.BlockSpec(memory_space=pltpu.VMEM)
    smem = pl.BlockSpec(memory_space=pltpu.SMEM)
    hbm = pl.BlockSpec(memory_space=pltpu.HBM)
    limit = pltpu.CompilerParams(vmem_limit_bytes=16 << 20)
    packet = (LINE, DEPTH, LANES)
    packets = pltpu.HBM(packet, f32)
    tiles = (STRIPS, BLOCKS, ROWS, LANES)
    state = (STRIPS, BLOCKS, MODES, SUB, LANES)
    params = (STRIPS * MODES, LANES)
    table = (STRIPS * MODES, SUB, LANES)
    whole = pltpu.VMEM((ROWS, WIDTH), bf16)
    query_rows, key_rows, value_rows, upstream = in_hbm(
        query_rows, key_rows, value_rows, upstream
    )
    ps, gs = pl.pallas_call(
        prepare_kernel,
        in_specs=[hbm] * 4,
        out_specs=[vmem] * 2,
        out_shape=[jax.ShapeDtypeStruct(tiles, f32)] * 2,
        scratch_shapes=[whole] * 4 + [pltpu.SemaphoreType.DMA((BLOCKS, 4))],
        compiler_params=limit,
        cost_estimate=pl.CostEstimate(flops=1 << 22, bytes_accessed=12 << 20, transcendentals=0),
        name="prepare",
    )(query_rows, key_rows, value_rows, upstream)
    send, enter_ahead, enter_behind, rates, residues, product, gated = pl.pallas_call(
        summarize_kernel,
        in_specs=[smem] + [vmem] * 4,
        out_specs=[hbm] * 7,
        out_shape=[packets]
        + [pltpu.HBM(state, f32)] * 2
        + [pltpu.HBM(params, f32)] * 2
        + [pltpu.HBM(tiles, f32)] * 2,
        scratch_shapes=[
            pltpu.VMEM((5,) + table, f32),
            pltpu.VMEM((HALF, SUB, LANES), f32),
            pltpu.VMEM((MODES, SUB, LANES), f32),
            pltpu.VMEM(packet, f32),
            pltpu.VMEM(state, f32),
            pltpu.VMEM(state, f32),
            pltpu.VMEM(params, f32),
            pltpu.VMEM(params, f32),
            pltpu.SemaphoreType.DMA((STRIPS, 4)),
            pltpu.SemaphoreType.DMA((5,)),
        ],
        compiler_params=limit,
        name="summarize",
    )(half.astype(jnp.int32).reshape(1), mine, other, ps, gs)
    arrived = lax.all_to_all(send, ALONG, 0, 0, tiled=True)

    def inner(xs, enter, reverse):
        return pl.pallas_call(
            functools.partial(inner_kernel, reverse),
            in_specs=[hbm] * 4,
            out_specs=hbm,
            out_shape=pltpu.HBM(tiles, f32),
            scratch_shapes=[
                pltpu.VMEM((5 if reverse else 2,) + table, f32),
                pltpu.VMEM(params, f32),
                pltpu.VMEM(params, f32),
                pltpu.VMEM(tiles, f32),
                pltpu.VMEM(state, f32),
                pltpu.VMEM(tiles, f32),
                pltpu.SemaphoreType.DMA((2,)),
                pltpu.SemaphoreType.DMA((STRIPS, 3)),
            ],
            cost_estimate=pl.CostEstimate(
                flops=1 << 24, bytes_accessed=16 << 20, transcendentals=0
            ),
            name="behind" if reverse else "ahead",
        )(rates, residues, xs, enter)

    conv = inner(product, enter_ahead, False)
    arrived, conv = lax.optimization_barrier((arrived, conv))
    where = jnp.stack([lax.axis_index(ALONG), lax.axis_index("yx")]).astype(jnp.int32)
    lines = pl.pallas_call(
        line_kernel,
        in_specs=[smem] + [vmem] * 2,
        out_specs=hbm,
        out_shape=pltpu.HBM((LINES, DEPTH, LANES), f32),
        scratch_shapes=[pltpu.VMEM((DEPTH, LANES), f32), pltpu.SemaphoreType.DMA((LINES,))],
        compiler_params=limit,
        name="line",
    )(where, rates, arrived)
    totals = lax.all_to_all(lines, "yx", 0, 0, tiled=True)
    flowing = inner(gated, enter_behind, True)
    totals, flowing = lax.optimization_barrier((totals, flowing))
    carries = pl.pallas_call(
        join_kernel,
        in_specs=[smem] + [vmem] * 3,
        out_specs=hbm,
        out_shape=packets,
        scratch_shapes=[pltpu.VMEM(packet, f32), pltpu.SemaphoreType.DMA],
        compiler_params=limit,
        name="join",
    )(where, rates, arrived, totals)
    back = lax.all_to_all(carries, ALONG, 0, 0, tiled=True)
    count = STRIPS // 2
    rows = lax.dynamic_slice_in_dim(back, TERMS + half * count, count, 1)
    rows = rows.reshape(MODES, count * LANES)
    rows = rows + lax.ppermute(rows, "ch", swap)
    gain = jnp.sqrt((1.0 + decay_rate) / TOKENS)
    residue_grad = gain * rows / math.sqrt(TOKENS)
    conv, flowing = in_hbm(conv, flowing)
    grads_out = pl.pallas_call(
        finish_kernel,
        in_specs=[vmem] * 2 + [hbm] * 5 + [vmem],
        out_specs=[hbm] * 3,
        out_shape=[pltpu.HBM((ROWS, WIDTH), bf16)] * 3,
        scratch_shapes=[
            pltpu.VMEM((3,) + table, f32),
            whole,
            whole,
            whole,
            pltpu.VMEM(tiles, f32),
            pltpu.VMEM(tiles, f32),
            whole,
            whole,
            whole,
            pltpu.SemaphoreType.DMA((BLOCKS, 5)),
            pltpu.SemaphoreType.DMA((BLOCKS, 3)),
        ],
        compiler_params=limit,
        name="finish",
    )(rates, residues, key_rows, value_rows, upstream, conv, flowing, back)
    return (*grads_out, residue_grad)


def solution(mesh):
    rows = P(ALL, "ch")
    params = P(None, "fsdp")
    return jax.shard_map(
        local,
        mesh=Mesh(mesh.devices.reshape(LINES, LINE // 2, 2, 2), ("yx", "zh", "ch", "fsdp")),
        in_specs=(rows, rows, rows, rows, params, params),
        out_specs=(rows, rows, rows, params),
        check_vma=False,
    )
```

```python
import functools
import math

import jax
import jax.numpy as jnp
from jax import lax
from jax.experimental import pallas as pl
from jax.experimental.pallas import tpu as pltpu
from jax.sharding import PartitionSpec as P

TOKENS = 16384
ROWS = 128
MODES = 8
FILTERS = 512
BLOCKS = 8
SUB = 8
RUN = ROWS // SUB
HALF = RUN // 2
LANES = 128
STRIPS = FILTERS // LANES
PAIRS = BLOCKS // 2
WIDTH = BLOCKS * FILTERS
SHARDS = TOKENS // ROWS
PACKET = 5 * LANES
ALL = ("ctx", "fsdp")
f32 = jnp.float32
bf16 = jnp.bfloat16


def sublane():
    return lax.broadcasted_iota(jnp.int32, (SUB, LANES), 0)


def owner(strip, pair, n):
    return (strip * PAIRS + pair) * MODES + n


def lanes_of(at):
    return pl.ds(pl.multiple_of(at * LANES, LANES), LANES)


def piece(r):
    return pl.ds(r * LANES, LANES)


def spread(ref, at, natural):
    half = RUN // SUB
    for r in range(ROWS // SUB):
        start = (r % half) * SUB * SUB + r // half
        ref[(*at, pl.ds(start, SUB, stride=SUB))] = natural[SUB * r : SUB * (r + 1), :]


def run_rows(ref, at, j):
    return ref[(*at, pl.ds(SUB * j, SUB))]


def for_filters(make):
    def body(i, _):
        make(i)
        return 0

    lax.fori_loop(0, STRIPS * MODES, body, 0)


def row_of(ref, i):
    return jnp.broadcast_to(ref[pl.ds(i, 1), :], (SUB, LANES))


def total(parts):
    while len(parts) > 1:
        parts = [a + b for a, b in zip(parts[::2], parts[1::2])]
    return parts[0]


def prepare_kernel(q_hbm, k_hbm, v_hbm, u_hbm, ps, gs, q_ref, k_ref, v_ref, u_ref, sems):
    def copies(blk):
        cols = pl.ds(blk * FILTERS, FILTERS)
        return [
            pltpu.make_async_copy(src.at[:, cols], dst.at[:, cols], sems.at[blk, i])
            for i, (src, dst) in enumerate(
                ((k_hbm, k_ref), (v_hbm, v_ref), (u_hbm, u_ref), (q_hbm, q_ref))
            )
        ]

    for blk in range(BLOCKS):
        for copy in copies(blk):
            copy.start()
    for blk in range(BLOCKS):
        for copy in copies(blk):
            copy.wait()

        def strip_body(strip, _):
            at = (strip, blk)
            cols = lanes_of(blk * STRIPS + strip)
            spread(ps, at, k_ref[:, cols].astype(f32) * v_ref[:, cols].astype(f32))
            spread(gs, at, u_ref[:, cols].astype(f32) * q_ref[:, cols].astype(f32))
            return 0

        lax.fori_loop(0, STRIPS, strip_body, 0)


def summarize_kernel(
    half_ref, mine_ref, other_ref, ps, gs,
    send_hbm, cf_hbm, cb_hbm, rates_hbm, residues_hbm, ps_hbm, gs_hbm,
    tab, lags, joins, send_ref, cf_ref, cb_ref, rates_ref, residues_ref, sems, early_sems,
):
    s = sublane()
    lower = jnp.broadcast_to(half_ref[0], (MODES, LANES)) == 0
    for strip in range(STRIPS):
        cols = pl.ds((strip % 2) * LANES, LANES)
        at = pl.ds(strip * MODES, MODES)
        for part, out in enumerate((rates_ref, residues_ref)):
            rows = pl.ds(part * MODES, MODES)
            here, there = mine_ref[rows, cols], other_ref[rows, cols]
            if strip < STRIPS // 2:
                out[at, :] = jnp.where(lower, here, there)
            else:
                out[at, :] = jnp.where(lower, there, here)

    stored = [
        pltpu.make_async_copy(a, b, early_sems.at[i])
        for i, (a, b) in enumerate(
            ((rates_ref, rates_hbm), (residues_ref, residues_hbm), (ps, ps_hbm), (gs, gs_hbm))
        )
    ]
    for copy in stored:
        copy.start()

    def make(i):
        log_decay = row_of(rates_ref, i) / TOKENS
        tab[0, i] = jnp.exp(-log_decay)
        for step in range(3):
            hop = 1 << step
            factor = jnp.exp(-log_decay * (RUN * hop))
            tab[1 + step, i] = jnp.where(s >= hop, factor, 0.0)
        tab[4, i] = jnp.exp(-log_decay * (RUN * s).astype(f32))

    for_filters(make)

    def sent(strip):
        at = pl.ds(strip * PAIRS * MODES, PAIRS * MODES)
        return [
            pltpu.make_async_copy(send_ref.at[at], send_hbm.at[at], sems.at[strip, 0]),
            pltpu.make_async_copy(cf_ref.at[strip], cf_hbm.at[strip], sems.at[strip, 1]),
            pltpu.make_async_copy(cb_ref.at[strip], cb_hbm.at[strip], sems.at[strip, 2]),
        ]

    def strip_body(strip, _):
        base = strip * MODES

        for lag in range(HALF):
            lags[lag] = jnp.zeros((SUB, LANES), f32)
        for n in range(MODES):
            joins[n] = jnp.zeros((SUB, LANES), f32)

        def pair_body(pair, _):
            for odd in range(2):
                at = (strip, 2 * pair + odd)
                decay = [tab[0, base + n] for n in range(MODES)]
                behind, middle = [None] * MODES, [None] * MODES
                for j in reversed(range(RUN)):
                    gated = run_rows(gs, at, j)
                    for n in range(MODES):
                        behind[n] = gated if j == RUN - 1 else decay[n] * behind[n] + gated
                    if j == HALF:
                        middle = list(behind)
                ahead, joint = [None] * MODES, [None] * MODES
                for j in range(RUN):
                    product = run_rows(ps, at, j)
                    for n in range(MODES):
                        ahead[n] = product if j == 0 else decay[n] * ahead[n] + product
                        if j == HALF - 1:
                            joint[n] = ahead[n] * middle[n]
                for lag in range(HALF):
                    starts = [j for j in range(RUN) if j // HALF == (j + lag) // HALF]
                    pairs = [run_rows(gs, at, j + lag) * run_rows(ps, at, j) for j in starts]
                    while len(pairs) > 1:
                        odd_one = pairs[-1:] if len(pairs) % 2 else []
                        pairs = [a + b for a, b in zip(pairs[::2], pairs[1::2])] + odd_one
                    lags[lag] = lags[lag] + pairs[0]
                for step in range(3):
                    for n in range(MODES):
                        moved = pltpu.roll(ahead[n], 1 << step, 0)
                        ahead[n] = ahead[n] + tab[1 + step, base + n] * moved
                for n in range(MODES):
                    place = owner(strip, pair, n)
                    send_ref[place, :, piece(odd)] = ahead[n][SUB - 1 :, :]
                    first = jnp.sum(tab[4, base + n] * behind[n], axis=0, keepdims=True)
                    send_ref[place, :, piece(2 + odd)] = first
                    enter = jnp.where(s >= 1, pltpu.roll(ahead[n], 1, 0), 0.0)
                    cf_ref[strip, 2 * pair + odd, n] = enter
                    cb_ref[strip, 2 * pair + odd, n] = behind[n]
                    joins[n] = joins[n] + (joint[n] + behind[n] * enter)
            return 0

        lax.fori_loop(0, PAIRS, pair_body, 0)
        for n in range(MODES):
            decay = tab[0, base + n]
            term = lags[HALF - 1]
            for lag in reversed(range(HALF - 1)):
                term = decay * term + lags[lag]
            term = jnp.sum(term + decay * joins[n], axis=0, keepdims=True)
            for pair in range(PAIRS):
                row = term if pair == 0 else jnp.zeros((1, LANES), f32)
                send_ref[owner(strip, pair, n), :, piece(4)] = row
        for copy in sent(strip):
            copy.start()
        return 0

    lax.fori_loop(0, STRIPS, strip_body, 0)
    for strip in range(STRIPS):
        for copy in sent(strip):
            copy.wait()
    for copy in stored:
        copy.wait()


def inner_kernel(reverse, rates_hbm, residues_hbm, xs_hbm, enter_hbm, *refs):
    if reverse:
        out_hbm, lead_ref = refs[:2]
    else:
        k_hbm, v_hbm, u_hbm, out_hbm, lead_ref, lead_k, lead_v, lead_u, late_tab = refs[:9]
    tab, rates_ref, residues_ref, xs, enter_ref, out_ref, param_sems, sems = refs[-8:]
    params = [
        pltpu.make_async_copy(rates_hbm, rates_ref, param_sems.at[0]),
        pltpu.make_async_copy(residues_hbm, residues_ref, param_sems.at[1]),
    ]

    def arrivals(strip):
        return [
            pltpu.make_async_copy(enter_hbm.at[strip], enter_ref.at[strip], sems.at[strip, 0]),
            pltpu.make_async_copy(xs_hbm.at[strip], xs.at[strip], sems.at[strip, 1]),
        ]

    def leaving(strip):
        return pltpu.make_async_copy(out_ref.at[strip], out_hbm.at[strip], sems.at[strip, 2])

    s = sublane()
    leads = []
    if not reverse:
        pairs = ((k_hbm, lead_k), (v_hbm, lead_v), (u_hbm, lead_u))
        for i, (a, b) in enumerate(pairs):
            source = a.at[:, pl.ds(0, FILTERS)]
            leads.append(pltpu.make_async_copy(source, b, param_sems.at[2 + i]))
    for copy in params:
        copy.start()
    for strip in range(STRIPS):
        for copy in arrivals(strip):
            copy.start()
    for copy in leads:
        copy.start()
    for copy in params:
        copy.wait()

    def make(i):
        rate = row_of(rates_ref, i)
        tab[0, i] = jnp.exp(-rate / TOKENS)
        tab[1, i] = row_of(residues_ref, i) * jnp.sqrt((1.0 + rate) / TOKENS)
        if not reverse:
            weight = tab[1, i]
            late_tab[0, i] = jnp.exp(-rate / TOKENS * SUB)
            late_tab[1, i] = weight * jnp.exp(-rate / TOKENS * (s + 1).astype(f32))
            late_tab[2, i] = weight * jnp.exp(-rate / TOKENS * (SUB - s).astype(f32))
        for step in range(3 if reverse else 0):
            factor = jnp.exp(-rate / TOKENS * (RUN << step))
            tab[2 + step, i] = jnp.where(s < SUB - (1 << step), factor, 0.0)

    for_filters(make)

    def strip_body(strip, _):
        for copy in arrivals(strip):
            copy.wait()
        base = strip * MODES

        def body(blk, _):
            at = (strip, blk)
            decay = [tab[0, base + n] for n in range(MODES)]
            weight = [tab[1, base + n] for n in range(MODES)]
            state = [enter_ref[strip, blk, n] for n in range(MODES)]
            if reverse:
                for step in range(3):
                    for n in range(MODES):
                        moved = pltpu.roll(state[n], SUB - (1 << step), 0)
                        state[n] = state[n] + tab[2 + step, base + n] * moved
                state = [jnp.where(s < SUB - 1, pltpu.roll(a, SUB - 1, 0), 0.0) for a in state]
            for j in reversed(range(RUN)) if reverse else range(RUN):
                x = run_rows(xs, at, j)
                state = [decay[n] * state[n] + x for n in range(MODES)]
                mixed = total([weight[n] * state[n] for n in range(MODES)])
                out_ref[strip, blk, pl.ds(j, SUB, stride=RUN), :] = mixed
            return 0

        lax.fori_loop(0, BLOCKS, body, 0)
        leaving(strip).start()
        lead_ref[strip] = out_ref[strip, 0]
        return 0

    lax.fori_loop(0, STRIPS, strip_body, 0)
    for strip in range(STRIPS):
        leaving(strip).wait()
    for copy in leads:
        copy.wait()


def carry_kernel(where_ref, rates_ref, x_ref, y_hbm, y_ref, sem):
    place = where_ref[0]
    at = (place // (PAIRS * MODES)) * MODES + place % MODES
    log_decay = rates_ref[pl.ds(at, 1), :] / TOKENS
    across = jnp.exp(-log_decay * ROWS)
    zero = jnp.zeros((1, LANES), f32)

    def step(i, carried):
        a0, a1, b0, b1, cross, terms = carried
        y_ref[i, :, piece(0)] = a0
        y_ref[i, :, piece(1)] = a1
        cross = cross + (a0 * x_ref[i, :, piece(2)] + a1 * x_ref[i, :, piece(3)])
        terms = terms + x_ref[i, :, piece(4)]
        back = SHARDS - 1 - i
        y_ref[back, :, piece(2)] = b0
        y_ref[back, :, piece(3)] = b1
        return (
            across * a0 + x_ref[i, :, piece(0)],
            across * a1 + x_ref[i, :, piece(1)],
            across * b0 + x_ref[back, :, piece(2)],
            across * b1 + x_ref[back, :, piece(3)],
            cross,
            terms,
        )

    carried = lax.fori_loop(0, SHARDS, step, (zero,) * 6, unroll=8)
    row = jnp.exp(-log_decay) * carried[4] + carried[5]

    def fill(i, _):
        y_ref[i, :, piece(4)] = row
        return 0

    lax.fori_loop(0, SHARDS, fill, 0, unroll=16)
    copy = pltpu.make_async_copy(y_ref, y_hbm, sem)
    copy.start()
    copy.wait()


def finish_kernel(
    tab, k_hbm, v_hbm, u_hbm, conv_hbm, flow_hbm, in_ref,
    lead_k, lead_v, lead_u, lead_conv, lead_flow,
    gq_hbm, gk_hbm, gv_hbm,
    k_ref, v_ref, u_ref, conv_ref, flow_ref, gq_ref, gk_ref, gv_ref, arrive_sems, sems,
):
    def arrivals(blk):
        cols = pl.ds(blk * FILTERS, FILTERS)
        if not isinstance(blk, int):
            cols = pl.ds(pl.multiple_of(blk * FILTERS, FILTERS), FILTERS)
        pairs = [
            (a.at[:, blk], b.at[:, blk]) for a, b in ((conv_hbm, conv_ref), (flow_hbm, flow_ref))
        ]
        for a, b in ((u_hbm, u_ref), (v_hbm, v_ref), (k_hbm, k_ref)):
            pairs.append((a.at[:, cols], b.at[:, cols]))
        return [
            pltpu.make_async_copy(a, b, arrive_sems.at[blk, i]) for i, (a, b) in enumerate(pairs)
        ]

    for blk in range(1, BLOCKS):
        for copy in arrivals(blk):
            copy.start()
    lead = pl.ds(0, FILTERS)
    for a, b in ((lead_k, k_ref), (lead_v, v_ref), (lead_u, u_ref)):
        b[:, lead] = a[...]
    for strip in range(STRIPS):
        conv_ref[strip, 0] = lead_conv[strip]
        flow_ref[strip, 0] = lead_flow[strip]

    def copies(blk):
        cols = pl.ds(pl.multiple_of(blk * FILTERS, FILTERS), FILTERS)
        return [
            pltpu.make_async_copy(src.at[:, cols], dst.at[:, cols], sems.at[blk, i])
            for i, (src, dst) in enumerate(((gq_ref, gq_hbm), (gk_ref, gk_hbm), (gv_ref, gv_hbm)))
        ]

    def pair_body(pair, _):
        for odd in range(2):
            blk = 2 * pair + odd

            @pl.when(blk > 0)
            def _():
                for copy in arrivals(blk):
                    copy.wait()

            def strip_body(strip, _):
                base = strip * MODES
                cols = lanes_of(blk * STRIPS + strip)
                leap = [tab[0, base + n] for n in range(MODES)]
                places = [owner(strip, pair, n) for n in range(MODES)]
                state = [
                    tab[1, base + n] * in_ref[places[n], :, piece(odd)] for n in range(MODES)
                ]
                for i in range(ROWS // 16):
                    parts = []
                    for _ in range(2):
                        parts.append(total(state))
                        state = [leap[n] * state[n] for n in range(MODES)]
                    at = pl.ds(16 * i, 16)
                    conv = conv_ref[strip, blk, at, :] + jnp.concatenate(parts, axis=0)
                    gq_ref[at, cols] = (u_ref[at, cols].astype(f32) * conv).astype(bf16)
                state = [
                    tab[2, base + n] * in_ref[places[n], :, piece(2 + odd)] for n in range(MODES)
                ]
                for i in reversed(range(ROWS // 16)):
                    parts = []
                    for _ in range(2):
                        parts.insert(0, total(state))
                        state = [leap[n] * state[n] for n in range(MODES)]
                    at = pl.ds(16 * i, 16)
                    flow = flow_ref[strip, blk, at, :] + jnp.concatenate(parts, axis=0)
                    gk_ref[at, cols] = (flow * v_ref[at, cols].astype(f32)).astype(bf16)
                    gv_ref[at, cols] = (flow * k_ref[at, cols].astype(f32)).astype(bf16)
                return 0

            lax.fori_loop(0, STRIPS, strip_body, 0)
            for copy in copies(blk):
                copy.start()
        return 0

    lax.fori_loop(0, PAIRS, pair_body, 0)
    for blk in range(BLOCKS):
        for copy in copies(blk):
            copy.wait()


def in_hbm(*arrays):
    return [pltpu.with_memory_space_constraint(a, pltpu.HBM) for a in arrays]


def local(query_rows, key_rows, value_rows, upstream, decay_rate, residue):
    half = lax.axis_index("fsdp")
    swap = [(0, 1), (1, 0)]
    first = lax.broadcasted_iota(jnp.int32, (2 * MODES, FILTERS // 2), 0) < MODES
    below, above = ((0, MODES, 0), (0, 0, 0)), ((MODES, 0, 0), (0, 0, 0))
    zero = jnp.zeros((), f32)
    mine = jnp.where(first, lax.pad(decay_rate, zero, below), lax.pad(residue, zero, above))
    other = lax.ppermute(mine, "fsdp", swap)
    vmem = pl.BlockSpec(memory_space=pltpu.VMEM)
    smem = pl.BlockSpec(memory_space=pltpu.SMEM)
    hbm = pl.BlockSpec(memory_space=pltpu.HBM)
    limit = pltpu.CompilerParams(vmem_limit_bytes=16 << 20)
    packet = (SHARDS, 1, PACKET)
    packets = pltpu.HBM(packet, f32)
    tiles = (STRIPS, BLOCKS, ROWS, LANES)
    state = (STRIPS, BLOCKS, MODES, SUB, LANES)
    params = (STRIPS * MODES, LANES)
    table = (STRIPS * MODES, SUB, LANES)
    whole = pltpu.VMEM((ROWS, WIDTH), bf16)
    query_rows, key_rows, value_rows, upstream = in_hbm(
        query_rows, key_rows, value_rows, upstream
    )
    ps, gs = pl.pallas_call(
        prepare_kernel,
        in_specs=[hbm] * 4,
        out_specs=[vmem] * 2,
        out_shape=[jax.ShapeDtypeStruct(tiles, f32)] * 2,
        scratch_shapes=[whole] * 4 + [pltpu.SemaphoreType.DMA((BLOCKS, 4))],
        compiler_params=limit,
        cost_estimate=pl.CostEstimate(flops=1 << 22, bytes_accessed=12 << 20, transcendentals=0),
        name="prepare",
    )(query_rows, key_rows, value_rows, upstream)
    send, enter_ahead, enter_behind, rates, residues, product, gated = pl.pallas_call(
        summarize_kernel,
        in_specs=[smem] + [vmem] * 4,
        out_specs=[hbm] * 7,
        out_shape=[packets]
        + [pltpu.HBM(state, f32)] * 2
        + [pltpu.HBM(params, f32)] * 2
        + [pltpu.HBM(tiles, f32)] * 2,
        scratch_shapes=[
            pltpu.VMEM((5,) + table, f32),
            pltpu.VMEM((HALF, SUB, LANES), f32),
            pltpu.VMEM((MODES, SUB, LANES), f32),
            pltpu.VMEM(packet, f32),
            pltpu.VMEM(state, f32),
            pltpu.VMEM(state, f32),
            pltpu.VMEM(params, f32),
            pltpu.VMEM(params, f32),
            pltpu.SemaphoreType.DMA((STRIPS, 3)),
            pltpu.SemaphoreType.DMA((4,)),
        ],
        compiler_params=limit,
        name="summarize",
    )(half.astype(jnp.int32).reshape(1), mine, other, ps, gs)
    arrived = lax.all_to_all(send, ALL, 0, 0, tiled=True)

    lead = jax.ShapeDtypeStruct((STRIPS, ROWS, LANES), f32)
    lead_rows = jax.ShapeDtypeStruct((ROWS, FILTERS), bf16)

    def inner(xs, enter, reverse, extra=(), more=()):
        return pl.pallas_call(
            functools.partial(inner_kernel, reverse),
            in_specs=[hbm] * (4 + len(extra)),
            out_specs=[hbm] + [vmem] * (1 + len(more)),
            out_shape=[pltpu.HBM(tiles, f32), lead, *more],
            scratch_shapes=[
                pltpu.VMEM((5 if reverse else 2,) + table, f32),
                pltpu.VMEM(params, f32),
                pltpu.VMEM(params, f32),
                pltpu.VMEM(tiles, f32),
                pltpu.VMEM(state, f32),
                pltpu.VMEM(tiles, f32),
                pltpu.SemaphoreType.DMA((5,)),
                pltpu.SemaphoreType.DMA((STRIPS, 3)),
            ],
            compiler_params=limit,
            cost_estimate=pl.CostEstimate(
                flops=1 << 24, bytes_accessed=16 << 20, transcendentals=0
            ),
            name="behind" if reverse else "ahead",
        )(*in_hbm(rates, residues, xs, enter), *extra)

    late = jax.ShapeDtypeStruct((3,) + table, f32)
    conv, lead_conv, lead_k, lead_v, lead_u, late_tab = inner(
        product,
        enter_ahead,
        False,
        (key_rows, value_rows, upstream),
        (lead_rows, lead_rows, lead_rows, late),
    )
    arrived, conv = lax.optimization_barrier((arrived, conv))
    place = lax.axis_index(ALL).astype(jnp.int32).reshape(1)
    carries = pl.pallas_call(
        carry_kernel,
        in_specs=[smem] + [vmem] * 2,
        out_specs=hbm,
        out_shape=packets,
        scratch_shapes=[pltpu.VMEM(packet, f32), pltpu.SemaphoreType.DMA],
        compiler_params=limit,
        name="carry",
    )(place, rates, arrived)
    back = lax.all_to_all(carries, ALL, 0, 0, tiled=True)
    flowing, lead_flow = inner(gated, enter_behind, True)
    back, flowing = lax.optimization_barrier((back, flowing))
    rows = back[:, 0, 4 * LANES :].reshape(STRIPS, PAIRS, MODES, LANES)
    count = STRIPS // 2
    rows = lax.dynamic_slice_in_dim(rows, half * count, count, 0).sum(axis=1)
    rows = rows + lax.ppermute(rows, "ch", swap)
    rows = rows.transpose(1, 0, 2).reshape(MODES, count * LANES)
    gain = jnp.sqrt((1.0 + decay_rate) / TOKENS)
    residue_grad = gain * rows / math.sqrt(TOKENS)
    conv, flowing = in_hbm(conv, flowing)
    grads_out = pl.pallas_call(
        finish_kernel,
        in_specs=[vmem] + [hbm] * 5 + [vmem] * 6,
        out_specs=[hbm] * 3,
        out_shape=[pltpu.HBM((ROWS, WIDTH), bf16)] * 3,
        scratch_shapes=[
            whole,
            whole,
            whole,
            pltpu.VMEM(tiles, f32),
            pltpu.VMEM(tiles, f32),
            whole,
            whole,
            whole,
            pltpu.SemaphoreType.DMA((BLOCKS, 5)),
            pltpu.SemaphoreType.DMA((BLOCKS, 3)),
        ],
        compiler_params=limit,
        name="finish",
    )(
        late_tab, key_rows, value_rows, upstream, conv, flowing, back,
        lead_k, lead_v, lead_u, lead_conv, lead_flow,
    )
    return (*grads_out, residue_grad)


def solution(mesh):
    rows = P(ALL, "ch")
    params = P(None, "fsdp")
    return jax.shard_map(
        local,
        mesh=mesh,
        in_specs=(rows, rows, rows, rows, params, params),
        out_specs=(rows, rows, rows, params),
        check_vma=False,
    )
```

```python
import functools
import math

import jax
import jax.numpy as jnp
from jax import lax
from jax.experimental import pallas as pl
from jax.experimental.pallas import tpu as pltpu
from jax.sharding import PartitionSpec as P

TOKENS = 16384
ROWS = 128
MODES = 8
FILTERS = 512
BLOCKS = 8
SUB = 8
RUN = ROWS // SUB
HALF = RUN // 2
LANES = 128
STRIPS = FILTERS // LANES
PAIRS = BLOCKS // 2
WIDTH = BLOCKS * FILTERS
SHARDS = TOKENS // ROWS
PACKET = 5 * LANES
ALL = ("ctx", "fsdp")
f32 = jnp.float32
bf16 = jnp.bfloat16


def sublane():
    return lax.broadcasted_iota(jnp.int32, (SUB, LANES), 0)


def owner(strip, pair, n):
    return (strip * PAIRS + pair) * MODES + n


def lanes_of(at):
    return pl.ds(pl.multiple_of(at * LANES, LANES), LANES)


def piece(r):
    return pl.ds(r * LANES, LANES)


def spread(ref, at, natural):
    half = RUN // SUB
    for r in range(ROWS // SUB):
        start = (r % half) * SUB * SUB + r // half
        ref[(*at, pl.ds(start, SUB, stride=SUB))] = natural[SUB * r : SUB * (r + 1), :]


def run_rows(ref, at, j):
    return ref[(*at, pl.ds(SUB * j, SUB))]


def for_filters(make):
    def body(i, _):
        make(i)
        return 0

    lax.fori_loop(0, STRIPS * MODES, body, 0)


def row_of(ref, i):
    return jnp.broadcast_to(ref[pl.ds(i, 1), :], (SUB, LANES))


def total(parts):
    while len(parts) > 1:
        parts = [a + b for a, b in zip(parts[::2], parts[1::2])]
    return parts[0]


def prepare_kernel(q_hbm, k_hbm, v_hbm, u_hbm, ps, gs, q_ref, k_ref, v_ref, u_ref, sems):
    def copies(blk):
        cols = pl.ds(blk * FILTERS, FILTERS)
        return [
            pltpu.make_async_copy(src.at[:, cols], dst.at[:, cols], sems.at[blk, i])
            for i, (src, dst) in enumerate(
                ((k_hbm, k_ref), (v_hbm, v_ref), (u_hbm, u_ref), (q_hbm, q_ref))
            )
        ]

    for blk in range(BLOCKS):
        for copy in copies(blk):
            copy.start()
    for blk in range(BLOCKS):
        for copy in copies(blk):
            copy.wait()

        def strip_body(strip, _):
            at = (strip, blk)
            cols = lanes_of(blk * STRIPS + strip)
            spread(ps, at, k_ref[:, cols].astype(f32) * v_ref[:, cols].astype(f32))
            spread(gs, at, u_ref[:, cols].astype(f32) * q_ref[:, cols].astype(f32))
            return 0

        lax.fori_loop(0, STRIPS, strip_body, 0)


def summarize_kernel(
    half_ref, mine_ref, other_ref, ps, gs,
    send_hbm, cf_hbm, cb_hbm, rates_hbm, residues_hbm, ps_hbm, gs_hbm,
    tab, lags, joins, send_ref, cf_ref, cb_ref, rates_ref, residues_ref, sems, early_sems,
):
    s = sublane()
    lower = jnp.broadcast_to(half_ref[0], (MODES, LANES)) == 0
    for strip in range(STRIPS):
        cols = pl.ds((strip % 2) * LANES, LANES)
        at = pl.ds(strip * MODES, MODES)
        for part, out in enumerate((rates_ref, residues_ref)):
            rows = pl.ds(part * MODES, MODES)
            here, there = mine_ref[rows, cols], other_ref[rows, cols]
            if strip < STRIPS // 2:
                out[at, :] = jnp.where(lower, here, there)
            else:
                out[at, :] = jnp.where(lower, there, here)

    stored = [
        pltpu.make_async_copy(a, b, early_sems.at[i])
        for i, (a, b) in enumerate(
            ((rates_ref, rates_hbm), (residues_ref, residues_hbm), (ps, ps_hbm), (gs, gs_hbm))
        )
    ]
    for copy in stored:
        copy.start()

    def make(i):
        log_decay = row_of(rates_ref, i) / TOKENS
        tab[0, i] = jnp.exp(-log_decay)
        for step in range(3):
            hop = 1 << step
            factor = jnp.exp(-log_decay * (RUN * hop))
            tab[1 + step, i] = jnp.where(s >= hop, factor, 0.0)
        tab[4, i] = jnp.exp(-log_decay * (RUN * s).astype(f32))

    for_filters(make)

    def sent(strip):
        at = pl.ds(strip * PAIRS * MODES, PAIRS * MODES)
        return [
            pltpu.make_async_copy(send_ref.at[at], send_hbm.at[at], sems.at[strip, 0]),
            pltpu.make_async_copy(cf_ref.at[strip], cf_hbm.at[strip], sems.at[strip, 1]),
            pltpu.make_async_copy(cb_ref.at[strip], cb_hbm.at[strip], sems.at[strip, 2]),
        ]

    def strip_body(strip, _):
        base = strip * MODES

        for lag in range(HALF):
            lags[lag] = jnp.zeros((SUB, LANES), f32)
        for n in range(MODES):
            joins[n] = jnp.zeros((SUB, LANES), f32)

        def pair_body(pair, _):
            for odd in range(2):
                at = (strip, 2 * pair + odd)
                decay = [tab[0, base + n] for n in range(MODES)]
                behind, middle = [None] * MODES, [None] * MODES
                for j in reversed(range(RUN)):
                    gated = run_rows(gs, at, j)
                    for n in range(MODES):
                        behind[n] = gated if j == RUN - 1 else decay[n] * behind[n] + gated
                    if j == HALF:
                        middle = list(behind)
                ahead, joint = [None] * MODES, [None] * MODES
                for j in range(RUN):
                    product = run_rows(ps, at, j)
                    for n in range(MODES):
                        ahead[n] = product if j == 0 else decay[n] * ahead[n] + product
                        if j == HALF - 1:
                            joint[n] = ahead[n] * middle[n]
                for lag in range(HALF):
                    starts = [j for j in range(RUN) if j // HALF == (j + lag) // HALF]
                    pairs = [run_rows(gs, at, j + lag) * run_rows(ps, at, j) for j in starts]
                    while len(pairs) > 1:
                        odd_one = pairs[-1:] if len(pairs) % 2 else []
                        pairs = [a + b for a, b in zip(pairs[::2], pairs[1::2])] + odd_one
                    lags[lag] = lags[lag] + pairs[0]
                for step in range(3):
                    for n in range(MODES):
                        moved = pltpu.roll(ahead[n], 1 << step, 0)
                        ahead[n] = ahead[n] + tab[1 + step, base + n] * moved
                for n in range(MODES):
                    place = owner(strip, pair, n)
                    send_ref[place, :, piece(odd)] = ahead[n][SUB - 1 :, :]
                    first = jnp.sum(tab[4, base + n] * behind[n], axis=0, keepdims=True)
                    send_ref[place, :, piece(2 + odd)] = first
                    enter = jnp.where(s >= 1, pltpu.roll(ahead[n], 1, 0), 0.0)
                    cf_ref[strip, 2 * pair + odd, n] = enter
                    cb_ref[strip, 2 * pair + odd, n] = behind[n]
                    joins[n] = joins[n] + (joint[n] + behind[n] * enter)
            return 0

        lax.fori_loop(0, PAIRS, pair_body, 0)
        for n in range(MODES):
            decay = tab[0, base + n]
            term = lags[HALF - 1]
            for lag in reversed(range(HALF - 1)):
                term = decay * term + lags[lag]
            term = jnp.sum(term + decay * joins[n], axis=0, keepdims=True)
            for pair in range(PAIRS):
                row = term if pair == 0 else jnp.zeros((1, LANES), f32)
                send_ref[owner(strip, pair, n), :, piece(4)] = row
        for copy in sent(strip):
            copy.start()
        return 0

    lax.fori_loop(0, STRIPS, strip_body, 0)
    for strip in range(STRIPS):
        for copy in sent(strip):
            copy.wait()
    for copy in stored:
        copy.wait()


def inner_kernel(reverse, rates_hbm, residues_hbm, xs_hbm, enter_hbm, *refs):
    if reverse:
        out_hbm, lead_ref = refs[:2]
    else:
        k_hbm, v_hbm, u_hbm, out_hbm, lead_ref, lead_k, lead_v, lead_u, late_tab = refs[:9]
    tab, rates_ref, residues_ref, xs, enter_ref, out_ref, param_sems, sems = refs[-8:]
    params = [
        pltpu.make_async_copy(rates_hbm, rates_ref, param_sems.at[0]),
        pltpu.make_async_copy(residues_hbm, residues_ref, param_sems.at[1]),
    ]

    def arrivals(strip):
        return [
            pltpu.make_async_copy(enter_hbm.at[strip], enter_ref.at[strip], sems.at[strip, 0]),
            pltpu.make_async_copy(xs_hbm.at[strip], xs.at[strip], sems.at[strip, 1]),
        ]

    def leaving(strip):
        return pltpu.make_async_copy(out_ref.at[strip], out_hbm.at[strip], sems.at[strip, 2])

    s = sublane()
    leads = []
    if not reverse:
        pairs = ((k_hbm, lead_k), (v_hbm, lead_v), (u_hbm, lead_u))
        for i, (a, b) in enumerate(pairs):
            source = a.at[:, pl.ds(0, FILTERS)]
            leads.append(pltpu.make_async_copy(source, b, param_sems.at[2 + i]))
    for copy in params:
        copy.start()
    for strip in range(STRIPS):
        for copy in arrivals(strip):
            copy.start()
    for copy in leads:
        copy.start()
    for copy in params:
        copy.wait()

    def make(i):
        rate = row_of(rates_ref, i)
        tab[0, i] = jnp.exp(-rate / TOKENS)
        tab[1, i] = row_of(residues_ref, i) * jnp.sqrt((1.0 + rate) / TOKENS)
        if not reverse:
            weight = tab[1, i]
            late_tab[0, i] = jnp.exp(-rate / TOKENS * SUB)
            late_tab[1, i] = weight * jnp.exp(-rate / TOKENS * (s + 1).astype(f32))
            late_tab[2, i] = weight * jnp.exp(-rate / TOKENS * (SUB - s).astype(f32))
        for step in range(3 if reverse else 0):
            factor = jnp.exp(-rate / TOKENS * (RUN << step))
            tab[2 + step, i] = jnp.where(s < SUB - (1 << step), factor, 0.0)

    for_filters(make)

    def strip_body(strip, _):
        for copy in arrivals(strip):
            copy.wait()
        base = strip * MODES

        def body(blk, _):
            at = (strip, blk)
            decay = [tab[0, base + n] for n in range(MODES)]
            weight = [tab[1, base + n] for n in range(MODES)]
            state = [enter_ref[strip, blk, n] for n in range(MODES)]
            if reverse:
                for step in range(3):
                    for n in range(MODES):
                        moved = pltpu.roll(state[n], SUB - (1 << step), 0)
                        state[n] = state[n] + tab[2 + step, base + n] * moved
                state = [jnp.where(s < SUB - 1, pltpu.roll(a, SUB - 1, 0), 0.0) for a in state]
            for j in reversed(range(RUN)) if reverse else range(RUN):
                x = run_rows(xs, at, j)
                state = [decay[n] * state[n] + x for n in range(MODES)]
                mixed = total([weight[n] * state[n] for n in range(MODES)])
                out_ref[strip, blk, pl.ds(j, SUB, stride=RUN), :] = mixed
            return 0

        lax.fori_loop(0, BLOCKS, body, 0)
        leaving(strip).start()
        lead_ref[strip] = out_ref[strip, 0]
        return 0

    lax.fori_loop(0, STRIPS, strip_body, 0)
    for strip in range(STRIPS):
        leaving(strip).wait()
    for copy in leads:
        copy.wait()


def carry_kernel(where_ref, rates_ref, x_ref, y_hbm, y_ref, sem):
    place = where_ref[0]
    at = (place // (PAIRS * MODES)) * MODES + place % MODES
    log_decay = rates_ref[pl.ds(at, 1), :] / TOKENS
    across = jnp.exp(-log_decay * ROWS)
    zero = jnp.zeros((1, LANES), f32)

    def step(i, carried):
        a0, a1, b0, b1, cross, terms = carried
        y_ref[i, :, piece(0)] = a0
        y_ref[i, :, piece(1)] = a1
        cross = cross + (a0 * x_ref[i, :, piece(2)] + a1 * x_ref[i, :, piece(3)])
        terms = terms + x_ref[i, :, piece(4)]
        back = SHARDS - 1 - i
        y_ref[back, :, piece(2)] = b0
        y_ref[back, :, piece(3)] = b1
        return (
            across * a0 + x_ref[i, :, piece(0)],
            across * a1 + x_ref[i, :, piece(1)],
            across * b0 + x_ref[back, :, piece(2)],
            across * b1 + x_ref[back, :, piece(3)],
            cross,
            terms,
        )

    carried = lax.fori_loop(0, SHARDS, step, (zero,) * 6, unroll=8)
    row = jnp.exp(-log_decay) * carried[4] + carried[5]

    def fill(i, _):
        y_ref[i, :, piece(4)] = row
        return 0

    lax.fori_loop(0, SHARDS, fill, 0, unroll=16)
    copy = pltpu.make_async_copy(y_ref, y_hbm, sem)
    copy.start()
    copy.wait()


def finish_kernel(turn, core_ref, *refs):
    @pl.when(core_ref[0] == turn)
    def _():
        finish_body(*refs[:12], *refs[-13:])


def finish_body(
    tab, k_hbm, v_hbm, u_hbm, conv_hbm, flow_hbm, in_ref,
    lead_k, lead_v, lead_u, lead_conv, lead_flow,
    gq_hbm, gk_hbm, gv_hbm,
    k_ref, v_ref, u_ref, conv_ref, flow_ref, gq_ref, gk_ref, gv_ref, arrive_sems, sems,
):
    def arrivals(blk):
        cols = pl.ds(blk * FILTERS, FILTERS)
        if not isinstance(blk, int):
            cols = pl.ds(pl.multiple_of(blk * FILTERS, FILTERS), FILTERS)
        pairs = [
            (a.at[:, blk], b.at[:, blk]) for a, b in ((conv_hbm, conv_ref), (flow_hbm, flow_ref))
        ]
        for a, b in ((u_hbm, u_ref), (v_hbm, v_ref), (k_hbm, k_ref)):
            pairs.append((a.at[:, cols], b.at[:, cols]))
        return [
            pltpu.make_async_copy(a, b, arrive_sems.at[blk, i]) for i, (a, b) in enumerate(pairs)
        ]

    for blk in range(1, BLOCKS):
        for copy in arrivals(blk):
            copy.start()
    lead = pl.ds(0, FILTERS)
    for a, b in ((lead_k, k_ref), (lead_v, v_ref), (lead_u, u_ref)):
        b[:, lead] = a[...]
    for strip in range(STRIPS):
        conv_ref[strip, 0] = lead_conv[strip]
        flow_ref[strip, 0] = lead_flow[strip]

    def copies(blk):
        cols = pl.ds(pl.multiple_of(blk * FILTERS, FILTERS), FILTERS)
        return [
            pltpu.make_async_copy(src.at[:, cols], dst.at[:, cols], sems.at[blk, i])
            for i, (src, dst) in enumerate(((gq_ref, gq_hbm), (gk_ref, gk_hbm), (gv_ref, gv_hbm)))
        ]

    def pair_body(pair, _):
        for odd in range(2):
            blk = 2 * pair + odd

            @pl.when(blk > 0)
            def _():
                for copy in arrivals(blk):
                    copy.wait()

            def strip_body(strip, _):
                base = strip * MODES
                cols = lanes_of(blk * STRIPS + strip)
                leap = [tab[0, base + n] for n in range(MODES)]
                places = [owner(strip, pair, n) for n in range(MODES)]
                state = [
                    tab[1, base + n] * in_ref[places[n], :, piece(odd)] for n in range(MODES)
                ]
                for i in range(ROWS // 16):
                    parts = []
                    for _ in range(2):
                        parts.append(total(state))
                        state = [leap[n] * state[n] for n in range(MODES)]
                    at = pl.ds(16 * i, 16)
                    conv = conv_ref[strip, blk, at, :] + jnp.concatenate(parts, axis=0)
                    gq_ref[at, cols] = (u_ref[at, cols].astype(f32) * conv).astype(bf16)
                state = [
                    tab[2, base + n] * in_ref[places[n], :, piece(2 + odd)] for n in range(MODES)
                ]
                for i in reversed(range(ROWS // 16)):
                    parts = []
                    for _ in range(2):
                        parts.insert(0, total(state))
                        state = [leap[n] * state[n] for n in range(MODES)]
                    at = pl.ds(16 * i, 16)
                    flow = flow_ref[strip, blk, at, :] + jnp.concatenate(parts, axis=0)
                    gk_ref[at, cols] = (flow * v_ref[at, cols].astype(f32)).astype(bf16)
                    gv_ref[at, cols] = (flow * k_ref[at, cols].astype(f32)).astype(bf16)
                return 0

            lax.fori_loop(0, STRIPS, strip_body, 0)
            for copy in copies(blk):
                copy.start()
        return 0

    lax.fori_loop(0, PAIRS, pair_body, 0)
    for blk in range(BLOCKS):
        for copy in copies(blk):
            copy.wait()


def in_hbm(*arrays):
    return [pltpu.with_memory_space_constraint(a, pltpu.HBM) for a in arrays]


def local(query_rows, key_rows, value_rows, upstream, decay_rate, residue):
    half = lax.axis_index("fsdp")
    swap = [(0, 1), (1, 0)]
    first = lax.broadcasted_iota(jnp.int32, (2 * MODES, FILTERS // 2), 0) < MODES
    below, above = ((0, MODES, 0), (0, 0, 0)), ((MODES, 0, 0), (0, 0, 0))
    zero = jnp.zeros((), f32)
    mine = jnp.where(first, lax.pad(decay_rate, zero, below), lax.pad(residue, zero, above))
    other = lax.ppermute(mine, "fsdp", swap)
    vmem = pl.BlockSpec(memory_space=pltpu.VMEM)
    smem = pl.BlockSpec(memory_space=pltpu.SMEM)
    hbm = pl.BlockSpec(memory_space=pltpu.HBM)
    limit = pltpu.CompilerParams(vmem_limit_bytes=16 << 20)
    packet = (SHARDS, 1, PACKET)
    packets = pltpu.HBM(packet, f32)
    tiles = (STRIPS, BLOCKS, ROWS, LANES)
    state = (STRIPS, BLOCKS, MODES, SUB, LANES)
    params = (STRIPS * MODES, LANES)
    table = (STRIPS * MODES, SUB, LANES)
    whole = pltpu.VMEM((ROWS, WIDTH), bf16)
    query_rows, key_rows, value_rows, upstream = in_hbm(
        query_rows, key_rows, value_rows, upstream
    )
    ps, gs = pl.pallas_call(
        prepare_kernel,
        in_specs=[hbm] * 4,
        out_specs=[vmem] * 2,
        out_shape=[jax.ShapeDtypeStruct(tiles, f32)] * 2,
        scratch_shapes=[whole] * 4 + [pltpu.SemaphoreType.DMA((BLOCKS, 4))],
        compiler_params=limit,
        cost_estimate=pl.CostEstimate(flops=1 << 22, bytes_accessed=12 << 20, transcendentals=0),
        name="prepare",
    )(query_rows, key_rows, value_rows, upstream)
    send, enter_ahead, enter_behind, rates, residues, product, gated = pl.pallas_call(
        summarize_kernel,
        in_specs=[smem] + [vmem] * 4,
        out_specs=[hbm] * 7,
        out_shape=[packets]
        + [pltpu.HBM(state, f32)] * 2
        + [pltpu.HBM(params, f32)] * 2
        + [pltpu.HBM(tiles, f32)] * 2,
        scratch_shapes=[
            pltpu.VMEM((5,) + table, f32),
            pltpu.VMEM((HALF, SUB, LANES), f32),
            pltpu.VMEM((MODES, SUB, LANES), f32),
            pltpu.VMEM(packet, f32),
            pltpu.VMEM(state, f32),
            pltpu.VMEM(state, f32),
            pltpu.VMEM(params, f32),
            pltpu.VMEM(params, f32),
            pltpu.SemaphoreType.DMA((STRIPS, 3)),
            pltpu.SemaphoreType.DMA((4,)),
        ],
        compiler_params=limit,
        name="summarize",
    )(half.astype(jnp.int32).reshape(1), mine, other, ps, gs)
    arrived = lax.all_to_all(send, ALL, 0, 0, tiled=True)

    lead = jax.ShapeDtypeStruct((STRIPS, ROWS, LANES), f32)
    lead_rows = jax.ShapeDtypeStruct((ROWS, FILTERS), bf16)

    def inner(xs, enter, reverse, extra=(), more=()):
        return pl.pallas_call(
            functools.partial(inner_kernel, reverse),
            in_specs=[hbm] * (4 + len(extra)),
            out_specs=[hbm] + [vmem] * (1 + len(more)),
            out_shape=[pltpu.HBM(tiles, f32), lead, *more],
            scratch_shapes=[
                pltpu.VMEM((5 if reverse else 2,) + table, f32),
                pltpu.VMEM(params, f32),
                pltpu.VMEM(params, f32),
                pltpu.VMEM(tiles, f32),
                pltpu.VMEM(state, f32),
                pltpu.VMEM(tiles, f32),
                pltpu.SemaphoreType.DMA((5,)),
                pltpu.SemaphoreType.DMA((STRIPS, 3)),
            ],
            compiler_params=limit,
            cost_estimate=pl.CostEstimate(
                flops=1 << 24, bytes_accessed=16 << 20, transcendentals=0
            ),
            name="behind" if reverse else "ahead",
        )(*in_hbm(rates, residues, xs, enter), *extra)

    late = jax.ShapeDtypeStruct((3,) + table, f32)
    conv, lead_conv, lead_k, lead_v, lead_u, late_tab = inner(
        product,
        enter_ahead,
        False,
        (key_rows, value_rows, upstream),
        (lead_rows, lead_rows, lead_rows, late),
    )
    arrived, conv = lax.optimization_barrier((arrived, conv))
    place = lax.axis_index(ALL).astype(jnp.int32).reshape(1)
    carries = pl.pallas_call(
        carry_kernel,
        in_specs=[smem] + [vmem] * 2,
        out_specs=hbm,
        out_shape=packets,
        scratch_shapes=[pltpu.VMEM(packet, f32), pltpu.SemaphoreType.DMA],
        compiler_params=limit,
        name="carry",
    )(place, rates, arrived)
    back = lax.all_to_all(carries, ALL, 0, 0, tiled=True)
    flowing, lead_flow = inner(gated, enter_behind, True)
    back, flowing = lax.optimization_barrier((back, flowing))
    rows = back[:, 0, 4 * LANES :].reshape(STRIPS, PAIRS, MODES, LANES)
    count = STRIPS // 2
    rows = lax.dynamic_slice_in_dim(rows, half * count, count, 0).sum(axis=1)
    conv, flowing = in_hbm(conv, flowing)
    core = lax.axis_index("ch").astype(jnp.int32).reshape(1)
    shapes = [pltpu.HBM((ROWS, WIDTH), bf16)] * 3

    def finish(turn, *before):
        return pl.pallas_call(
            functools.partial(finish_kernel, turn),
            in_specs=[smem, vmem] + [hbm] * 5 + [vmem] * 6 + [hbm] * len(before),
            out_specs=[hbm] * 3,
            out_shape=shapes,
            input_output_aliases={13 + i: i for i in range(len(before))},
            scratch_shapes=[
                whole,
                whole,
                whole,
                pltpu.VMEM(tiles, f32),
                pltpu.VMEM(tiles, f32),
                whole,
                whole,
                whole,
                pltpu.SemaphoreType.DMA((BLOCKS, 5)),
                pltpu.SemaphoreType.DMA((BLOCKS, 3)),
            ],
            compiler_params=limit,
            cost_estimate=pl.CostEstimate(
                flops=1 << 24, bytes_accessed=10 << 20, transcendentals=0
            ),
            name=f"finish{turn}",
        )(
            core, late_tab, key_rows, value_rows, upstream, conv, flowing, back,
            lead_k, lead_v, lead_u, lead_conv, lead_flow, *before,
        )

    from_first = lax.ppermute(rows, "ch", [(0, 1)])
    early = finish(1)
    own, from_first, *early = lax.optimization_barrier((rows, from_first, *early))
    from_second = lax.ppermute(own, "ch", [(1, 0)])
    grads_out = finish(0, *early)
    rows = rows + (from_first + from_second)
    rows = rows.transpose(1, 0, 2).reshape(MODES, count * LANES)
    gain = jnp.sqrt((1.0 + decay_rate) / TOKENS)
    residue_grad = gain * rows / math.sqrt(TOKENS)
    return (*grads_out, residue_grad)


def solution(mesh):
    rows = P(ALL, "ch")
    params = P(None, "fsdp")
    return jax.shard_map(
        local,
        mesh=mesh,
        in_specs=(rows, rows, rows, rows, params, params),
        out_specs=(rows, rows, rows, params),
        check_vma=False,
    )
```

```python
import functools
import math

import jax
import jax.numpy as jnp
from jax import lax
from jax.experimental import pallas as pl
from jax.experimental.pallas import tpu as pltpu
from jax.sharding import PartitionSpec as P

TOKENS = 16384
ROWS = 128
MODES = 8
FILTERS = 512
BLOCKS = 8
SUB = 8
RUN = ROWS // SUB
HALF = RUN // 2
LANES = 128
STRIPS = FILTERS // LANES
PAIRS = BLOCKS // 2
WIDTH = BLOCKS * FILTERS
SHARDS = TOKENS // ROWS
PACKET = 5 * LANES
HELD = 3
ALL = ("ctx", "fsdp")
f32 = jnp.float32
bf16 = jnp.bfloat16


def sublane():
    return lax.broadcasted_iota(jnp.int32, (SUB, LANES), 0)


def owner(strip, pair, n):
    return (strip * PAIRS + pair) * MODES + n


def lanes_of(at):
    return pl.ds(pl.multiple_of(at * LANES, LANES), LANES)


def piece(r):
    return pl.ds(r * LANES, LANES)


def spread(ref, at, natural):
    half = RUN // SUB
    for r in range(ROWS // SUB):
        start = (r % half) * SUB * SUB + r // half
        ref[(*at, pl.ds(start, SUB, stride=SUB))] = natural[SUB * r : SUB * (r + 1), :]


def run_rows(ref, at, j):
    return ref[(*at, pl.ds(SUB * j, SUB))]


def for_filters(make):
    def body(i, _):
        make(i)
        return 0

    lax.fori_loop(0, STRIPS * MODES, body, 0)


def row_of(ref, i):
    return jnp.broadcast_to(ref[pl.ds(i, 1), :], (SUB, LANES))


def total(parts):
    while len(parts) > 1:
        parts = [a + b for a, b in zip(parts[::2], parts[1::2])]
    return parts[0]


def prepare_kernel(q_hbm, k_hbm, v_hbm, u_hbm, ps, gs, q_ref, k_ref, v_ref, u_ref, sems):
    def copies(blk):
        cols = pl.ds(blk * FILTERS, FILTERS)
        return [
            pltpu.make_async_copy(src.at[:, cols], dst.at[:, cols], sems.at[blk, i])
            for i, (src, dst) in enumerate(
                ((k_hbm, k_ref), (v_hbm, v_ref), (u_hbm, u_ref), (q_hbm, q_ref))
            )
        ]

    for blk in range(BLOCKS):
        for copy in copies(blk):
            copy.start()
    for blk in range(BLOCKS):
        for copy in copies(blk):
            copy.wait()

        def strip_body(strip, _):
            at = (strip, blk)
            cols = lanes_of(blk * STRIPS + strip)
            spread(ps, at, k_ref[:, cols].astype(f32) * v_ref[:, cols].astype(f32))
            spread(gs, at, u_ref[:, cols].astype(f32) * q_ref[:, cols].astype(f32))
            return 0

        lax.fori_loop(0, STRIPS, strip_body, 0)


def summarize_kernel(
    half_ref, mine_ref, other_ref, ps, gs,
    send_hbm, cf_hbm, cb_hbm, rates_hbm, residues_hbm, ps_hbm, gs_hbm,
    tab, lags, joins, send_ref, cf_ref, cb_ref, rates_ref, residues_ref, sems, early_sems,
):
    s = sublane()
    lower = jnp.broadcast_to(half_ref[0], (MODES, LANES)) == 0
    for strip in range(STRIPS):
        cols = pl.ds((strip % 2) * LANES, LANES)
        at = pl.ds(strip * MODES, MODES)
        for part, out in enumerate((rates_ref, residues_ref)):
            rows = pl.ds(part * MODES, MODES)
            here, there = mine_ref[rows, cols], other_ref[rows, cols]
            if strip < STRIPS // 2:
                out[at, :] = jnp.where(lower, here, there)
            else:
                out[at, :] = jnp.where(lower, there, here)

    stored = [
        pltpu.make_async_copy(a, b, early_sems.at[i])
        for i, (a, b) in enumerate(
            ((rates_ref, rates_hbm), (residues_ref, residues_hbm), (ps, ps_hbm), (gs, gs_hbm))
        )
    ]
    for copy in stored:
        copy.start()

    def make(i):
        log_decay = row_of(rates_ref, i) / TOKENS
        tab[0, i] = jnp.exp(-log_decay)
        for step in range(3):
            hop = 1 << step
            factor = jnp.exp(-log_decay * (RUN * hop))
            tab[1 + step, i] = jnp.where(s >= hop, factor, 0.0)
        tab[4, i] = jnp.exp(-log_decay * (RUN * s).astype(f32))

    for_filters(make)

    def sent(strip):
        at = pl.ds(strip * PAIRS * MODES, PAIRS * MODES)
        return [
            pltpu.make_async_copy(send_ref.at[at], send_hbm.at[at], sems.at[strip, 0]),
            pltpu.make_async_copy(cf_ref.at[strip], cf_hbm.at[strip], sems.at[strip, 1]),
            pltpu.make_async_copy(cb_ref.at[strip], cb_hbm.at[strip], sems.at[strip, 2]),
        ]

    def strip_body(strip, _):
        base = strip * MODES

        for lag in range(HALF):
            lags[lag] = jnp.zeros((SUB, LANES), f32)
        for n in range(MODES):
            joins[n] = jnp.zeros((SUB, LANES), f32)

        def pair_body(pair, _):
            for odd in range(2):
                at = (strip, 2 * pair + odd)
                decay = [tab[0, base + n] for n in range(MODES)]
                behind, middle = [None] * MODES, [None] * MODES
                for j in reversed(range(RUN)):
                    gated = run_rows(gs, at, j)
                    for n in range(MODES):
                        behind[n] = gated if j == RUN - 1 else decay[n] * behind[n] + gated
                    if j == HALF:
                        middle = list(behind)
                ahead, joint = [None] * MODES, [None] * MODES
                for j in range(RUN):
                    product = run_rows(ps, at, j)
                    for n in range(MODES):
                        ahead[n] = product if j == 0 else decay[n] * ahead[n] + product
                        if j == HALF - 1:
                            joint[n] = ahead[n] * middle[n]
                for lag in range(HALF):
                    starts = [j for j in range(RUN) if j // HALF == (j + lag) // HALF]
                    pairs = [run_rows(gs, at, j + lag) * run_rows(ps, at, j) for j in starts]
                    while len(pairs) > 1:
                        odd_one = pairs[-1:] if len(pairs) % 2 else []
                        pairs = [a + b for a, b in zip(pairs[::2], pairs[1::2])] + odd_one
                    lags[lag] = lags[lag] + pairs[0]
                for step in range(3):
                    for n in range(MODES):
                        moved = pltpu.roll(ahead[n], 1 << step, 0)
                        ahead[n] = ahead[n] + tab[1 + step, base + n] * moved
                for n in range(MODES):
                    place = owner(strip, pair, n)
                    send_ref[place, :, piece(odd)] = ahead[n][SUB - 1 :, :]
                    first = jnp.sum(tab[4, base + n] * behind[n], axis=0, keepdims=True)
                    send_ref[place, :, piece(2 + odd)] = first
                    enter = jnp.where(s >= 1, pltpu.roll(ahead[n], 1, 0), 0.0)
                    cf_ref[strip, 2 * pair + odd, n] = enter
                    cb_ref[strip, 2 * pair + odd, n] = behind[n]
                    joins[n] = joins[n] + (joint[n] + behind[n] * enter)
            return 0

        lax.fori_loop(0, PAIRS, pair_body, 0)
        for n in range(MODES):
            decay = tab[0, base + n]
            term = lags[HALF - 1]
            for lag in reversed(range(HALF - 1)):
                term = decay * term + lags[lag]
            term = jnp.sum(term + decay * joins[n], axis=0, keepdims=True)
            for pair in range(PAIRS):
                row = term if pair == 0 else jnp.zeros((1, LANES), f32)
                send_ref[owner(strip, pair, n), :, piece(4)] = row
        for copy in sent(strip):
            copy.start()
        return 0

    lax.fori_loop(0, STRIPS, strip_body, 0)
    for strip in range(STRIPS):
        for copy in sent(strip):
            copy.wait()
    for copy in stored:
        copy.wait()


def inner_kernel(reverse, rates_hbm, residues_hbm, xs_hbm, enter_hbm, *refs):
    if reverse:
        out_hbm, lead_ref = refs[:2]
    else:
        k_hbm, v_hbm, u_hbm, out_hbm, lead_ref, lead_k, lead_v, lead_u, late_tab = refs[:9]
    tab, rates_ref, residues_ref, xs, enter_ref, out_ref, param_sems, sems = refs[-8:]
    params = [
        pltpu.make_async_copy(rates_hbm, rates_ref, param_sems.at[0]),
        pltpu.make_async_copy(residues_hbm, residues_ref, param_sems.at[1]),
    ]

    def arrivals(strip):
        return [
            pltpu.make_async_copy(enter_hbm.at[strip], enter_ref.at[strip], sems.at[strip, 0]),
            pltpu.make_async_copy(xs_hbm.at[strip], xs.at[strip], sems.at[strip, 1]),
        ]

    def leaving(strip):
        return pltpu.make_async_copy(out_ref.at[strip], out_hbm.at[strip], sems.at[strip, 2])

    s = sublane()
    leads = []
    if not reverse:
        pairs = ((k_hbm, lead_k), (v_hbm, lead_v), (u_hbm, lead_u))
        for i, (a, b) in enumerate(pairs):
            source = a.at[:, pl.ds(0, FILTERS)]
            leads.append(pltpu.make_async_copy(source, b, param_sems.at[2 + i]))
    for copy in params:
        copy.start()
    for strip in range(STRIPS):
        for copy in arrivals(strip):
            copy.start()
    for copy in leads:
        copy.start()
    for copy in params:
        copy.wait()

    def make(i):
        rate = row_of(rates_ref, i)
        tab[0, i] = jnp.exp(-rate / TOKENS)
        tab[1, i] = row_of(residues_ref, i) * jnp.sqrt((1.0 + rate) / TOKENS)
        if not reverse:
            weight = tab[1, i]
            late_tab[0, i] = jnp.exp(-rate / TOKENS * SUB)
            late_tab[1, i] = weight * jnp.exp(-rate / TOKENS * (s + 1).astype(f32))
            late_tab[2, i] = weight * jnp.exp(-rate / TOKENS * (SUB - s).astype(f32))
        for step in range(3 if reverse else 0):
            factor = jnp.exp(-rate / TOKENS * (RUN << step))
            tab[2 + step, i] = jnp.where(s < SUB - (1 << step), factor, 0.0)

    for_filters(make)

    def strip_body(strip, _):
        for copy in arrivals(strip):
            copy.wait()
        base = strip * MODES

        def body(blk, _):
            at = (strip, blk)
            decay = [tab[0, base + n] for n in range(MODES)]
            weight = [tab[1, base + n] for n in range(MODES)]
            state = [enter_ref[strip, blk, n] for n in range(MODES)]
            if reverse:
                for step in range(3):
                    for n in range(MODES):
                        moved = pltpu.roll(state[n], SUB - (1 << step), 0)
                        state[n] = state[n] + tab[2 + step, base + n] * moved
                state = [jnp.where(s < SUB - 1, pltpu.roll(a, SUB - 1, 0), 0.0) for a in state]
            for j in reversed(range(RUN)) if reverse else range(RUN):
                x = run_rows(xs, at, j)
                state = [decay[n] * state[n] + x for n in range(MODES)]
                mixed = total([weight[n] * state[n] for n in range(MODES)])
                out_ref[strip, blk, pl.ds(j, SUB, stride=RUN), :] = mixed
            return 0

        lax.fori_loop(0, BLOCKS, body, 0)
        leaving(strip).start()
        lead_ref[strip] = out_ref[strip, 0]
        return 0

    lax.fori_loop(0, STRIPS, strip_body, 0)
    for strip in range(STRIPS):
        leaving(strip).wait()
    for copy in leads:
        copy.wait()


def carry_kernel(where_ref, rates_ref, x_ref, y_hbm, y_ref, sem):
    place = where_ref[0]
    at = (place // (PAIRS * MODES)) * MODES + place % MODES
    log_decay = rates_ref[pl.ds(at, 1), :] / TOKENS
    across = jnp.exp(-log_decay * ROWS)
    zero = jnp.zeros((1, LANES), f32)

    def step(i, carried):
        a0, a1, b0, b1, cross, terms = carried
        y_ref[i, :, piece(0)] = a0
        y_ref[i, :, piece(1)] = a1
        cross = cross + (a0 * x_ref[i, :, piece(2)] + a1 * x_ref[i, :, piece(3)])
        terms = terms + x_ref[i, :, piece(4)]
        back = SHARDS - 1 - i
        y_ref[back, :, piece(2)] = b0
        y_ref[back, :, piece(3)] = b1
        return (
            across * a0 + x_ref[i, :, piece(0)],
            across * a1 + x_ref[i, :, piece(1)],
            across * b0 + x_ref[back, :, piece(2)],
            across * b1 + x_ref[back, :, piece(3)],
            cross,
            terms,
        )

    carried = lax.fori_loop(0, SHARDS, step, (zero,) * 6, unroll=8)
    row = jnp.exp(-log_decay) * carried[4] + carried[5]

    def fill(i, _):
        y_ref[i, :, piece(4)] = row
        return 0

    lax.fori_loop(0, SHARDS, fill, 0, unroll=16)
    copy = pltpu.make_async_copy(y_ref, y_hbm, sem)
    copy.start()
    copy.wait()


def finish_kernel(last, core_ref, tab, k_hbm, v_hbm, u_hbm, conv_hbm, flow_hbm, in_ref, *refs):
    gq_hbm, gk_hbm, gv_hbm, k_ref, v_ref, u_ref, conv_ref, flow_ref = refs[-13:-5]
    gq_ref, gk_ref, gv_ref, arrive_sems, sems = refs[-5:]
    second = core_ref[0] == 1
    if last:
        low, high = 0, jnp.where(second, HELD, BLOCKS)
    else:
        low, high = HELD, jnp.where(second, BLOCKS, HELD)

    def for_blocks(do, first=low):
        def body(blk, _):
            do(blk)
            return 0

        lax.fori_loop(first, high, body, 0)

    def arrivals(blk):
        cols = pl.ds(pl.multiple_of(blk * FILTERS, FILTERS), FILTERS)
        pairs = [
            (a.at[:, blk], b.at[:, blk]) for a, b in ((conv_hbm, conv_ref), (flow_hbm, flow_ref))
        ]
        for a, b in ((u_hbm, u_ref), (v_hbm, v_ref), (k_hbm, k_ref)):
            pairs.append((a.at[:, cols], b.at[:, cols]))
        return [
            pltpu.make_async_copy(a, b, arrive_sems.at[blk, i]) for i, (a, b) in enumerate(pairs)
        ]

    def fetch(blk):
        for copy in arrivals(blk):
            copy.start()

    for_blocks(fetch, max(low, 1))
    if last:
        lead_k, lead_v, lead_u, lead_conv, lead_flow = refs[:5]
        lead = pl.ds(0, FILTERS)
        for a, b in ((lead_k, k_ref), (lead_v, v_ref), (lead_u, u_ref)):
            b[:, lead] = a[...]
        for strip in range(STRIPS):
            conv_ref[strip, 0] = lead_conv[strip]
            flow_ref[strip, 0] = lead_flow[strip]

    def copies(blk):
        cols = pl.ds(pl.multiple_of(blk * FILTERS, FILTERS), FILTERS)
        return [
            pltpu.make_async_copy(src.at[:, cols], dst.at[:, cols], sems.at[blk, i])
            for i, (src, dst) in enumerate(((gq_ref, gq_hbm), (gk_ref, gk_hbm), (gv_ref, gv_hbm)))
        ]

    def block(blk):
        pair, odd = blk // 2, blk % 2

        @pl.when(blk > 0)
        def _():
            for copy in arrivals(blk):
                copy.wait()

        def strip_body(strip, _):
            base = strip * MODES
            cols = lanes_of(blk * STRIPS + strip)
            leap = [tab[0, base + n] for n in range(MODES)]
            places = [owner(strip, pair, n) for n in range(MODES)]
            state = [
                tab[1, base + n] * in_ref[places[n], :, lanes_of(odd)] for n in range(MODES)
            ]
            for i in range(ROWS // 16):
                parts = []
                for _ in range(2):
                    parts.append(total(state))
                    state = [leap[n] * state[n] for n in range(MODES)]
                at = pl.ds(16 * i, 16)
                conv = conv_ref[strip, blk, at, :] + jnp.concatenate(parts, axis=0)
                gq_ref[at, cols] = (u_ref[at, cols].astype(f32) * conv).astype(bf16)
            state = [
                tab[2, base + n] * in_ref[places[n], :, lanes_of(2 + odd)] for n in range(MODES)
            ]
            for i in reversed(range(ROWS // 16)):
                parts = []
                for _ in range(2):
                    parts.insert(0, total(state))
                    state = [leap[n] * state[n] for n in range(MODES)]
                at = pl.ds(16 * i, 16)
                flow = flow_ref[strip, blk, at, :] + jnp.concatenate(parts, axis=0)
                gk_ref[at, cols] = (flow * v_ref[at, cols].astype(f32)).astype(bf16)
                gv_ref[at, cols] = (flow * k_ref[at, cols].astype(f32)).astype(bf16)
            return 0

        lax.fori_loop(0, STRIPS, strip_body, 0)
        for copy in copies(blk):
            copy.start()

    for_blocks(block)

    def drain(blk):
        for copy in copies(blk):
            copy.wait()

    for_blocks(drain)


def in_hbm(*arrays):
    return [pltpu.with_memory_space_constraint(a, pltpu.HBM) for a in arrays]


def local(query_rows, key_rows, value_rows, upstream, decay_rate, residue):
    half = lax.axis_index("fsdp")
    swap = [(0, 1), (1, 0)]
    first = lax.broadcasted_iota(jnp.int32, (2 * MODES, FILTERS // 2), 0) < MODES
    below, above = ((0, MODES, 0), (0, 0, 0)), ((MODES, 0, 0), (0, 0, 0))
    zero = jnp.zeros((), f32)
    mine = jnp.where(first, lax.pad(decay_rate, zero, below), lax.pad(residue, zero, above))
    other = lax.ppermute(mine, "fsdp", swap)
    vmem = pl.BlockSpec(memory_space=pltpu.VMEM)
    smem = pl.BlockSpec(memory_space=pltpu.SMEM)
    hbm = pl.BlockSpec(memory_space=pltpu.HBM)
    limit = pltpu.CompilerParams(vmem_limit_bytes=16 << 20)
    packet = (SHARDS, 1, PACKET)
    packets = pltpu.HBM(packet, f32)
    tiles = (STRIPS, BLOCKS, ROWS, LANES)
    state = (STRIPS, BLOCKS, MODES, SUB, LANES)
    params = (STRIPS * MODES, LANES)
    table = (STRIPS * MODES, SUB, LANES)
    whole = pltpu.VMEM((ROWS, WIDTH), bf16)
    query_rows, key_rows, value_rows, upstream = in_hbm(
        query_rows, key_rows, value_rows, upstream
    )
    ps, gs = pl.pallas_call(
        prepare_kernel,
        in_specs=[hbm] * 4,
        out_specs=[vmem] * 2,
        out_shape=[jax.ShapeDtypeStruct(tiles, f32)] * 2,
        scratch_shapes=[whole] * 4 + [pltpu.SemaphoreType.DMA((BLOCKS, 4))],
        compiler_params=limit,
        cost_estimate=pl.CostEstimate(flops=1 << 22, bytes_accessed=12 << 20, transcendentals=0),
        name="prepare",
    )(query_rows, key_rows, value_rows, upstream)
    send, enter_ahead, enter_behind, rates, residues, product, gated = pl.pallas_call(
        summarize_kernel,
        in_specs=[smem] + [vmem] * 4,
        out_specs=[hbm] * 7,
        out_shape=[packets]
        + [pltpu.HBM(state, f32)] * 2
        + [pltpu.HBM(params, f32)] * 2
        + [pltpu.HBM(tiles, f32)] * 2,
        scratch_shapes=[
            pltpu.VMEM((5,) + table, f32),
            pltpu.VMEM((HALF, SUB, LANES), f32),
            pltpu.VMEM((MODES, SUB, LANES), f32),
            pltpu.VMEM(packet, f32),
            pltpu.VMEM(state, f32),
            pltpu.VMEM(state, f32),
            pltpu.VMEM(params, f32),
            pltpu.VMEM(params, f32),
            pltpu.SemaphoreType.DMA((STRIPS, 3)),
            pltpu.SemaphoreType.DMA((4,)),
        ],
        compiler_params=limit,
        name="summarize",
    )(half.astype(jnp.int32).reshape(1), mine, other, ps, gs)
    arrived = lax.all_to_all(send, ALL, 0, 0, tiled=True)

    lead = jax.ShapeDtypeStruct((STRIPS, ROWS, LANES), f32)
    lead_rows = jax.ShapeDtypeStruct((ROWS, FILTERS), bf16)

    def inner(xs, enter, reverse, extra=(), more=()):
        return pl.pallas_call(
            functools.partial(inner_kernel, reverse),
            in_specs=[hbm] * (4 + len(extra)),
            out_specs=[hbm] + [vmem] * (1 + len(more)),
            out_shape=[pltpu.HBM(tiles, f32), lead, *more],
            scratch_shapes=[
                pltpu.VMEM((5 if reverse else 2,) + table, f32),
                pltpu.VMEM(params, f32),
                pltpu.VMEM(params, f32),
                pltpu.VMEM(tiles, f32),
                pltpu.VMEM(state, f32),
                pltpu.VMEM(tiles, f32),
                pltpu.SemaphoreType.DMA((5,)),
                pltpu.SemaphoreType.DMA((STRIPS, 3)),
            ],
            compiler_params=limit,
            cost_estimate=pl.CostEstimate(
                flops=1 << 24, bytes_accessed=16 << 20, transcendentals=0
            ),
            name="behind" if reverse else "ahead",
        )(*in_hbm(rates, residues, xs, enter), *extra)

    late = jax.ShapeDtypeStruct((3,) + table, f32)
    conv, lead_conv, lead_k, lead_v, lead_u, late_tab = inner(
        product,
        enter_ahead,
        False,
        (key_rows, value_rows, upstream),
        (lead_rows, lead_rows, lead_rows, late),
    )
    arrived, conv = lax.optimization_barrier((arrived, conv))
    place = lax.axis_index(ALL).astype(jnp.int32).reshape(1)
    carries = pl.pallas_call(
        carry_kernel,
        in_specs=[smem] + [vmem] * 2,
        out_specs=hbm,
        out_shape=packets,
        scratch_shapes=[pltpu.VMEM(packet, f32), pltpu.SemaphoreType.DMA],
        compiler_params=limit,
        name="carry",
    )(place, rates, arrived)
    back = lax.all_to_all(carries, ALL, 0, 0, tiled=True)
    flowing, lead_flow = inner(gated, enter_behind, True)
    back, flowing = lax.optimization_barrier((back, flowing))
    rows = back[:, 0, 4 * LANES :].reshape(STRIPS, PAIRS, MODES, LANES)
    count = STRIPS // 2
    rows = lax.dynamic_slice_in_dim(rows, half * count, count, 0).sum(axis=1)
    conv, flowing = in_hbm(conv, flowing)
    core = lax.axis_index("ch").astype(jnp.int32).reshape(1)
    shapes = [pltpu.HBM((ROWS, WIDTH), bf16)] * 3

    def finish(last, leads=(), before=()):
        count_in = 8 + len(leads)
        return pl.pallas_call(
            functools.partial(finish_kernel, last),
            in_specs=[smem, vmem]
            + [hbm] * 5
            + [vmem] * (1 + len(leads))
            + [hbm] * len(before),
            out_specs=[hbm] * 3,
            out_shape=shapes,
            input_output_aliases={count_in + i: i for i in range(len(before))},
            scratch_shapes=[
                whole,
                whole,
                whole,
                pltpu.VMEM(tiles, f32),
                pltpu.VMEM(tiles, f32),
                whole,
                whole,
                whole,
                pltpu.SemaphoreType.DMA((BLOCKS, 5)),
                pltpu.SemaphoreType.DMA((BLOCKS, 3)),
            ],
            compiler_params=limit,
            cost_estimate=pl.CostEstimate(
                flops=1 << 24, bytes_accessed=10 << 20, transcendentals=0
            ),
            name="finish" if last else "begin",
        )(
            core, late_tab, key_rows, value_rows, upstream, conv, flowing, back, *leads, *before
        )

    early = finish(False)
    own, *early = lax.optimization_barrier((rows, *early))
    rows = rows + lax.ppermute(own, "ch", swap)
    grads_out = finish(True, (lead_k, lead_v, lead_u, lead_conv, lead_flow), early)
    rows = rows.transpose(1, 0, 2).reshape(MODES, count * LANES)
    gain = jnp.sqrt((1.0 + decay_rate) / TOKENS)
    residue_grad = gain * rows / math.sqrt(TOKENS)
    return (*grads_out, residue_grad)


def solution(mesh):
    rows = P(ALL, "ch")
    params = P(None, "fsdp")
    return jax.shard_map(
        local,
        mesh=mesh,
        in_specs=(rows, rows, rows, rows, params, params),
        out_specs=(rows, rows, rows, params),
        check_vma=False,
    )
```

```python
import functools
import math

import jax
import jax.numpy as jnp
from jax import lax
from jax.experimental import pallas as pl
from jax.experimental.pallas import tpu as pltpu
from jax.sharding import PartitionSpec as P

TOKENS = 16384
ROWS = 128
MODES = 8
FILTERS = 512
BLOCKS = 8
SUB = 8
RUN = ROWS // SUB
HALF = RUN // 2
LANES = 128
STRIPS = FILTERS // LANES
PAIRS = BLOCKS // 2
WIDTH = BLOCKS * FILTERS
SHARDS = TOKENS // ROWS
PACKET = 5 * LANES
HELD = 3
ALL = ("ctx", "fsdp")
f32 = jnp.float32
bf16 = jnp.bfloat16


def sublane():
    return lax.broadcasted_iota(jnp.int32, (SUB, LANES), 0)


def owner(strip, pair, n):
    return (strip * PAIRS + pair) * MODES + n


def lanes_of(at):
    return pl.ds(pl.multiple_of(at * LANES, LANES), LANES)


def piece(r):
    return pl.ds(r * LANES, LANES)


def spread(ref, at, natural):
    half = RUN // SUB
    for r in range(ROWS // SUB):
        start = (r % half) * SUB * SUB + r // half
        ref[(*at, pl.ds(start, SUB, stride=SUB))] = natural[SUB * r : SUB * (r + 1), :]


def run_rows(ref, at, j):
    return ref[(*at, pl.ds(SUB * j, SUB))]


def for_filters(make):
    def body(i, _):
        make(i)
        return 0

    lax.fori_loop(0, STRIPS * MODES, body, 0)


def row_of(ref, i):
    return jnp.broadcast_to(ref[pl.ds(i, 1), :], (SUB, LANES))


def total(parts):
    while len(parts) > 1:
        parts = [a + b for a, b in zip(parts[::2], parts[1::2])]
    return parts[0]


def prepare_kernel(q_hbm, k_hbm, v_hbm, u_hbm, ps, gs, q_ref, k_ref, v_ref, u_ref, sems):
    def copies(blk):
        cols = pl.ds(blk * FILTERS, FILTERS)
        return [
            pltpu.make_async_copy(src.at[:, cols], dst.at[:, cols], sems.at[blk, i])
            for i, (src, dst) in enumerate(
                ((k_hbm, k_ref), (v_hbm, v_ref), (u_hbm, u_ref), (q_hbm, q_ref))
            )
        ]

    for blk in range(BLOCKS):
        for copy in copies(blk):
            copy.start()
    for blk in range(BLOCKS):
        for copy in copies(blk):
            copy.wait()

        def strip_body(strip, _):
            at = (strip, blk)
            cols = lanes_of(blk * STRIPS + strip)
            spread(ps, at, k_ref[:, cols].astype(f32) * v_ref[:, cols].astype(f32))
            spread(gs, at, u_ref[:, cols].astype(f32) * q_ref[:, cols].astype(f32))
            return 0

        lax.fori_loop(0, STRIPS, strip_body, 0)


def summarize_kernel(
    half_ref, mine_ref, other_ref, ps, gs,
    send_hbm, cf_hbm, cb_hbm, rates_hbm, residues_hbm, ps_hbm, gs_hbm,
    tab, lags, joins, send_ref, cf_ref, cb_ref, rates_ref, residues_ref, sems, early_sems,
):
    s = sublane()
    lower = jnp.broadcast_to(half_ref[0], (MODES, LANES)) == 0
    for strip in range(STRIPS):
        cols = pl.ds((strip % 2) * LANES, LANES)
        at = pl.ds(strip * MODES, MODES)
        for part, out in enumerate((rates_ref, residues_ref)):
            rows = pl.ds(part * MODES, MODES)
            here, there = mine_ref[rows, cols], other_ref[rows, cols]
            if strip < STRIPS // 2:
                out[at, :] = jnp.where(lower, here, there)
            else:
                out[at, :] = jnp.where(lower, there, here)

    stored = [
        pltpu.make_async_copy(a, b, early_sems.at[i])
        for i, (a, b) in enumerate(
            ((rates_ref, rates_hbm), (residues_ref, residues_hbm), (ps, ps_hbm), (gs, gs_hbm))
        )
    ]
    for copy in stored:
        copy.start()

    def make(i):
        log_decay = row_of(rates_ref, i) / TOKENS
        tab[0, i] = jnp.exp(-log_decay)
        for step in range(3):
            hop = 1 << step
            factor = jnp.exp(-log_decay * (RUN * hop))
            tab[1 + step, i] = jnp.where(s >= hop, factor, 0.0)
        tab[4, i] = jnp.exp(-log_decay * (RUN * s).astype(f32))

    for_filters(make)

    def sent(strip):
        at = pl.ds(strip * PAIRS * MODES, PAIRS * MODES)
        return [
            pltpu.make_async_copy(send_ref.at[at], send_hbm.at[at], sems.at[strip, 0]),
            pltpu.make_async_copy(cf_ref.at[strip], cf_hbm.at[strip], sems.at[strip, 1]),
            pltpu.make_async_copy(cb_ref.at[strip], cb_hbm.at[strip], sems.at[strip, 2]),
        ]

    def strip_body(strip, _):
        base = strip * MODES

        for lag in range(HALF):
            lags[lag] = jnp.zeros((SUB, LANES), f32)
        for n in range(MODES):
            joins[n] = jnp.zeros((SUB, LANES), f32)

        def pair_body(pair, _):
            for odd in range(2):
                at = (strip, 2 * pair + odd)
                decay = [tab[0, base + n] for n in range(MODES)]
                behind, middle = [None] * MODES, [None] * MODES
                for j in reversed(range(RUN)):
                    gated = run_rows(gs, at, j)
                    for n in range(MODES):
                        behind[n] = gated if j == RUN - 1 else decay[n] * behind[n] + gated
                    if j == HALF:
                        middle = list(behind)
                ahead, joint = [None] * MODES, [None] * MODES
                for j in range(RUN):
                    product = run_rows(ps, at, j)
                    for n in range(MODES):
                        ahead[n] = product if j == 0 else decay[n] * ahead[n] + product
                        if j == HALF - 1:
                            joint[n] = ahead[n] * middle[n]
                for lag in range(HALF):
                    starts = [j for j in range(RUN) if j // HALF == (j + lag) // HALF]
                    pairs = [run_rows(gs, at, j + lag) * run_rows(ps, at, j) for j in starts]
                    while len(pairs) > 1:
                        odd_one = pairs[-1:] if len(pairs) % 2 else []
                        pairs = [a + b for a, b in zip(pairs[::2], pairs[1::2])] + odd_one
                    lags[lag] = lags[lag] + pairs[0]
                for step in range(3):
                    for n in range(MODES):
                        moved = pltpu.roll(ahead[n], 1 << step, 0)
                        ahead[n] = ahead[n] + tab[1 + step, base + n] * moved
                for n in range(MODES):
                    place = owner(strip, pair, n)
                    send_ref[place, :, piece(odd)] = ahead[n][SUB - 1 :, :]
                    first = jnp.sum(tab[4, base + n] * behind[n], axis=0, keepdims=True)
                    send_ref[place, :, piece(2 + odd)] = first
                    enter = jnp.where(s >= 1, pltpu.roll(ahead[n], 1, 0), 0.0)
                    cf_ref[strip, 2 * pair + odd, n] = enter
                    cb_ref[strip, 2 * pair + odd, n] = behind[n]
                    joins[n] = joins[n] + (joint[n] + behind[n] * enter)
            return 0

        lax.fori_loop(0, PAIRS, pair_body, 0)
        for n in range(MODES):
            decay = tab[0, base + n]
            term = lags[HALF - 1]
            for lag in reversed(range(HALF - 1)):
                term = decay * term + lags[lag]
            term = jnp.sum(term + decay * joins[n], axis=0, keepdims=True)
            for pair in range(PAIRS):
                row = term if pair == 0 else jnp.zeros((1, LANES), f32)
                send_ref[owner(strip, pair, n), :, piece(4)] = row
        for copy in sent(strip):
            copy.start()
        return 0

    lax.fori_loop(0, STRIPS, strip_body, 0)
    for strip in range(STRIPS):
        for copy in sent(strip):
            copy.wait()
    for copy in stored:
        copy.wait()


def inner_kernel(reverse, rates_hbm, residues_hbm, xs_hbm, enter_hbm, *refs):
    if reverse:
        out_hbm, *lead_refs = refs[:3]
    else:
        rows_hbm, out_hbm, lead_refs, late_tab = refs[:3], refs[3], refs[4:6], refs[6]
        lead_rows = refs[7:13]
    tab, rates_ref, residues_ref, xs, enter_ref, out_ref, param_sems, sems = refs[-8:]
    params = [
        pltpu.make_async_copy(rates_hbm, rates_ref, param_sems.at[0]),
        pltpu.make_async_copy(residues_hbm, residues_ref, param_sems.at[1]),
    ]

    def arrivals(strip):
        return [
            pltpu.make_async_copy(enter_hbm.at[strip], enter_ref.at[strip], sems.at[strip, 0]),
            pltpu.make_async_copy(xs_hbm.at[strip], xs.at[strip], sems.at[strip, 1]),
        ]

    def leaving(strip):
        return pltpu.make_async_copy(out_ref.at[strip], out_hbm.at[strip], sems.at[strip, 2])

    s = sublane()
    leads = []
    if not reverse:
        for i, b in enumerate(lead_rows):
            source = rows_hbm[i % 3].at[:, pl.ds((i // 3) * HELD * FILTERS, FILTERS)]
            leads.append(pltpu.make_async_copy(source, b, param_sems.at[2 + i]))
    for copy in params:
        copy.start()
    for strip in range(STRIPS):
        for copy in arrivals(strip):
            copy.start()
    for copy in leads:
        copy.start()
    for copy in params:
        copy.wait()

    def make(i):
        rate = row_of(rates_ref, i)
        tab[0, i] = jnp.exp(-rate / TOKENS)
        tab[1, i] = row_of(residues_ref, i) * jnp.sqrt((1.0 + rate) / TOKENS)
        if not reverse:
            weight = tab[1, i]
            late_tab[0, i] = jnp.exp(-rate / TOKENS * SUB)
            late_tab[1, i] = weight * jnp.exp(-rate / TOKENS * (s + 1).astype(f32))
            late_tab[2, i] = weight * jnp.exp(-rate / TOKENS * (SUB - s).astype(f32))
        for step in range(3 if reverse else 0):
            factor = jnp.exp(-rate / TOKENS * (RUN << step))
            tab[2 + step, i] = jnp.where(s < SUB - (1 << step), factor, 0.0)

    for_filters(make)

    def strip_body(strip, _):
        for copy in arrivals(strip):
            copy.wait()
        base = strip * MODES

        def body(blk, _):
            at = (strip, blk)
            decay = [tab[0, base + n] for n in range(MODES)]
            weight = [tab[1, base + n] for n in range(MODES)]
            state = [enter_ref[strip, blk, n] for n in range(MODES)]
            if reverse:
                for step in range(3):
                    for n in range(MODES):
                        moved = pltpu.roll(state[n], SUB - (1 << step), 0)
                        state[n] = state[n] + tab[2 + step, base + n] * moved
                state = [jnp.where(s < SUB - 1, pltpu.roll(a, SUB - 1, 0), 0.0) for a in state]
            for j in reversed(range(RUN)) if reverse else range(RUN):
                x = run_rows(xs, at, j)
                state = [decay[n] * state[n] + x for n in range(MODES)]
                mixed = total([weight[n] * state[n] for n in range(MODES)])
                out_ref[strip, blk, pl.ds(j, SUB, stride=RUN), :] = mixed
            return 0

        lax.fori_loop(0, BLOCKS, body, 0)
        leaving(strip).start()
        lead_refs[0][strip] = out_ref[strip, 0]
        lead_refs[1][strip] = out_ref[strip, HELD]
        return 0

    lax.fori_loop(0, STRIPS, strip_body, 0)
    for strip in range(STRIPS):
        leaving(strip).wait()
    for copy in leads:
        copy.wait()


def carry_kernel(where_ref, rates_ref, x_ref, y_hbm, y_ref, sem):
    place = where_ref[0]
    at = (place // (PAIRS * MODES)) * MODES + place % MODES
    log_decay = rates_ref[pl.ds(at, 1), :] / TOKENS
    across = jnp.exp(-log_decay * ROWS)
    zero = jnp.zeros((1, LANES), f32)

    def step(i, carried):
        a0, a1, b0, b1, cross, terms = carried
        y_ref[i, :, piece(0)] = a0
        y_ref[i, :, piece(1)] = a1
        cross = cross + (a0 * x_ref[i, :, piece(2)] + a1 * x_ref[i, :, piece(3)])
        terms = terms + x_ref[i, :, piece(4)]
        back = SHARDS - 1 - i
        y_ref[back, :, piece(2)] = b0
        y_ref[back, :, piece(3)] = b1
        return (
            across * a0 + x_ref[i, :, piece(0)],
            across * a1 + x_ref[i, :, piece(1)],
            across * b0 + x_ref[back, :, piece(2)],
            across * b1 + x_ref[back, :, piece(3)],
            cross,
            terms,
        )

    carried = lax.fori_loop(0, SHARDS, step, (zero,) * 6, unroll=8)
    row = jnp.exp(-log_decay) * carried[4] + carried[5]

    def fill(i, _):
        y_ref[i, :, piece(4)] = row
        return 0

    lax.fori_loop(0, SHARDS, fill, 0, unroll=16)
    copy = pltpu.make_async_copy(y_ref, y_hbm, sem)
    copy.start()
    copy.wait()


def finish_kernel(last, core_ref, tab, k_hbm, v_hbm, u_hbm, conv_hbm, flow_hbm, in_ref, *refs):
    gq_hbm, gk_hbm, gv_hbm, k_ref, v_ref, u_ref, conv_ref, flow_ref = refs[-13:-5]
    gq_ref, gk_ref, gv_ref, arrive_sems, sems = refs[-5:]
    second = core_ref[0] == 1
    if last:
        low, high = 0, jnp.where(second, HELD, BLOCKS)
    else:
        low, high = HELD, jnp.where(second, BLOCKS, HELD)

    def for_blocks(do, first=low):
        def body(blk, _):
            do(blk)
            return 0

        lax.fori_loop(first, high, body, 0)

    def arrivals(blk):
        cols = pl.ds(pl.multiple_of(blk * FILTERS, FILTERS), FILTERS)
        pairs = [
            (a.at[:, blk], b.at[:, blk]) for a, b in ((conv_hbm, conv_ref), (flow_hbm, flow_ref))
        ]
        for a, b in ((u_hbm, u_ref), (v_hbm, v_ref), (k_hbm, k_ref)):
            pairs.append((a.at[:, cols], b.at[:, cols]))
        return [
            pltpu.make_async_copy(a, b, arrive_sems.at[blk, i]) for i, (a, b) in enumerate(pairs)
        ]

    def fetch(blk):
        for copy in arrivals(blk):
            copy.start()

    for_blocks(fetch, low + 1)

    @pl.when(high > low)
    def _():
        lead_k, lead_v, lead_u, lead_conv, lead_flow = refs[:5]
        lead = pl.ds(low * FILTERS, FILTERS)
        for a, b in ((lead_k, k_ref), (lead_v, v_ref), (lead_u, u_ref)):
            b[:, lead] = a[...]
        for strip in range(STRIPS):
            conv_ref[strip, low] = lead_conv[strip]
            flow_ref[strip, low] = lead_flow[strip]

    def copies(blk):
        cols = pl.ds(pl.multiple_of(blk * FILTERS, FILTERS), FILTERS)
        return [
            pltpu.make_async_copy(src.at[:, cols], dst.at[:, cols], sems.at[blk, i])
            for i, (src, dst) in enumerate(((gq_ref, gq_hbm), (gk_ref, gk_hbm), (gv_ref, gv_hbm)))
        ]

    def block(blk):
        pair, odd = blk // 2, blk % 2

        @pl.when(blk > low)
        def _():
            for copy in arrivals(blk):
                copy.wait()

        def strip_body(strip, _):
            base = strip * MODES
            cols = lanes_of(blk * STRIPS + strip)
            leap = [tab[0, base + n] for n in range(MODES)]
            places = [owner(strip, pair, n) for n in range(MODES)]
            state = [
                tab[1, base + n] * in_ref[places[n], :, lanes_of(odd)] for n in range(MODES)
            ]
            for i in range(ROWS // 16):
                parts = []
                for _ in range(2):
                    parts.append(total(state))
                    state = [leap[n] * state[n] for n in range(MODES)]
                at = pl.ds(16 * i, 16)
                conv = conv_ref[strip, blk, at, :] + jnp.concatenate(parts, axis=0)
                gq_ref[at, cols] = (u_ref[at, cols].astype(f32) * conv).astype(bf16)
            state = [
                tab[2, base + n] * in_ref[places[n], :, lanes_of(2 + odd)] for n in range(MODES)
            ]
            for i in reversed(range(ROWS // 16)):
                parts = []
                for _ in range(2):
                    parts.insert(0, total(state))
                    state = [leap[n] * state[n] for n in range(MODES)]
                at = pl.ds(16 * i, 16)
                flow = flow_ref[strip, blk, at, :] + jnp.concatenate(parts, axis=0)
                gk_ref[at, cols] = (flow * v_ref[at, cols].astype(f32)).astype(bf16)
                gv_ref[at, cols] = (flow * k_ref[at, cols].astype(f32)).astype(bf16)
            return 0

        lax.fori_loop(0, STRIPS, strip_body, 0)
        for copy in copies(blk):
            copy.start()

    for_blocks(block)

    def drain(blk):
        for copy in copies(blk):
            copy.wait()

    for_blocks(drain)


def in_hbm(*arrays):
    return [pltpu.with_memory_space_constraint(a, pltpu.HBM) for a in arrays]


def local(query_rows, key_rows, value_rows, upstream, decay_rate, residue):
    half = lax.axis_index("fsdp")
    swap = [(0, 1), (1, 0)]
    first = lax.broadcasted_iota(jnp.int32, (2 * MODES, FILTERS // 2), 0) < MODES
    below, above = ((0, MODES, 0), (0, 0, 0)), ((MODES, 0, 0), (0, 0, 0))
    zero = jnp.zeros((), f32)
    mine = jnp.where(first, lax.pad(decay_rate, zero, below), lax.pad(residue, zero, above))
    other = lax.ppermute(mine, "fsdp", swap)
    vmem = pl.BlockSpec(memory_space=pltpu.VMEM)
    smem = pl.BlockSpec(memory_space=pltpu.SMEM)
    hbm = pl.BlockSpec(memory_space=pltpu.HBM)
    limit = pltpu.CompilerParams(vmem_limit_bytes=16 << 20)
    packet = (SHARDS, 1, PACKET)
    packets = pltpu.HBM(packet, f32)
    tiles = (STRIPS, BLOCKS, ROWS, LANES)
    state = (STRIPS, BLOCKS, MODES, SUB, LANES)
    params = (STRIPS * MODES, LANES)
    table = (STRIPS * MODES, SUB, LANES)
    whole = pltpu.VMEM((ROWS, WIDTH), bf16)
    query_rows, key_rows, value_rows, upstream = in_hbm(
        query_rows, key_rows, value_rows, upstream
    )
    ps, gs = pl.pallas_call(
        prepare_kernel,
        in_specs=[hbm] * 4,
        out_specs=[vmem] * 2,
        out_shape=[jax.ShapeDtypeStruct(tiles, f32)] * 2,
        scratch_shapes=[whole] * 4 + [pltpu.SemaphoreType.DMA((BLOCKS, 4))],
        compiler_params=limit,
        cost_estimate=pl.CostEstimate(flops=1 << 22, bytes_accessed=12 << 20, transcendentals=0),
        name="prepare",
    )(query_rows, key_rows, value_rows, upstream)
    send, enter_ahead, enter_behind, rates, residues, product, gated = pl.pallas_call(
        summarize_kernel,
        in_specs=[smem] + [vmem] * 4,
        out_specs=[hbm] * 7,
        out_shape=[packets]
        + [pltpu.HBM(state, f32)] * 2
        + [pltpu.HBM(params, f32)] * 2
        + [pltpu.HBM(tiles, f32)] * 2,
        scratch_shapes=[
            pltpu.VMEM((5,) + table, f32),
            pltpu.VMEM((HALF, SUB, LANES), f32),
            pltpu.VMEM((MODES, SUB, LANES), f32),
            pltpu.VMEM(packet, f32),
            pltpu.VMEM(state, f32),
            pltpu.VMEM(state, f32),
            pltpu.VMEM(params, f32),
            pltpu.VMEM(params, f32),
            pltpu.SemaphoreType.DMA((STRIPS, 3)),
            pltpu.SemaphoreType.DMA((4,)),
        ],
        compiler_params=limit,
        name="summarize",
    )(half.astype(jnp.int32).reshape(1), mine, other, ps, gs)
    arrived = lax.all_to_all(send, ALL, 0, 0, tiled=True)

    lead = jax.ShapeDtypeStruct((STRIPS, ROWS, LANES), f32)
    lead_rows = jax.ShapeDtypeStruct((ROWS, FILTERS), bf16)

    def inner(xs, enter, reverse, extra=(), more=()):
        return pl.pallas_call(
            functools.partial(inner_kernel, reverse),
            in_specs=[hbm] * (4 + len(extra)),
            out_specs=[hbm] + [vmem] * (2 + len(more)),
            out_shape=[pltpu.HBM(tiles, f32), lead, lead, *more],
            scratch_shapes=[
                pltpu.VMEM((5 if reverse else 2,) + table, f32),
                pltpu.VMEM(params, f32),
                pltpu.VMEM(params, f32),
                pltpu.VMEM(tiles, f32),
                pltpu.VMEM(state, f32),
                pltpu.VMEM(tiles, f32),
                pltpu.SemaphoreType.DMA((8,)),
                pltpu.SemaphoreType.DMA((STRIPS, 3)),
            ],
            compiler_params=limit,
            cost_estimate=pl.CostEstimate(
                flops=1 << 24, bytes_accessed=16 << 20, transcendentals=0
            ),
            name="behind" if reverse else "ahead",
        )(*in_hbm(rates, residues, xs, enter), *extra)

    late = jax.ShapeDtypeStruct((3,) + table, f32)
    conv, lead_conv, held_conv, late_tab, *rows_in = inner(
        product,
        enter_ahead,
        False,
        (key_rows, value_rows, upstream),
        (late,) + (lead_rows,) * 6,
    )
    arrived, conv = lax.optimization_barrier((arrived, conv))
    place = lax.axis_index(ALL).astype(jnp.int32).reshape(1)
    carries = pl.pallas_call(
        carry_kernel,
        in_specs=[smem] + [vmem] * 2,
        out_specs=hbm,
        out_shape=packets,
        scratch_shapes=[pltpu.VMEM(packet, f32), pltpu.SemaphoreType.DMA],
        compiler_params=limit,
        name="carry",
    )(place, rates, arrived)
    back = lax.all_to_all(carries, ALL, 0, 0, tiled=True)
    flowing, lead_flow, held_flow = inner(gated, enter_behind, True)
    back, flowing = lax.optimization_barrier((back, flowing))
    rows = back[:, 0, 4 * LANES :].reshape(STRIPS, PAIRS, MODES, LANES)
    count = STRIPS // 2
    rows = lax.dynamic_slice_in_dim(rows, half * count, count, 0).sum(axis=1)
    conv, flowing = in_hbm(conv, flowing)
    core = lax.axis_index("ch").astype(jnp.int32).reshape(1)
    shapes = [pltpu.HBM((ROWS, WIDTH), bf16)] * 3

    def finish(last, leads=(), before=()):
        count_in = 8 + len(leads)
        return pl.pallas_call(
            functools.partial(finish_kernel, last),
            in_specs=[smem, vmem]
            + [hbm] * 5
            + [vmem] * (1 + len(leads))
            + [hbm] * len(before),
            out_specs=[hbm] * 3,
            out_shape=shapes,
            input_output_aliases={count_in + i: i for i in range(len(before))},
            scratch_shapes=[
                whole,
                whole,
                whole,
                pltpu.VMEM(tiles, f32),
                pltpu.VMEM(tiles, f32),
                whole,
                whole,
                whole,
                pltpu.SemaphoreType.DMA((BLOCKS, 5)),
                pltpu.SemaphoreType.DMA((BLOCKS, 3)),
            ],
            compiler_params=limit,
            cost_estimate=pl.CostEstimate(
                flops=1 << 24, bytes_accessed=10 << 20, transcendentals=0
            ),
            name="finish" if last else "begin",
        )(
            core, late_tab, key_rows, value_rows, upstream, conv, flowing, back, *leads, *before
        )

    early = finish(False, (*rows_in[3:], held_conv, held_flow))
    own, *early = lax.optimization_barrier((rows, *early))
    rows = rows + lax.ppermute(own, "ch", swap)
    grads_out = finish(True, (*rows_in[:3], lead_conv, lead_flow), early)
    rows = rows.transpose(1, 0, 2).reshape(MODES, count * LANES)
    gain = jnp.sqrt((1.0 + decay_rate) / TOKENS)
    residue_grad = gain * rows / math.sqrt(TOKENS)
    return (*grads_out, residue_grad)


def solution(mesh):
    rows = P(ALL, "ch")
    params = P(None, "fsdp")
    return jax.shard_map(
        local,
        mesh=mesh,
        in_specs=(rows, rows, rows, rows, params, params),
        out_specs=(rows, rows, rows, params),
        check_vma=False,
    )
```

```python
import functools
import math

import jax
import jax.numpy as jnp
from jax import lax
from jax.experimental import pallas as pl
from jax.experimental.pallas import tpu as pltpu
from jax.sharding import PartitionSpec as P

TOKENS = 16384
ROWS = 128
MODES = 8
FILTERS = 512
BLOCKS = 8
SUB = 8
RUN = ROWS // SUB
HALF = RUN // 2
LANES = 128
STRIPS = FILTERS // LANES
PAIRS = BLOCKS // 2
WIDTH = BLOCKS * FILTERS
SHARDS = TOKENS // ROWS
PACKET = 5 * LANES
HELD = 3
ALL = ("ctx", "fsdp")
f32 = jnp.float32
bf16 = jnp.bfloat16


def sublane():
    return lax.broadcasted_iota(jnp.int32, (SUB, LANES), 0)


def owner(strip, pair, n):
    return (strip * PAIRS + pair) * MODES + n


def lanes_of(at):
    return pl.ds(pl.multiple_of(at * LANES, LANES), LANES)


def piece(r):
    return pl.ds(r * LANES, LANES)


def spread(ref, at, natural):
    half = RUN // SUB
    for r in range(ROWS // SUB):
        start = (r % half) * SUB * SUB + r // half
        ref[(*at, pl.ds(start, SUB, stride=SUB))] = natural[SUB * r : SUB * (r + 1), :]


def run_rows(ref, at, j):
    return ref[(*at, pl.ds(SUB * j, SUB))]


def for_filters(make):
    def body(i, _):
        make(i)
        return 0

    lax.fori_loop(0, STRIPS * MODES, body, 0)


def row_of(ref, i):
    return jnp.broadcast_to(ref[pl.ds(i, 1), :], (SUB, LANES))


def total(parts):
    while len(parts) > 1:
        parts = [a + b for a, b in zip(parts[::2], parts[1::2])]
    return parts[0]


def prepare_kernel(q_hbm, k_hbm, v_hbm, u_hbm, ps, gs, q_ref, k_ref, v_ref, u_ref, sems):
    def copies(blk):
        cols = pl.ds(blk * FILTERS, FILTERS)
        return [
            pltpu.make_async_copy(src.at[:, cols], dst.at[:, cols], sems.at[blk, i])
            for i, (src, dst) in enumerate(
                ((k_hbm, k_ref), (v_hbm, v_ref), (u_hbm, u_ref), (q_hbm, q_ref))
            )
        ]

    for blk in range(BLOCKS):
        for copy in copies(blk):
            copy.start()
    for blk in range(BLOCKS):
        for copy in copies(blk):
            copy.wait()

        def strip_body(strip, _):
            at = (strip, blk)
            cols = lanes_of(blk * STRIPS + strip)
            spread(ps, at, k_ref[:, cols].astype(f32) * v_ref[:, cols].astype(f32))
            spread(gs, at, u_ref[:, cols].astype(f32) * q_ref[:, cols].astype(f32))
            return 0

        lax.fori_loop(0, STRIPS, strip_body, 0)


def summarize_kernel(
    mine_ref, other_ref, ps, gs,
    send_hbm, cf_hbm, cb_hbm, rates_hbm, residues_hbm, ps_hbm, gs_hbm,
    tab, lags, joins, send_ref, cf_ref, cb_ref, rates_ref, residues_ref, sems, early_sems,
):
    s = sublane()
    lower = jnp.broadcast_to(lax.axis_index("fsdp"), (MODES, LANES)) == 0
    for strip in range(STRIPS):
        cols = pl.ds((strip % 2) * LANES, LANES)
        at = pl.ds(strip * MODES, MODES)
        for part, out in enumerate((rates_ref, residues_ref)):
            rows = pl.ds(part * MODES, MODES)
            here, there = mine_ref[rows, cols], other_ref[rows, cols]
            if strip < STRIPS // 2:
                out[at, :] = jnp.where(lower, here, there)
            else:
                out[at, :] = jnp.where(lower, there, here)

    stored = [
        pltpu.make_async_copy(a, b, early_sems.at[i])
        for i, (a, b) in enumerate(
            ((rates_ref, rates_hbm), (residues_ref, residues_hbm), (ps, ps_hbm), (gs, gs_hbm))
        )
    ]
    for copy in stored:
        copy.start()

    def make(i):
        log_decay = row_of(rates_ref, i) / TOKENS
        tab[0, i] = jnp.exp(-log_decay)
        for step in range(3):
            hop = 1 << step
            factor = jnp.exp(-log_decay * (RUN * hop))
            tab[1 + step, i] = jnp.where(s >= hop, factor, 0.0)
        tab[4, i] = jnp.exp(-log_decay * (RUN * s).astype(f32))

    for_filters(make)

    def sent(strip):
        at = pl.ds(strip * PAIRS * MODES, PAIRS * MODES)
        return [
            pltpu.make_async_copy(send_ref.at[at], send_hbm.at[at], sems.at[strip, 0]),
            pltpu.make_async_copy(cf_ref.at[strip], cf_hbm.at[strip], sems.at[strip, 1]),
            pltpu.make_async_copy(cb_ref.at[strip], cb_hbm.at[strip], sems.at[strip, 2]),
        ]

    def strip_body(strip, _):
        base = strip * MODES

        for lag in range(HALF):
            lags[lag] = jnp.zeros((SUB, LANES), f32)
        for n in range(MODES):
            joins[n] = jnp.zeros((SUB, LANES), f32)

        def pair_body(pair, _):
            for odd in range(2):
                at = (strip, 2 * pair + odd)
                decay = [tab[0, base + n] for n in range(MODES)]
                behind, middle = [None] * MODES, [None] * MODES
                for j in reversed(range(RUN)):
                    gated = run_rows(gs, at, j)
                    for n in range(MODES):
                        behind[n] = gated if j == RUN - 1 else decay[n] * behind[n] + gated
                    if j == HALF:
                        middle = list(behind)
                ahead, joint = [None] * MODES, [None] * MODES
                for j in range(RUN):
                    product = run_rows(ps, at, j)
                    for n in range(MODES):
                        ahead[n] = product if j == 0 else decay[n] * ahead[n] + product
                        if j == HALF - 1:
                            joint[n] = ahead[n] * middle[n]
                for lag in range(HALF):
                    starts = [j for j in range(RUN) if j // HALF == (j + lag) // HALF]
                    pairs = [run_rows(gs, at, j + lag) * run_rows(ps, at, j) for j in starts]
                    while len(pairs) > 1:
                        odd_one = pairs[-1:] if len(pairs) % 2 else []
                        pairs = [a + b for a, b in zip(pairs[::2], pairs[1::2])] + odd_one
                    lags[lag] = lags[lag] + pairs[0]
                for step in range(3):
                    for n in range(MODES):
                        moved = pltpu.roll(ahead[n], 1 << step, 0)
                        ahead[n] = ahead[n] + tab[1 + step, base + n] * moved
                for n in range(MODES):
                    place = owner(strip, pair, n)
                    send_ref[place, :, piece(odd)] = ahead[n][SUB - 1 :, :]
                    first = jnp.sum(tab[4, base + n] * behind[n], axis=0, keepdims=True)
                    send_ref[place, :, piece(2 + odd)] = first
                    enter = jnp.where(s >= 1, pltpu.roll(ahead[n], 1, 0), 0.0)
                    cf_ref[strip, 2 * pair + odd, n] = enter
                    cb_ref[strip, 2 * pair + odd, n] = behind[n]
                    joins[n] = joins[n] + (joint[n] + behind[n] * enter)
            return 0

        lax.fori_loop(0, PAIRS, pair_body, 0)
        for n in range(MODES):
            decay = tab[0, base + n]
            term = lags[HALF - 1]
            for lag in reversed(range(HALF - 1)):
                term = decay * term + lags[lag]
            term = jnp.sum(term + decay * joins[n], axis=0, keepdims=True)
            for pair in range(PAIRS):
                row = term if pair == 0 else jnp.zeros((1, LANES), f32)
                send_ref[owner(strip, pair, n), :, piece(4)] = row
        for copy in sent(strip):
            copy.start()
        return 0

    lax.fori_loop(0, STRIPS, strip_body, 0)
    for strip in range(STRIPS):
        for copy in sent(strip):
            copy.wait()
    for copy in stored:
        copy.wait()


def inner_kernel(reverse, rates_hbm, residues_hbm, xs_hbm, enter_hbm, *refs):
    if reverse:
        out_hbm, *lead_refs = refs[:3]
    else:
        rows_hbm, out_hbm, lead_refs, late_tab = refs[:3], refs[3], refs[4:6], refs[6]
        lead_rows = refs[7:13]
    tab, rates_ref, residues_ref, xs, enter_ref, out_ref, param_sems, sems = refs[-8:]
    params = [
        pltpu.make_async_copy(rates_hbm, rates_ref, param_sems.at[0]),
        pltpu.make_async_copy(residues_hbm, residues_ref, param_sems.at[1]),
    ]

    def arrivals(strip):
        return [
            pltpu.make_async_copy(enter_hbm.at[strip], enter_ref.at[strip], sems.at[strip, 0]),
            pltpu.make_async_copy(xs_hbm.at[strip], xs.at[strip], sems.at[strip, 1]),
        ]

    def leaving(strip):
        return pltpu.make_async_copy(out_ref.at[strip], out_hbm.at[strip], sems.at[strip, 2])

    s = sublane()
    leads = []
    if not reverse:
        for i, b in enumerate(lead_rows):
            source = rows_hbm[i % 3].at[:, pl.ds((i // 3) * HELD * FILTERS, FILTERS)]
            leads.append(pltpu.make_async_copy(source, b, param_sems.at[2 + i]))
    for copy in params:
        copy.start()
    for strip in range(STRIPS):
        for copy in arrivals(strip):
            copy.start()
    for copy in leads:
        copy.start()
    for copy in params:
        copy.wait()

    def make(i):
        rate = row_of(rates_ref, i)
        tab[0, i] = jnp.exp(-rate / TOKENS)
        tab[1, i] = row_of(residues_ref, i) * jnp.sqrt((1.0 + rate) / TOKENS)
        if not reverse:
            weight = tab[1, i]
            late_tab[0, i] = jnp.exp(-rate / TOKENS * SUB)
            late_tab[1, i] = weight * jnp.exp(-rate / TOKENS * (s + 1).astype(f32))
            late_tab[2, i] = weight * jnp.exp(-rate / TOKENS * (SUB - s).astype(f32))
        for step in range(3 if reverse else 0):
            factor = jnp.exp(-rate / TOKENS * (RUN << step))
            tab[2 + step, i] = jnp.where(s < SUB - (1 << step), factor, 0.0)

    for_filters(make)

    def strip_body(strip, _):
        for copy in arrivals(strip):
            copy.wait()
        base = strip * MODES

        def body(blk, _):
            at = (strip, blk)
            decay = [tab[0, base + n] for n in range(MODES)]
            weight = [tab[1, base + n] for n in range(MODES)]
            state = [enter_ref[strip, blk, n] for n in range(MODES)]
            if reverse:
                for step in range(3):
                    for n in range(MODES):
                        moved = pltpu.roll(state[n], SUB - (1 << step), 0)
                        state[n] = state[n] + tab[2 + step, base + n] * moved
                state = [jnp.where(s < SUB - 1, pltpu.roll(a, SUB - 1, 0), 0.0) for a in state]
            for j in reversed(range(RUN)) if reverse else range(RUN):
                x = run_rows(xs, at, j)
                state = [decay[n] * state[n] + x for n in range(MODES)]
                mixed = total([weight[n] * state[n] for n in range(MODES)])
                out_ref[strip, blk, pl.ds(j, SUB, stride=RUN), :] = mixed
            return 0

        lax.fori_loop(0, BLOCKS, body, 0)
        leaving(strip).start()
        lead_refs[0][strip] = out_ref[strip, 0]
        lead_refs[1][strip] = out_ref[strip, HELD]
        return 0

    lax.fori_loop(0, STRIPS, strip_body, 0)
    for strip in range(STRIPS):
        leaving(strip).wait()
    for copy in leads:
        copy.wait()


def carry_kernel(rates_ref, x_ref, y_hbm, y_ref, sem):
    place = lax.axis_index("ctx") * 2 + lax.axis_index("fsdp")
    at = (place // (PAIRS * MODES)) * MODES + place % MODES
    log_decay = rates_ref[pl.ds(at, 1), :] / TOKENS
    across = jnp.exp(-log_decay * ROWS)
    zero = jnp.zeros((1, LANES), f32)

    def step(i, carried):
        a0, a1, b0, b1, cross, terms = carried
        y_ref[i, :, piece(0)] = a0
        y_ref[i, :, piece(1)] = a1
        cross = cross + (a0 * x_ref[i, :, piece(2)] + a1 * x_ref[i, :, piece(3)])
        terms = terms + x_ref[i, :, piece(4)]
        back = SHARDS - 1 - i
        y_ref[back, :, piece(2)] = b0
        y_ref[back, :, piece(3)] = b1
        return (
            across * a0 + x_ref[i, :, piece(0)],
            across * a1 + x_ref[i, :, piece(1)],
            across * b0 + x_ref[back, :, piece(2)],
            across * b1 + x_ref[back, :, piece(3)],
            cross,
            terms,
        )

    carried = lax.fori_loop(0, SHARDS, step, (zero,) * 6, unroll=8)
    row = jnp.exp(-log_decay) * carried[4] + carried[5]

    def fill(i, _):
        y_ref[i, :, piece(4)] = row
        return 0

    lax.fori_loop(0, SHARDS, fill, 0, unroll=16)
    copy = pltpu.make_async_copy(y_ref, y_hbm, sem)
    copy.start()
    copy.wait()


def finish_kernel(last, tab, k_hbm, v_hbm, u_hbm, conv_hbm, flow_hbm, in_ref, *refs):
    gq_hbm, gk_hbm, gv_hbm, k_ref, v_ref, u_ref, conv_ref, flow_ref = refs[-13:-5]
    gq_ref, gk_ref, gv_ref, arrive_sems, sems = refs[-5:]
    second = lax.axis_index("ch") == 1
    if last:
        low, high = 0, jnp.where(second, HELD, BLOCKS)
    else:
        low, high = HELD, jnp.where(second, BLOCKS, HELD)

    def for_blocks(do, first=low):
        def body(blk, _):
            do(blk)
            return 0

        lax.fori_loop(first, high, body, 0)

    def arrivals(blk):
        cols = pl.ds(pl.multiple_of(blk * FILTERS, FILTERS), FILTERS)
        pairs = [
            (a.at[:, blk], b.at[:, blk]) for a, b in ((conv_hbm, conv_ref), (flow_hbm, flow_ref))
        ]
        for a, b in ((u_hbm, u_ref), (v_hbm, v_ref), (k_hbm, k_ref)):
            pairs.append((a.at[:, cols], b.at[:, cols]))
        return [
            pltpu.make_async_copy(a, b, arrive_sems.at[blk, i]) for i, (a, b) in enumerate(pairs)
        ]

    def fetch(blk):
        for copy in arrivals(blk):
            copy.start()

    for_blocks(fetch, low + 1)

    @pl.when(high > low)
    def _():
        lead_k, lead_v, lead_u, lead_conv, lead_flow = refs[:5]
        lead = pl.ds(low * FILTERS, FILTERS)
        for a, b in ((lead_k, k_ref), (lead_v, v_ref), (lead_u, u_ref)):
            b[:, lead] = a[...]
        for strip in range(STRIPS):
            conv_ref[strip, low] = lead_conv[strip]
            flow_ref[strip, low] = lead_flow[strip]

    def copies(blk):
        cols = pl.ds(pl.multiple_of(blk * FILTERS, FILTERS), FILTERS)
        return [
            pltpu.make_async_copy(src.at[:, cols], dst.at[:, cols], sems.at[blk, i])
            for i, (src, dst) in enumerate(((gq_ref, gq_hbm), (gk_ref, gk_hbm), (gv_ref, gv_hbm)))
        ]

    def block(blk):
        pair, odd = blk // 2, blk % 2

        @pl.when(blk > low)
        def _():
            for copy in arrivals(blk):
                copy.wait()

        def strip_body(strip, _):
            base = strip * MODES
            cols = lanes_of(blk * STRIPS + strip)
            leap = [tab[0, base + n] for n in range(MODES)]
            places = [owner(strip, pair, n) for n in range(MODES)]
            state = [
                tab[1, base + n] * in_ref[places[n], :, lanes_of(odd)] for n in range(MODES)
            ]
            for i in range(ROWS // 16):
                parts = []
                for _ in range(2):
                    parts.append(total(state))
                    state = [leap[n] * state[n] for n in range(MODES)]
                at = pl.ds(16 * i, 16)
                conv = conv_ref[strip, blk, at, :] + jnp.concatenate(parts, axis=0)
                gq_ref[at, cols] = (u_ref[at, cols].astype(f32) * conv).astype(bf16)
            state = [
                tab[2, base + n] * in_ref[places[n], :, lanes_of(2 + odd)] for n in range(MODES)
            ]
            for i in reversed(range(ROWS // 16)):
                parts = []
                for _ in range(2):
                    parts.insert(0, total(state))
                    state = [leap[n] * state[n] for n in range(MODES)]
                at = pl.ds(16 * i, 16)
                flow = flow_ref[strip, blk, at, :] + jnp.concatenate(parts, axis=0)
                gk_ref[at, cols] = (flow * v_ref[at, cols].astype(f32)).astype(bf16)
                gv_ref[at, cols] = (flow * k_ref[at, cols].astype(f32)).astype(bf16)
            return 0

        lax.fori_loop(0, STRIPS, strip_body, 0)
        for copy in copies(blk):
            copy.start()

    for_blocks(block)

    def drain(blk):
        for copy in copies(blk):
            copy.wait()

    for_blocks(drain)


def in_hbm(*arrays):
    return [pltpu.with_memory_space_constraint(a, pltpu.HBM) for a in arrays]


def local(query_rows, key_rows, value_rows, upstream, decay_rate, residue):
    half = lax.axis_index("fsdp")
    swap = [(0, 1), (1, 0)]
    first = lax.broadcasted_iota(jnp.int32, (2 * MODES, FILTERS // 2), 0) < MODES
    below, above = ((0, MODES, 0), (0, 0, 0)), ((MODES, 0, 0), (0, 0, 0))
    zero = jnp.zeros((), f32)
    mine = jnp.where(first, lax.pad(decay_rate, zero, below), lax.pad(residue, zero, above))
    other = lax.ppermute(mine, "fsdp", swap)
    vmem = pl.BlockSpec(memory_space=pltpu.VMEM)
    hbm = pl.BlockSpec(memory_space=pltpu.HBM)
    limit = pltpu.CompilerParams(vmem_limit_bytes=16 << 20)
    packet = (SHARDS, 1, PACKET)
    packets = pltpu.HBM(packet, f32)
    tiles = (STRIPS, BLOCKS, ROWS, LANES)
    state = (STRIPS, BLOCKS, MODES, SUB, LANES)
    params = (STRIPS * MODES, LANES)
    table = (STRIPS * MODES, SUB, LANES)
    whole = pltpu.VMEM((ROWS, WIDTH), bf16)
    query_rows, key_rows, value_rows, upstream = in_hbm(
        query_rows, key_rows, value_rows, upstream
    )
    ps, gs = pl.pallas_call(
        prepare_kernel,
        in_specs=[hbm] * 4,
        out_specs=[vmem] * 2,
        out_shape=[jax.ShapeDtypeStruct(tiles, f32)] * 2,
        scratch_shapes=[whole] * 4 + [pltpu.SemaphoreType.DMA((BLOCKS, 4))],
        compiler_params=limit,
        cost_estimate=pl.CostEstimate(flops=1 << 22, bytes_accessed=12 << 20, transcendentals=0),
        name="prepare",
    )(query_rows, key_rows, value_rows, upstream)
    send, enter_ahead, enter_behind, rates, residues, product, gated = pl.pallas_call(
        summarize_kernel,
        in_specs=[vmem] * 4,
        out_specs=[hbm] * 7,
        out_shape=[packets]
        + [pltpu.HBM(state, f32)] * 2
        + [pltpu.HBM(params, f32)] * 2
        + [pltpu.HBM(tiles, f32)] * 2,
        scratch_shapes=[
            pltpu.VMEM((5,) + table, f32),
            pltpu.VMEM((HALF, SUB, LANES), f32),
            pltpu.VMEM((MODES, SUB, LANES), f32),
            pltpu.VMEM(packet, f32),
            pltpu.VMEM(state, f32),
            pltpu.VMEM(state, f32),
            pltpu.VMEM(params, f32),
            pltpu.VMEM(params, f32),
            pltpu.SemaphoreType.DMA((STRIPS, 3)),
            pltpu.SemaphoreType.DMA((4,)),
        ],
        compiler_params=limit,
        name="summarize",
    )(mine, other, ps, gs)
    arrived = lax.all_to_all(send, ALL, 0, 0, tiled=True)

    lead = jax.ShapeDtypeStruct((STRIPS, ROWS, LANES), f32)
    lead_rows = jax.ShapeDtypeStruct((ROWS, FILTERS), bf16)

    def inner(xs, enter, reverse, extra=(), more=()):
        return pl.pallas_call(
            functools.partial(inner_kernel, reverse),
            in_specs=[hbm] * (4 + len(extra)),
            out_specs=[hbm] + [vmem] * (2 + len(more)),
            out_shape=[pltpu.HBM(tiles, f32), lead, lead, *more],
            scratch_shapes=[
                pltpu.VMEM((5 if reverse else 2,) + table, f32),
                pltpu.VMEM(params, f32),
                pltpu.VMEM(params, f32),
                pltpu.VMEM(tiles, f32),
                pltpu.VMEM(state, f32),
                pltpu.VMEM(tiles, f32),
                pltpu.SemaphoreType.DMA((8,)),
                pltpu.SemaphoreType.DMA((STRIPS, 3)),
            ],
            compiler_params=limit,
            cost_estimate=pl.CostEstimate(
                flops=1 << 24, bytes_accessed=16 << 20, transcendentals=0
            ),
            name="behind" if reverse else "ahead",
        )(*in_hbm(rates, residues, xs, enter), *extra)

    late = jax.ShapeDtypeStruct((3,) + table, f32)
    conv, lead_conv, held_conv, late_tab, *rows_in = inner(
        product,
        enter_ahead,
        False,
        (key_rows, value_rows, upstream),
        (late,) + (lead_rows,) * 6,
    )
    arrived, conv = lax.optimization_barrier((arrived, conv))
    carries = pl.pallas_call(
        carry_kernel,
        in_specs=[vmem] * 2,
        out_specs=hbm,
        out_shape=packets,
        scratch_shapes=[pltpu.VMEM(packet, f32), pltpu.SemaphoreType.DMA],
        compiler_params=limit,
        name="carry",
    )(rates, arrived)
    back = lax.all_to_all(carries, ALL, 0, 0, tiled=True)
    flowing, lead_flow, held_flow = inner(gated, enter_behind, True)
    back, flowing = lax.optimization_barrier((back, flowing))
    rows = back[:, 0, 4 * LANES :].reshape(STRIPS, PAIRS, MODES, LANES)
    count = STRIPS // 2
    rows = lax.dynamic_slice_in_dim(rows, half * count, count, 0).sum(axis=1)
    conv, flowing = in_hbm(conv, flowing)
    shapes = [pltpu.HBM((ROWS, WIDTH), bf16)] * 3

    def finish(last, leads=(), before=()):
        count_in = 7 + len(leads)
        return pl.pallas_call(
            functools.partial(finish_kernel, last),
            in_specs=[vmem]
            + [hbm] * 5
            + [vmem] * (1 + len(leads))
            + [hbm] * len(before),
            out_specs=[hbm] * 3,
            out_shape=shapes,
            input_output_aliases={count_in + i: i for i in range(len(before))},
            scratch_shapes=[
                whole,
                whole,
                whole,
                pltpu.VMEM(tiles, f32),
                pltpu.VMEM(tiles, f32),
                whole,
                whole,
                whole,
                pltpu.SemaphoreType.DMA((BLOCKS, 5)),
                pltpu.SemaphoreType.DMA((BLOCKS, 3)),
            ],
            compiler_params=limit,
            cost_estimate=pl.CostEstimate(
                flops=1 << 24, bytes_accessed=10 << 20, transcendentals=0
            ),
            name="finish" if last else "begin",
        )(
            late_tab, key_rows, value_rows, upstream, conv, flowing, back, *leads, *before
        )

    early = finish(False, (*rows_in[3:], held_conv, held_flow))
    own, *early = lax.optimization_barrier((rows, *early))
    rows = rows + lax.ppermute(own, "ch", swap)
    grads_out = finish(True, (*rows_in[:3], lead_conv, lead_flow), early)
    rows = rows.transpose(1, 0, 2).reshape(MODES, count * LANES)
    gain = jnp.sqrt((1.0 + decay_rate) / TOKENS)
    residue_grad = gain * rows / math.sqrt(TOKENS)
    return (*grads_out, residue_grad)


def solution(mesh):
    rows = P(ALL, "ch")
    params = P(None, "fsdp")
    return jax.shard_map(
        local,
        mesh=mesh,
        in_specs=(rows, rows, rows, rows, params, params),
        out_specs=(rows, rows, rows, params),
        check_vma=False,
    )
```

```python
import functools
import math

import jax
import jax.numpy as jnp
from jax import lax
from jax.experimental import pallas as pl
from jax.experimental.pallas import tpu as pltpu
from jax.sharding import PartitionSpec as P

TOKENS = 16384
ROWS = 128
MODES = 8
FILTERS = 512
BLOCKS = 8
SUB = 8
RUN = ROWS // SUB
HALF = RUN // 2
LANES = 128
STRIPS = FILTERS // LANES
PAIRS = BLOCKS // 2
WIDTH = BLOCKS * FILTERS
SHARDS = TOKENS // ROWS
PACKET = 5 * LANES
HELD = 4
ALL = ("ctx", "fsdp")
f32 = jnp.float32
bf16 = jnp.bfloat16


def sublane():
    return lax.broadcasted_iota(jnp.int32, (SUB, LANES), 0)


def owner(strip, pair, n):
    return (strip * PAIRS + pair) * MODES + n


def lanes_of(at):
    return pl.ds(pl.multiple_of(at * LANES, LANES), LANES)


def piece(r):
    return pl.ds(r * LANES, LANES)


def spread(ref, at, natural):
    half = RUN // SUB
    for r in range(ROWS // SUB):
        start = (r % half) * SUB * SUB + r // half
        ref[(*at, pl.ds(start, SUB, stride=SUB))] = natural[SUB * r : SUB * (r + 1), :]


def run_rows(ref, at, j):
    return ref[(*at, pl.ds(SUB * j, SUB))]


def for_filters(make):
    def body(i, _):
        make(i)
        return 0

    lax.fori_loop(0, STRIPS * MODES, body, 0)


def row_of(ref, i):
    return jnp.broadcast_to(ref[pl.ds(i, 1), :], (SUB, LANES))


def total(parts):
    while len(parts) > 1:
        parts = [a + b for a, b in zip(parts[::2], parts[1::2])]
    return parts[0]


def prepare_kernel(q_hbm, k_hbm, v_hbm, u_hbm, ps, gs, q_ref, k_ref, v_ref, u_ref, sems):
    def copies(blk):
        cols = pl.ds(blk * FILTERS, FILTERS)
        return [
            pltpu.make_async_copy(src.at[:, cols], dst.at[:, cols], sems.at[blk, i])
            for i, (src, dst) in enumerate(
                ((k_hbm, k_ref), (v_hbm, v_ref), (u_hbm, u_ref), (q_hbm, q_ref))
            )
        ]

    for blk in range(BLOCKS):
        for copy in copies(blk):
            copy.start()
    for blk in range(BLOCKS):
        for copy in copies(blk):
            copy.wait()

        def strip_body(strip, _):
            at = (strip, blk)
            cols = lanes_of(blk * STRIPS + strip)
            spread(ps, at, k_ref[:, cols].astype(f32) * v_ref[:, cols].astype(f32))
            spread(gs, at, u_ref[:, cols].astype(f32) * q_ref[:, cols].astype(f32))
            return 0

        lax.fori_loop(0, STRIPS, strip_body, 0)


def summarize_kernel(
    half_ref, mine_ref, other_ref, ps, gs,
    send_hbm, cf_hbm, cb_hbm, rates_hbm, residues_hbm, ps_hbm, gs_hbm,
    tab, lags, joins, send_ref, cf_ref, cb_ref, rates_ref, residues_ref, sems, early_sems,
):
    s = sublane()
    lower = jnp.broadcast_to(half_ref[0], (MODES, LANES)) == 0
    for strip in range(STRIPS):
        cols = pl.ds((strip % 2) * LANES, LANES)
        at = pl.ds(strip * MODES, MODES)
        for part, out in enumerate((rates_ref, residues_ref)):
            rows = pl.ds(part * MODES, MODES)
            here, there = mine_ref[rows, cols], other_ref[rows, cols]
            if strip < STRIPS // 2:
                out[at, :] = jnp.where(lower, here, there)
            else:
                out[at, :] = jnp.where(lower, there, here)

    stored = [
        pltpu.make_async_copy(a, b, early_sems.at[i])
        for i, (a, b) in enumerate(
            ((rates_ref, rates_hbm), (residues_ref, residues_hbm), (ps, ps_hbm), (gs, gs_hbm))
        )
    ]
    for copy in stored:
        copy.start()

    def make(i):
        log_decay = row_of(rates_ref, i) / TOKENS
        tab[0, i] = jnp.exp(-log_decay)
        for step in range(3):
            hop = 1 << step
            factor = jnp.exp(-log_decay * (RUN * hop))
            tab[1 + step, i] = jnp.where(s >= hop, factor, 0.0)
        tab[4, i] = jnp.exp(-log_decay * (RUN * s).astype(f32))

    for_filters(make)

    def sent(strip):
        at = pl.ds(strip * PAIRS * MODES, PAIRS * MODES)
        return [
            pltpu.make_async_copy(send_ref.at[at], send_hbm.at[at], sems.at[strip, 0]),
            pltpu.make_async_copy(cf_ref.at[strip], cf_hbm.at[strip], sems.at[strip, 1]),
            pltpu.make_async_copy(cb_ref.at[strip], cb_hbm.at[strip], sems.at[strip, 2]),
        ]

    def strip_body(strip, _):
        base = strip * MODES

        for lag in range(HALF):
            lags[lag] = jnp.zeros((SUB, LANES), f32)
        for n in range(MODES):
            joins[n] = jnp.zeros((SUB, LANES), f32)

        def pair_body(pair, _):
            for odd in range(2):
                at = (strip, 2 * pair + odd)
                decay = [tab[0, base + n] for n in range(MODES)]
                behind, middle = [None] * MODES, [None] * MODES
                for j in reversed(range(RUN)):
                    gated = run_rows(gs, at, j)
                    for n in range(MODES):
                        behind[n] = gated if j == RUN - 1 else decay[n] * behind[n] + gated
                    if j == HALF:
                        middle = list(behind)
                ahead, joint = [None] * MODES, [None] * MODES
                for j in range(RUN):
                    product = run_rows(ps, at, j)
                    for n in range(MODES):
                        ahead[n] = product if j == 0 else decay[n] * ahead[n] + product
                        if j == HALF - 1:
                            joint[n] = ahead[n] * middle[n]
                for lag in range(HALF):
                    starts = [j for j in range(RUN) if j // HALF == (j + lag) // HALF]
                    pairs = [run_rows(gs, at, j + lag) * run_rows(ps, at, j) for j in starts]
                    while len(pairs) > 1:
                        odd_one = pairs[-1:] if len(pairs) % 2 else []
                        pairs = [a + b for a, b in zip(pairs[::2], pairs[1::2])] + odd_one
                    lags[lag] = lags[lag] + pairs[0]
                for step in range(3):
                    for n in range(MODES):
                        moved = pltpu.roll(ahead[n], 1 << step, 0)
                        ahead[n] = ahead[n] + tab[1 + step, base + n] * moved
                for n in range(MODES):
                    place = owner(strip, pair, n)
                    send_ref[place, :, piece(odd)] = ahead[n][SUB - 1 :, :]
                    first = jnp.sum(tab[4, base + n] * behind[n], axis=0, keepdims=True)
                    send_ref[place, :, piece(2 + odd)] = first
                    enter = jnp.where(s >= 1, pltpu.roll(ahead[n], 1, 0), 0.0)
                    cf_ref[strip, 2 * pair + odd, n] = enter
                    cb_ref[strip, 2 * pair + odd, n] = behind[n]
                    joins[n] = joins[n] + (joint[n] + behind[n] * enter)
            return 0

        lax.fori_loop(0, PAIRS, pair_body, 0)
        for n in range(MODES):
            decay = tab[0, base + n]
            term = lags[HALF - 1]
            for lag in reversed(range(HALF - 1)):
                term = decay * term + lags[lag]
            term = jnp.sum(term + decay * joins[n], axis=0, keepdims=True)
            for pair in range(PAIRS):
                row = term if pair == 0 else jnp.zeros((1, LANES), f32)
                send_ref[owner(strip, pair, n), :, piece(4)] = row
        for copy in sent(strip):
            copy.start()
        return 0

    lax.fori_loop(0, STRIPS, strip_body, 0)
    for strip in range(STRIPS):
        for copy in sent(strip):
            copy.wait()
    for copy in stored:
        copy.wait()


def inner_kernel(reverse, rates_hbm, residues_hbm, xs_hbm, enter_hbm, *refs):
    if reverse:
        out_hbm, *lead_refs = refs[:3]
    else:
        rows_hbm, out_hbm, lead_refs, late_tab = refs[:3], refs[3], refs[4:6], refs[6]
        lead_rows = refs[7:13]
    tab, rates_ref, residues_ref, xs, enter_ref, out_ref, param_sems, sems = refs[-8:]
    params = [
        pltpu.make_async_copy(rates_hbm, rates_ref, param_sems.at[0]),
        pltpu.make_async_copy(residues_hbm, residues_ref, param_sems.at[1]),
    ]

    def arrivals(strip):
        return [
            pltpu.make_async_copy(enter_hbm.at[strip], enter_ref.at[strip], sems.at[strip, 0]),
            pltpu.make_async_copy(xs_hbm.at[strip], xs.at[strip], sems.at[strip, 1]),
        ]

    def leaving(strip):
        return pltpu.make_async_copy(out_ref.at[strip], out_hbm.at[strip], sems.at[strip, 2])

    s = sublane()
    leads = []
    if not reverse:
        for i, b in enumerate(lead_rows):
            source = rows_hbm[i % 3].at[:, pl.ds((i // 3) * HELD * FILTERS, FILTERS)]
            leads.append(pltpu.make_async_copy(source, b, param_sems.at[2 + i]))
    for copy in params:
        copy.start()
    for strip in range(STRIPS):
        for copy in arrivals(strip):
            copy.start()
    for copy in leads:
        copy.start()
    for copy in params:
        copy.wait()

    def make(i):
        rate = row_of(rates_ref, i)
        tab[0, i] = jnp.exp(-rate / TOKENS)
        tab[1, i] = row_of(residues_ref, i) * jnp.sqrt((1.0 + rate) / TOKENS)
        if not reverse:
            weight = tab[1, i]
            late_tab[0, i] = jnp.exp(-rate / TOKENS * SUB)
            late_tab[1, i] = weight * jnp.exp(-rate / TOKENS * (s + 1).astype(f32))
            late_tab[2, i] = weight * jnp.exp(-rate / TOKENS * (SUB - s).astype(f32))
        for step in range(3 if reverse else 0):
            factor = jnp.exp(-rate / TOKENS * (RUN << step))
            tab[2 + step, i] = jnp.where(s < SUB - (1 << step), factor, 0.0)

    for_filters(make)

    def strip_body(strip, _):
        for copy in arrivals(strip):
            copy.wait()
        base = strip * MODES

        def body(blk, _):
            at = (strip, blk)
            decay = [tab[0, base + n] for n in range(MODES)]
            weight = [tab[1, base + n] for n in range(MODES)]
            state = [enter_ref[strip, blk, n] for n in range(MODES)]
            if reverse:
                for step in range(3):
                    for n in range(MODES):
                        moved = pltpu.roll(state[n], SUB - (1 << step), 0)
                        state[n] = state[n] + tab[2 + step, base + n] * moved
                state = [jnp.where(s < SUB - 1, pltpu.roll(a, SUB - 1, 0), 0.0) for a in state]
            for j in reversed(range(RUN)) if reverse else range(RUN):
                x = run_rows(xs, at, j)
                state = [decay[n] * state[n] + x for n in range(MODES)]
                mixed = total([weight[n] * state[n] for n in range(MODES)])
                out_ref[strip, blk, pl.ds(j, SUB, stride=RUN), :] = mixed
            return 0

        lax.fori_loop(0, BLOCKS, body, 0)
        leaving(strip).start()
        lead_refs[0][strip] = out_ref[strip, 0]
        lead_refs[1][strip] = out_ref[strip, HELD]
        return 0

    lax.fori_loop(0, STRIPS, strip_body, 0)
    for strip in range(STRIPS):
        leaving(strip).wait()
    for copy in leads:
        copy.wait()


def carry_kernel(where_ref, rates_ref, x_ref, y_hbm, y_ref, sem):
    place = where_ref[0]
    at = (place // (PAIRS * MODES)) * MODES + place % MODES
    log_decay = rates_ref[pl.ds(at, 1), :] / TOKENS
    across = jnp.exp(-log_decay * ROWS)
    zero = jnp.zeros((1, LANES), f32)

    def step(i, carried):
        a0, a1, b0, b1, cross, terms = carried
        y_ref[i, :, piece(0)] = a0
        y_ref[i, :, piece(1)] = a1
        cross = cross + (a0 * x_ref[i, :, piece(2)] + a1 * x_ref[i, :, piece(3)])
        terms = terms + x_ref[i, :, piece(4)]
        back = SHARDS - 1 - i
        y_ref[back, :, piece(2)] = b0
        y_ref[back, :, piece(3)] = b1
        return (
            across * a0 + x_ref[i, :, piece(0)],
            across * a1 + x_ref[i, :, piece(1)],
            across * b0 + x_ref[back, :, piece(2)],
            across * b1 + x_ref[back, :, piece(3)],
            cross,
            terms,
        )

    carried = lax.fori_loop(0, SHARDS, step, (zero,) * 6, unroll=8)
    row = jnp.exp(-log_decay) * carried[4] + carried[5]

    def fill(i, _):
        y_ref[i, :, piece(4)] = row
        return 0

    lax.fori_loop(0, SHARDS, fill, 0, unroll=16)
    copy = pltpu.make_async_copy(y_ref, y_hbm, sem)
    copy.start()
    copy.wait()


def finish_kernel(last, core_ref, tab, k_hbm, v_hbm, u_hbm, conv_hbm, flow_hbm, in_ref, *refs):
    gq_hbm, gk_hbm, gv_hbm, k_ref, v_ref, u_ref, conv_ref, flow_ref = refs[-13:-5]
    gq_ref, gk_ref, gv_ref, arrive_sems, sems = refs[-5:]
    second = core_ref[0] == 1
    if last:
        low, high = 0, jnp.where(second, HELD, BLOCKS)
    else:
        low, high = HELD, jnp.where(second, BLOCKS, HELD)

    def for_blocks(do, first=low):
        def body(blk, _):
            do(blk)
            return 0

        lax.fori_loop(first, high, body, 0)

    def arrivals(blk):
        cols = pl.ds(pl.multiple_of(blk * FILTERS, FILTERS), FILTERS)
        pairs = [
            (a.at[:, blk], b.at[:, blk]) for a, b in ((conv_hbm, conv_ref), (flow_hbm, flow_ref))
        ]
        for a, b in ((u_hbm, u_ref), (v_hbm, v_ref), (k_hbm, k_ref)):
            pairs.append((a.at[:, cols], b.at[:, cols]))
        return [
            pltpu.make_async_copy(a, b, arrive_sems.at[blk, i]) for i, (a, b) in enumerate(pairs)
        ]

    def fetch(blk):
        for copy in arrivals(blk):
            copy.start()

    for_blocks(fetch, low + 1)

    @pl.when(high > low)
    def _():
        lead_k, lead_v, lead_u, lead_conv, lead_flow = refs[:5]
        lead = pl.ds(low * FILTERS, FILTERS)
        for a, b in ((lead_k, k_ref), (lead_v, v_ref), (lead_u, u_ref)):
            b[:, lead] = a[...]
        for strip in range(STRIPS):
            conv_ref[strip, low] = lead_conv[strip]
            flow_ref[strip, low] = lead_flow[strip]

    def copies(blk):
        cols = pl.ds(pl.multiple_of(blk * FILTERS, FILTERS), FILTERS)
        return [
            pltpu.make_async_copy(src.at[:, cols], dst.at[:, cols], sems.at[blk, i])
            for i, (src, dst) in enumerate(((gq_ref, gq_hbm), (gk_ref, gk_hbm), (gv_ref, gv_hbm)))
        ]

    def block(blk):
        pair, odd = blk // 2, blk % 2

        @pl.when(blk > low)
        def _():
            for copy in arrivals(blk):
                copy.wait()

        def strip_body(strip, _):
            base = strip * MODES
            cols = lanes_of(blk * STRIPS + strip)
            leap = [tab[0, base + n] for n in range(MODES)]
            places = [owner(strip, pair, n) for n in range(MODES)]
            state = [
                tab[1, base + n] * in_ref[places[n], :, lanes_of(odd)] for n in range(MODES)
            ]
            for i in range(ROWS // 16):
                parts = []
                for _ in range(2):
                    parts.append(total(state))
                    state = [leap[n] * state[n] for n in range(MODES)]
                at = pl.ds(16 * i, 16)
                conv = conv_ref[strip, blk, at, :] + jnp.concatenate(parts, axis=0)
                gq_ref[at, cols] = (u_ref[at, cols].astype(f32) * conv).astype(bf16)
            state = [
                tab[2, base + n] * in_ref[places[n], :, lanes_of(2 + odd)] for n in range(MODES)
            ]
            for i in reversed(range(ROWS // 16)):
                parts = []
                for _ in range(2):
                    parts.insert(0, total(state))
                    state = [leap[n] * state[n] for n in range(MODES)]
                at = pl.ds(16 * i, 16)
                flow = flow_ref[strip, blk, at, :] + jnp.concatenate(parts, axis=0)
                gk_ref[at, cols] = (flow * v_ref[at, cols].astype(f32)).astype(bf16)
                gv_ref[at, cols] = (flow * k_ref[at, cols].astype(f32)).astype(bf16)
            return 0

        lax.fori_loop(0, STRIPS, strip_body, 0)
        for copy in copies(blk):
            copy.start()

    for_blocks(block)

    def drain(blk):
        for copy in copies(blk):
            copy.wait()

    for_blocks(drain)


def in_hbm(*arrays):
    return [pltpu.with_memory_space_constraint(a, pltpu.HBM) for a in arrays]


def local(query_rows, key_rows, value_rows, upstream, decay_rate, residue):
    half = lax.axis_index("fsdp")
    swap = [(0, 1), (1, 0)]
    first = lax.broadcasted_iota(jnp.int32, (2 * MODES, FILTERS // 2), 0) < MODES
    below, above = ((0, MODES, 0), (0, 0, 0)), ((MODES, 0, 0), (0, 0, 0))
    zero = jnp.zeros((), f32)
    mine = jnp.where(first, lax.pad(decay_rate, zero, below), lax.pad(residue, zero, above))
    other = lax.ppermute(mine, "fsdp", swap)
    vmem = pl.BlockSpec(memory_space=pltpu.VMEM)
    smem = pl.BlockSpec(memory_space=pltpu.SMEM)
    hbm = pl.BlockSpec(memory_space=pltpu.HBM)
    limit = pltpu.CompilerParams(vmem_limit_bytes=16 << 20)
    packet = (SHARDS, 1, PACKET)
    packets = pltpu.HBM(packet, f32)
    tiles = (STRIPS, BLOCKS, ROWS, LANES)
    state = (STRIPS, BLOCKS, MODES, SUB, LANES)
    params = (STRIPS * MODES, LANES)
    table = (STRIPS * MODES, SUB, LANES)
    whole = pltpu.VMEM((ROWS, WIDTH), bf16)
    query_rows, key_rows, value_rows, upstream = in_hbm(
        query_rows, key_rows, value_rows, upstream
    )
    ps, gs = pl.pallas_call(
        prepare_kernel,
        in_specs=[hbm] * 4,
        out_specs=[vmem] * 2,
        out_shape=[jax.ShapeDtypeStruct(tiles, f32)] * 2,
        scratch_shapes=[whole] * 4 + [pltpu.SemaphoreType.DMA((BLOCKS, 4))],
        compiler_params=limit,
        cost_estimate=pl.CostEstimate(flops=1 << 22, bytes_accessed=12 << 20, transcendentals=0),
        name="prepare",
    )(query_rows, key_rows, value_rows, upstream)
    send, enter_ahead, enter_behind, rates, residues, product, gated = pl.pallas_call(
        summarize_kernel,
        in_specs=[smem] + [vmem] * 4,
        out_specs=[hbm] * 7,
        out_shape=[packets]
        + [pltpu.HBM(state, f32)] * 2
        + [pltpu.HBM(params, f32)] * 2
        + [pltpu.HBM(tiles, f32)] * 2,
        scratch_shapes=[
            pltpu.VMEM((5,) + table, f32),
            pltpu.VMEM((HALF, SUB, LANES), f32),
            pltpu.VMEM((MODES, SUB, LANES), f32),
            pltpu.VMEM(packet, f32),
            pltpu.VMEM(state, f32),
            pltpu.VMEM(state, f32),
            pltpu.VMEM(params, f32),
            pltpu.VMEM(params, f32),
            pltpu.SemaphoreType.DMA((STRIPS, 3)),
            pltpu.SemaphoreType.DMA((4,)),
        ],
        compiler_params=limit,
        name="summarize",
    )(half.astype(jnp.int32).reshape(1), mine, other, ps, gs)
    arrived = lax.all_to_all(send, ALL, 0, 0, tiled=True)

    lead = jax.ShapeDtypeStruct((STRIPS, ROWS, LANES), f32)
    lead_rows = jax.ShapeDtypeStruct((ROWS, FILTERS), bf16)

    def inner(xs, enter, reverse, extra=(), more=()):
        return pl.pallas_call(
            functools.partial(inner_kernel, reverse),
            in_specs=[hbm] * (4 + len(extra)),
            out_specs=[hbm] + [vmem] * (2 + len(more)),
            out_shape=[pltpu.HBM(tiles, f32), lead, lead, *more],
            scratch_shapes=[
                pltpu.VMEM((5 if reverse else 2,) + table, f32),
                pltpu.VMEM(params, f32),
                pltpu.VMEM(params, f32),
                pltpu.VMEM(tiles, f32),
                pltpu.VMEM(state, f32),
                pltpu.VMEM(tiles, f32),
                pltpu.SemaphoreType.DMA((8,)),
                pltpu.SemaphoreType.DMA((STRIPS, 3)),
            ],
            compiler_params=limit,
            cost_estimate=pl.CostEstimate(
                flops=1 << 24, bytes_accessed=16 << 20, transcendentals=0
            ),
            name="behind" if reverse else "ahead",
        )(*in_hbm(rates, residues, xs, enter), *extra)

    late = jax.ShapeDtypeStruct((3,) + table, f32)
    conv, lead_conv, held_conv, late_tab, *rows_in = inner(
        product,
        enter_ahead,
        False,
        (key_rows, value_rows, upstream),
        (late,) + (lead_rows,) * 6,
    )
    arrived, conv = lax.optimization_barrier((arrived, conv))
    place = lax.axis_index(ALL).astype(jnp.int32).reshape(1)
    carries = pl.pallas_call(
        carry_kernel,
        in_specs=[smem] + [vmem] * 2,
        out_specs=hbm,
        out_shape=packets,
        scratch_shapes=[pltpu.VMEM(packet, f32), pltpu.SemaphoreType.DMA],
        compiler_params=limit,
        name="carry",
    )(place, rates, arrived)
    back = lax.all_to_all(carries, ALL, 0, 0, tiled=True)
    flowing, lead_flow, held_flow = inner(gated, enter_behind, True)
    back, flowing = lax.optimization_barrier((back, flowing))
    rows = back[:, 0, 4 * LANES :].reshape(STRIPS, PAIRS, MODES, LANES)
    count = STRIPS // 2
    rows = lax.dynamic_slice_in_dim(rows, half * count, count, 0).sum(axis=1)
    conv, flowing = in_hbm(conv, flowing)
    core = lax.axis_index("ch").astype(jnp.int32).reshape(1)
    shapes = [pltpu.HBM((ROWS, WIDTH), bf16)] * 3

    def finish(last, leads=(), before=()):
        count_in = 8 + len(leads)
        return pl.pallas_call(
            functools.partial(finish_kernel, last),
            in_specs=[smem, vmem]
            + [hbm] * 5
            + [vmem] * (1 + len(leads))
            + [hbm] * len(before),
            out_specs=[hbm] * 3,
            out_shape=shapes,
            input_output_aliases={count_in + i: i for i in range(len(before))},
            scratch_shapes=[
                whole,
                whole,
                whole,
                pltpu.VMEM(tiles, f32),
                pltpu.VMEM(tiles, f32),
                whole,
                whole,
                whole,
                pltpu.SemaphoreType.DMA((BLOCKS, 5)),
                pltpu.SemaphoreType.DMA((BLOCKS, 3)),
            ],
            compiler_params=limit,
            cost_estimate=pl.CostEstimate(
                flops=1 << 24, bytes_accessed=10 << 20, transcendentals=0
            ),
            name="finish" if last else "begin",
        )(
            core, late_tab, key_rows, value_rows, upstream, conv, flowing, back, *leads, *before
        )

    early = finish(False, (*rows_in[3:], held_conv, held_flow))
    own, *early = lax.optimization_barrier((rows, *early))
    rows = rows + lax.ppermute(own, "ch", swap)
    grads_out = finish(True, (*rows_in[:3], lead_conv, lead_flow), early)
    rows = rows.transpose(1, 0, 2).reshape(MODES, count * LANES)
    gain = jnp.sqrt((1.0 + decay_rate) / TOKENS)
    residue_grad = gain * rows / math.sqrt(TOKENS)
    return (*grads_out, residue_grad)


def solution(mesh):
    rows = P(ALL, "ch")
    params = P(None, "fsdp")
    return jax.shard_map(
        local,
        mesh=mesh,
        in_specs=(rows, rows, rows, rows, params, params),
        out_specs=(rows, rows, rows, params),
        check_vma=False,
    )
```
